32 devices in a mesh: dp: 8 (over z, y), pipe: 2 (over x), tensor: 2 (over core).
Axes of the slice: x: 2, y: 2, z: 4, core: 2. Of those that a mesh axis runs over, the one named last changes fastest.
Arguments:
- hidden: bfloat16 [2, 1024, 8192], P('pipe', 'dp', 'tensor'), may hold values from -6 to 6
- doc_lengths: int32 [2, 8, 8], P('pipe', 'dp'), may hold values from 1 to 32, 128 in all within a row
- doc_target: int32 [2, 8, 8], P('pipe', 'dp'), may hold values from 0 to 7, each once within a row
- norm_gain: float32 [2, 8192], P('pipe'), may hold values from 0.5 to 1.5
- q_weight: bfloat16 [2, 8192, 8192], P('pipe', None, 'tensor'), may hold values from -0.0625 to 0.0625
- kv_weight: bfloat16 [2, 8192, 2048], P('pipe', None, 'tensor'), may hold values from -0.0625 to 0.0625
Outputs:
- balanced: bfloat16 [2, 2048, 8192], P('pipe', 'dp', 'tensor')
The draws below stay inside these ranges and needn't reach their ends.
Inputs may be any that keep to these rules, and one draw needn't show every extreme that they name: `doc_lengths`: each row of lengths sums to 128 and its largest entry is exactly 32. `doc_target`: each row is a permutation of the dp indices.
All inputs are finite; a program needn't handle non-finite values.
Results may differ from the reference program's by a relative error of at most 0.0067.
Values may be sent and summed in bfloat16 or wider, within the bound.
A program may use at most 128 MiB of HBM per device.

```python
import math
from functools import partial
import jax
import jax.numpy as jnp
import numpy as np
from jax import lax

D = 8192
HD = 128
KV_HEADS = 8
TOK_DEV = 128
STEPS = 2
CAPR = 32
TOKENS = 1024
N_DP = 8
N_PIPE = 2


def steps_of(stream_key, dims, cuts, low, largest):
    def one(position, shards_of):
        heights = jax.random.uniform(jax.random.fold_in(jax.random.fold_in(stream_key, 6), position), (shards_of,), jnp.float32, low / len(cuts), largest / len(cuts))
        return jnp.repeat(jnp.exp(heights), dims[position] // shards_of).reshape((-1,) + (1,) * (len(dims) - position - 1))

    loudness = one(*cuts[0])
    for cut in cuts[1:]:
        loudness = loudness * one(*cut)
    return loudness


def split_up(amount, total, limit, slope):
    weights = [(1 << 20) // math.isqrt(standing ** slope) + 1 for standing in range(2, amount + 1)]
    surplus, counts = total - limit - (amount - 1), [1] * (amount - 1)
    while surplus > 0:
        free = [i for i in range(amount - 1) if counts[i] < limit]
        mass, remaining = sum([weights[i] for i in free]), surplus
        for i in free:
            extra = min(limit - counts[i], max(1, remaining * weights[i] // mass), surplus)
            counts[i] = counts[i] + extra
            surplus = surplus - extra
    return np.array([limit] + counts)


def uneven_parts(rng, count, total, most, skew):
    if count == 2:
        one = jax.random.randint(rng, (), max(1, total - most), min(most, total - 1) + 1)
        return jnp.stack([one, total - one])
    sizes = jnp.asarray(split_up(count, total, most, skew), jnp.int32)
    pairs = (count - 1) // 2
    donor, sink = sizes[1:1 + 2 * pairs:2], sizes[2:2 + 2 * pairs:2]
    room = jnp.minimum(donor - 1, most - sink)
    moved = jax.random.randint(jax.random.fold_in(rng, 1), (pairs,), 0, 1 << 20) % (room + 1)
    sizes = sizes.at[1:1 + 2 * pairs:2].set(donor - moved).at[2:2 + 2 * pairs:2].set(sink + moved)
    return sizes[jax.random.permutation(jax.random.fold_in(rng, 2), count)]


def bell_draw(rng, extent, scale, bound, split=(), held_as=jnp.bfloat16):
    array = scale * jax.random.normal(rng, extent, jnp.float32)
    if split:
        array = array * steps_of(rng, extent, split, -0.22, 0.18)
    return jnp.clip(array, -bound, bound).astype(held_as)


def setup_inputs(seed: int = 0) -> dict:
    streams_of = jax.random.split(jax.random.key(seed), 7)
    return {
        "hidden": bell_draw(streams_of[0], (N_PIPE, TOKENS, D), 1.0, 6.0, ((0, 2), (1, 8), (2, 2))),
        "doc_lengths": jax.vmap(lambda own: uneven_parts(own, N_DP, TOK_DEV, CAPR, 2))(jax.random.split(streams_of[1], N_PIPE * N_DP)).reshape((N_PIPE, N_DP, N_DP)).astype(jnp.int32),
        "doc_target": jax.vmap(lambda own: jax.random.permutation(own, N_DP))(jax.random.split(streams_of[2], N_PIPE * N_DP)).reshape((N_PIPE, N_DP, N_DP)).astype(jnp.int32),
        "norm_gain": jnp.clip(1.0 + 0.1 * jax.random.normal(streams_of[3], (N_PIPE, D), jnp.float32), 0.5, 1.5),
        "q_weight": bell_draw(streams_of[4], (N_PIPE, D, D), D ** -0.5, 0.0625, ((0, 2), (2, 2))),
        "kv_weight": bell_draw(streams_of[5], (N_PIPE, D, 2 * KV_HEADS * HD), D ** -0.5, 0.0625, ((0, 2), (2, 2))),
    }


def build_send(token_rows, lengths, targets, capacity, groups):
    ordinal = jnp.arange(groups, dtype=jnp.int32)
    offsets = jnp.cumsum(lengths) - lengths
    onehot = (targets[None, :] == ordinal[:, None]).astype(jnp.int32)
    doc_sizes = lax.optimization_barrier(jnp.sum(onehot * lengths[None, :], axis=1))
    doc_starts = lax.optimization_barrier(jnp.sum(onehot * offsets[None, :], axis=1))
    within = jnp.arange(capacity, dtype=jnp.int32)
    row_index = jnp.minimum(doc_starts[:, None] + within[None, :], token_rows.shape[0] - 1).astype(jnp.int32)
    picked = jnp.take(token_rows, row_index.reshape(-1), axis=0).reshape(groups, capacity, token_rows.shape[1])
    inside = within[None, :] < doc_sizes[:, None]
    return (jnp.where(inside[:, :, None], picked, jnp.zeros_like(picked)), doc_sizes)

def ref_layer(current, gain_row, query_weight, pair_weight, allowed):
    blocks, length, features = current.shape
    per_group = D // HD // KV_HEADS
    widened = current.astype(jnp.float32)
    total_sq = lax.optimization_barrier(jnp.sum(widened * widened, axis=-1))
    scale_row = lax.rsqrt(total_sq / D + 1e-05)
    normed = (widened * scale_row[..., None] * gain_row).astype(jnp.bfloat16)
    flat_rows = normed.reshape(blocks * length, features)
    queries = jnp.dot(flat_rows, query_weight, preferred_element_type=jnp.float32).astype(jnp.bfloat16)
    key_value = jnp.dot(flat_rows, pair_weight, preferred_element_type=jnp.float32).astype(jnp.bfloat16)
    queries = queries.reshape(blocks, length, KV_HEADS, per_group, HD).astype(jnp.float32)
    key_value = key_value.reshape(blocks, length, 2, HD, KV_HEADS).astype(jnp.float32)
    key_rows = key_value[:, :, 0]
    values = key_value[:, :, 1]
    scores = jnp.einsum('bqgph,bkhg->bgpqk', queries, key_rows) * HD ** (-0.5)
    exp_scores = jnp.where(allowed[:, None, None], jnp.exp(scores), 0.0)
    probabilities = (exp_scores / lax.optimization_barrier(jnp.sum(exp_scores, axis=-1, keepdims=True))).astype(jnp.bfloat16)
    attended = jnp.einsum('bgpqk,bkhg->bqgph', probabilities.astype(jnp.float32), values)
    attended = attended.reshape(blocks, length, features)
    return (widened + attended).astype(jnp.bfloat16)

def reference(hidden, doc_lengths, doc_target, norm_gain, q_weight, kv_weight):
    results = []
    within = jnp.arange(TOK_DEV, dtype=jnp.int32)
    causal = within[:, None] >= within[None, :]
    for micro_batch in range(N_PIPE):
        lengths = doc_lengths[micro_batch]
        targets = doc_target[micro_batch]
        current = hidden[micro_batch].reshape(N_DP, TOK_DEV, D)
        doc_ends = jnp.cumsum(lengths, axis=1)
        segment = lax.optimization_barrier(jnp.sum((within[None, :, None] >= doc_ends[:, None, :]).astype(jnp.int32), axis=2))
        allowed = (segment[:, :, None] == segment[:, None, :]) & causal[None]
        for layer_step in range(STEPS):
            section_index = (micro_batch + layer_step) % N_PIPE
            current = ref_layer(current, norm_gain[section_index], q_weight[section_index], kv_weight[section_index], allowed)
        packed, doc_sizes = jax.vmap(partial(build_send, capacity=CAPR, groups=N_DP))(current, lengths, targets)
        results.append(jnp.transpose(packed, (1, 0, 2, 3)).reshape(N_DP * N_DP * CAPR, D))
    stacked = jnp.stack(results)
    return jnp.roll(stacked, STEPS - 1, axis=0)
```

```python
import contextlib
import functools

import jax
import jax.numpy as jnp
from jax import lax
from jax.experimental import pallas as pl
from jax.experimental.pallas import tpu as pltpu
from jax.sharding import PartitionSpec as P

D = 8192
HD = 128
KV_HEADS = 8
STEPS = 2


def passed_along(block, axis, distance):
    devices = range(lax.axis_size(axis))
    route = [((i - distance) % len(devices), i) for i in devices]
    return lax.ppermute(block, axis, route)


def build_send(token_rows, lengths, targets, capacity, groups):
    ordinal = jnp.arange(groups, dtype=jnp.int32)
    offsets = jnp.cumsum(lengths) - lengths
    onehot = (targets[None, :] == ordinal[:, None]).astype(jnp.int32)
    doc_sizes = jnp.sum(onehot * lengths[None, :], axis=1)
    doc_starts = jnp.sum(onehot * offsets[None, :], axis=1)
    within = jnp.arange(capacity, dtype=jnp.int32)
    row_index = jnp.minimum(doc_starts[:, None] + within[None, :], token_rows.shape[0] - 1)
    picked = jnp.take(token_rows, row_index.reshape(-1), axis=0).reshape(
        groups, capacity, token_rows.shape[1]
    )
    inside = within[None, :] < doc_sizes[:, None]
    return (jnp.where(inside[:, :, None], picked, jnp.zeros_like(picked)), doc_sizes)


def doc_masks(lengths, length):
    within = jnp.arange(length, dtype=jnp.int32)
    doc_ends = jnp.cumsum(lengths)
    segment = jnp.sum((within[:, None] >= doc_ends[None, :]).astype(jnp.int32), axis=1)
    causal = within[:, None] >= within[None, :]
    return (segment[:, None] == segment[None, :]) & causal


def attend_heads(queries, kv_local, allowed, local_rank):
    row_count = queries.shape[0]
    local_heads = queries.shape[1] // HD
    per_group = D // HD // KV_HEADS
    kv_count = max(1, local_heads // per_group)
    kv_first = local_rank * local_heads // per_group
    kv_whole = lax.all_gather(kv_local, "tensor", axis=1, tiled=True)
    kv_heads = kv_whole.reshape(row_count, 2, HD, KV_HEADS)
    own_heads = lax.dynamic_slice_in_dim(kv_heads, kv_first, kv_count, 3)
    key_rows = own_heads[:, 0]
    values = own_heads[:, 1]
    grouped = queries.reshape(row_count, kv_count, local_heads // kv_count, HD)
    scores = jnp.einsum(
        "qcph,khc->cpqk", grouped, key_rows, preferred_element_type=jnp.float32
    ) * HD ** (-0.5)
    exp_scores = jnp.where(allowed[None, None], jnp.exp(scores), 0.0)
    probabilities = (exp_scores / jnp.sum(exp_scores, axis=-1, keepdims=True)).astype(jnp.bfloat16)
    attended = jnp.einsum(
        "cpqk,khc->qcph", probabilities, values, preferred_element_type=jnp.float32
    )
    return attended.reshape(row_count, queries.shape[1])


def layer_pass(current, gain_full, query_cols, kv_cols, allowed):
    local_rank = lax.axis_index("tensor")
    widened = current.astype(jnp.float32)
    whole = lax.all_gather(current, "tensor", axis=1, tiled=True)
    whole_wide = whole.astype(jnp.float32)
    scale_row = lax.rsqrt(jnp.sum(whole_wide * whole_wide, axis=-1) / D + 1e-05)
    normed_full = (whole_wide * scale_row[:, None] * gain_full).astype(jnp.bfloat16)
    query_sum = jnp.dot(normed_full, query_cols, preferred_element_type=jnp.float32)
    kv_sum = jnp.dot(normed_full, kv_cols, preferred_element_type=jnp.float32)
    queries = query_sum.astype(jnp.bfloat16)
    kv_local = kv_sum.astype(jnp.bfloat16)
    attended = attend_heads(queries, kv_local, allowed, local_rank)
    return (widened + attended).astype(jnp.bfloat16)


def on_device(hidden, doc_lengths, doc_target, norm_gain, q_weight, kv_weight):
    groups = lax.axis_size("dp")
    current = hidden[0]
    lengths = doc_lengths[0, 0]
    targets = doc_target[0, 0]
    capacity = current.shape[0] // 4
    gain_full = norm_gain[0]
    query_cols = q_weight[0]
    kv_cols = kv_weight[0]
    carried = jnp.stack([lengths, targets]).astype(jnp.bfloat16)
    for layer_step in range(STEPS):
        allowed = doc_masks(carried[0].astype(jnp.int32), current.shape[0])
        current = layer_pass(current, gain_full, query_cols, kv_cols, allowed)
        if layer_step + 1 < STEPS:
            current, carried = passed_along((current, carried), "pipe", 1)
    final_lengths = carried[0].astype(jnp.int32)
    final_targets = carried[1].astype(jnp.int32)
    packed, doc_sizes = build_send(current, final_lengths, final_targets, capacity, groups)
    received = lax.all_to_all(packed, "dp", split_axis=0, concat_axis=0, tiled=True)
    return received.reshape(1, groups * capacity, received.shape[2])


CHUNK = 256
SLOTS = 6
KV_ROWS = 1024
LEAD = 5


mark = contextlib.nullcontext


def split_masks(n_dp):
    early = [m for m in range(n_dp) if m >= n_dp // 2 and m % 2 == 0]
    return early, [m for m in range(n_dp) if m not in early]


def fused_kernel(
    sizes, hidden, lengths, targets, gain, wq, wkv, out, meta,
    x_own, x_other, h_send, next_own, next_other, early_own, early_other, early_send,
    meta_next, meta_early, normed_first, normed_next, spread, kv_acc, squares, scales,
    kv_send, kv_heads, kv_weights, ring, mask, early_mask, valid, early_chooser, late_chooser,
    q_held, packed, early_out,
    sem_x, sem_xs, sem_xr, sem_ms, sem_mr, sem_kvw, sem_ring, sem_kvs, sem_kvr,
    sem_hs, sem_hr, sem_fs, sem_fr, sem_as, sem_ar, sem_own,
    sem_es, sem_er, sem_gs, sem_gr, sem_mes, sem_mer,
):
    n_dp, n_pipe, docs = sizes
    rows, width = hidden.shape
    features = gain.shape[1]
    n_chunks = width // CHUNK
    n_kv = wkv.shape[1]
    half_blocks = width // KV_ROWS
    own_kv = kv_heads.shape[2]
    chunk_heads = CHUNK // HD
    group_chunks = n_chunks // own_kv
    capacity = packed.shape[1]
    early_masks, late_masks = split_masks(n_dp)
    half = len(early_masks)
    early_rows = half * capacity
    dp = lax.axis_index("dp")
    pipe = lax.axis_index("pipe")
    side = lax.axis_index("tensor")
    other = 1 - side
    following = lax.rem(pipe + 1, n_pipe)
    preceding = lax.rem(pipe + n_pipe - 1, n_pipe)
    total = STEPS * n_chunks + LEAD
    normed_of = (normed_first, normed_next)

    def partner(flips):
        index, bit = dp, 1
        while bit < n_dp:
            if flips & bit:
                index = index + bit - 2 * bit * lax.rem(dp // bit, 2)
            bit *= 2
        return index

    early_partners = [partner(m) for m in early_masks]
    late_partners = [partner(m) for m in late_masks]

    def cols(j):
        return pl.ds(pl.multiple_of(j * CHUNK, CHUNK), CHUNK)

    def kv_rows(which, b):
        return pl.ds(pl.multiple_of((which * half_blocks + b) * KV_ROWS, KV_ROWS), KV_ROWS)

    def kv_copy(order, b):
        here = kv_rows((side, other)[order], b)
        return pltpu.make_async_copy(
            wkv.at[here], kv_weights.at[here], sem_kvw.at[order * half_blocks + b]
        )

    def ring_copy(c):
        slot = lax.rem(c, SLOTS)
        return pltpu.make_async_copy(
            wq.at[:, cols(lax.rem(c, n_chunks))], ring.at[slot], sem_ring.at[slot]
        )

    def x_copy(j):
        return pltpu.make_async_copy(hidden.at[:, cols(j)], x_own.at[j], sem_x.at[j])

    def x_remote(j):
        return pltpu.make_async_remote_copy(
            x_own.at[j], x_other.at[j], sem_xs.at[j], sem_xr.at[j],
            device_id={"tensor": other}, device_id_type=pl.DeviceIdType.MESH,
        )

    def meta_remote():
        return pltpu.make_async_remote_copy(
            meta, meta_next, sem_ms, sem_mr,
            device_id={"pipe": following}, device_id_type=pl.DeviceIdType.MESH,
        )

    def meta_on(k):
        return pltpu.make_async_remote_copy(
            meta_next, meta_early.at[k], sem_mes.at[k], sem_mer.at[k],
            device_id={"dp": early_partners[k]}, device_id_type=pl.DeviceIdType.MESH,
        )

    def early_remote(k, j):
        return pltpu.make_async_remote_copy(
            early_send.at[j, k], early_own.at[j, k * capacity:(k + 1) * capacity],
            sem_es.at[k, j], sem_er.at[k, j],
            device_id={"dp": early_partners[k]}, device_id_type=pl.DeviceIdType.MESH,
        )

    def early_forward(j):
        return pltpu.make_async_remote_copy(
            early_own.at[j], early_other.at[j], sem_gs.at[j], sem_gr.at[j],
            device_id={"tensor": other}, device_id_type=pl.DeviceIdType.MESH,
        )

    parts = ((0, 0, rows), (1, 0, rows), (1, rows, early_rows))

    def kv_remote(part):
        layer, first, count = parts[part]
        here = pl.ds(first, count)
        return pltpu.make_async_remote_copy(
            kv_send.at[layer, :, here], kv_heads.at[layer, side, :, here],
            sem_kvs.at[part], sem_kvr.at[part],
            device_id={"tensor": other}, device_id_type=pl.DeviceIdType.MESH,
        )

    def h_remote(j):
        return pltpu.make_async_remote_copy(
            h_send.at[j], next_own.at[j], sem_hs.at[j], sem_hr.at[j],
            device_id={"pipe": following}, device_id_type=pl.DeviceIdType.MESH,
        )

    def forward_remote(j):
        return pltpu.make_async_remote_copy(
            next_own.at[j], next_other.at[j], sem_fs.at[j], sem_fr.at[j],
            device_id={"tensor": other}, device_id_type=pl.DeviceIdType.MESH,
        )

    def doc_rows(index):
        return pl.ds(pl.multiple_of(index * capacity, capacity), capacity)

    def doc_remote(k, j):
        return pltpu.make_async_remote_copy(
            packed.at[k, :, cols(j)], out.at[doc_rows(dp), cols(j)],
            sem_as.at[k], sem_ar.at[k],
            device_id={"dp": late_partners[k]}, device_id_type=pl.DeviceIdType.MESH,
        )

    def doc_all(k):
        return pltpu.make_async_remote_copy(
            packed.at[k], out.at[doc_rows(late_partners[k])],
            sem_as.at[k], sem_ar.at[k],
            device_id={"dp": late_partners[k]}, device_id_type=pl.DeviceIdType.MESH,
        )

    def own_store(j):
        return pltpu.make_async_copy(
            packed.at[0, :, cols(j)], out.at[doc_rows(dp), cols(j)], sem_own.at[half]
        )

    def own_stored():
        return pltpu.make_async_copy(packed.at[0], out.at[doc_rows(dp)], sem_own.at[half])

    def early_store(k, j):
        return pltpu.make_async_copy(
            early_out.at[k, :, cols(j)], out.at[doc_rows(early_partners[k]), cols(j)],
            sem_own.at[k],
        )

    def early_stored(k):
        return pltpu.make_async_copy(
            early_out.at[k], out.at[doc_rows(early_partners[k])], sem_own.at[k]
        )

    for j in range(n_chunks):
        x_copy(j).start()
    barrier = pltpu.get_barrier_semaphore()
    pl.semaphore_signal(
        barrier, inc=1, device_id={"tensor": other}, device_id_type=pl.DeviceIdType.MESH
    )
    pl.semaphore_signal(
        barrier, inc=1, device_id={"pipe": following}, device_id_type=pl.DeviceIdType.MESH
    )
    greeted = n_dp + 1
    if n_pipe > 2:
        pl.semaphore_signal(
            barrier, inc=1, device_id={"pipe": preceding}, device_id_type=pl.DeviceIdType.MESH
        )
        greeted += 1
    for away in range(1, n_dp):
        pl.semaphore_signal(
            barrier, inc=1, device_id={"dp": lax.rem(dp + away, n_dp)},
            device_id_type=pl.DeviceIdType.MESH,
        )
    for order in range(2):
        for b in range(half_blocks):
            kv_copy(order, b).start()

    meta[...] = jnp.zeros(meta.shape, jnp.int32)
    meta[0:1, 0:docs] = lengths[...]
    meta[1:2, 0:docs] = targets[...]
    cols_wide = spread.shape[0]
    out_col = lax.broadcasted_iota(jnp.int32, (128, n_kv), 1)
    wanted = lax.rem(out_col, HD) * KV_HEADS + out_col // HD

    def fill_spread(i, carry):
        base = pl.multiple_of(i * 128, 128)
        row = lax.broadcasted_iota(jnp.int32, (128, n_kv), 0) + base
        spread[pl.ds(base, 128), :] = (row == wanted).astype(jnp.float32).astype(jnp.bfloat16)
        return carry

    def fill_mask(source):
        row = lax.broadcasted_iota(jnp.int32, (rows, rows), 0)
        col = lax.broadcasted_iota(jnp.int32, (rows, rows), 1)
        row_doc = jnp.zeros((rows, rows), jnp.int32)
        col_doc = jnp.zeros((rows, rows), jnp.int32)
        end = jnp.zeros((1, 1), jnp.int32)
        for d in range(docs):
            end = end + source[0:1, d:d + 1]
            row_doc = row_doc + (row >= end).astype(jnp.int32)
            col_doc = col_doc + (col >= end).astype(jnp.int32)
        allowed = jnp.where((row_doc == col_doc) & (row >= col), 1.0, 0.0)
        for i in range(chunk_heads):
            mask[i * rows:(i + 1) * rows, :] = allowed

    def fill_early_mask():
        row = lax.broadcasted_iota(jnp.int32, (early_rows, early_rows), 0)
        col = lax.broadcasted_iota(jnp.int32, (early_rows, early_rows), 1)
        allowed = jnp.where((row // capacity == col // capacity) & (row >= col), 1.0, 0.0)
        for i in range(chunk_heads):
            early_mask[i * early_rows:(i + 1) * early_rows, :] = allowed

    def fill_valid():
        row = lax.broadcasted_iota(jnp.int32, (capacity, CHUNK), 0)
        for slot in range(half):
            size = jnp.zeros((1, 1), jnp.int32)
            for d in range(docs):
                here = meta_early[slot, 1:2, d:d + 1] == dp
                size = size + jnp.where(here, meta_early[slot, 0:1, d:d + 1], 0)
            valid[slot * capacity:(slot + 1) * capacity, :] = jnp.where(row < size, 1.0, 0.0)

    def fill_choosers(source):
        row = lax.broadcasted_iota(jnp.int32, (1, rows), 1)
        goals = [jnp.full((1, rows), -1, jnp.int32) for _ in range(2)]
        begin = jnp.zeros((1, 1), jnp.int32)
        for d in range(docs):
            end = begin + source[0:1, d:d + 1]
            target = source[1:2, d:d + 1]
            inside = (row >= begin) & (row < end)
            for i, partners in enumerate((early_partners, late_partners)):
                first = jnp.full((1, 1), -n_dp * capacity, jnp.int32)
                for k, index in enumerate(partners):
                    first = jnp.where(target == index, k * capacity, first)
                goals[i] = jnp.where(inside, first + row - begin, goals[i])
            begin = end
        for ref, goal in zip((early_chooser, late_chooser), goals):
            slot = lax.broadcasted_iota(jnp.int32, ref.shape, 0)
            ref[...] = (slot == goal).astype(jnp.float32).astype(jnp.bfloat16)

    def absorb_half(held, which):
        def one(j, acc):
            wide = held[j].astype(jnp.float32)
            where = cols(which * n_chunks + j)
            normed_first[:, where] = (wide * gain[:, where]).astype(jnp.bfloat16)
            return acc + wide * wide

        squares[0:rows] = lax.fori_loop(0, n_chunks, one, squares[0:rows])

    def multiply_half(order):
        which = (side, other)[order]

        def one(b, carry):
            kv_copy(order, b).wait()
            here = kv_rows(which, b)
            kv_acc[0:rows] += jnp.dot(
                normed_first[:, here], kv_weights[here, :], preferred_element_type=jnp.float32
            )
            return carry

        lax.fori_loop(0, half_blocks, one, 0)

    def absorb_next(mine, theirs, first, count, j):
        here = slice(first, first + count)
        left, right = cols(side * n_chunks + j), cols(other * n_chunks + j)
        a = mine[j].astype(jnp.float32)
        b = theirs[j].astype(jnp.float32)
        squares[here] += a * a + b * b
        a = (a * gain[:, left]).astype(jnp.bfloat16)
        b = (b * gain[:, right]).astype(jnp.bfloat16)
        normed_next[here, left] = a
        normed_next[here, right] = b
        kv_acc[here] += jnp.dot(
            jnp.concatenate([a, b], axis=1),
            jnp.concatenate([kv_weights[left, :], kv_weights[right, :]], axis=0),
            preferred_element_type=jnp.float32,
        )

    def clear_sums():
        kv_acc[...] = jnp.zeros(kv_acc.shape, jnp.float32)
        squares[...] = jnp.zeros(squares.shape, jnp.float32)

    def keys_values(part):
        layer, first, count = parts[part]
        here = slice(first, first + count)
        scale = lax.rsqrt(jnp.sum(squares[here], axis=-1, keepdims=True) / features + 1e-05)
        scales[here] = jnp.broadcast_to(scale, (count, CHUNK))
        kv_cols = (kv_acc[here] * scale).astype(jnp.bfloat16)
        for which, keep in ((other, False), (side, True)):
            start = pl.multiple_of(which * own_kv * HD, own_kv * HD)
            heads = jnp.dot(
                kv_cols, spread[:, pl.ds(start, own_kv * HD)], preferred_element_type=jnp.float32
            ).astype(jnp.bfloat16)
            for g in range(own_kv):
                if keep:
                    kv_heads[layer, side, g, here] = heads[:, g * HD:(g + 1) * HD]
                else:
                    kv_send[layer, g, here] = heads[:, g * HD:(g + 1) * HD]
            if not keep:
                kv_remote(part).start()

    def query(layer, c, first, count):
        here = slice(first, first + count)
        product = jnp.dot(
            normed_of[layer][here, :], ring[lax.rem(c, SLOTS)], preferred_element_type=jnp.float32
        )
        return (product * scales[here]).astype(jnp.bfloat16)

    def attend(layer, j, mine, first, count, allowed):
        here = slice(first, first + count)
        q = q_held[lax.rem(j, 2), here]
        g = j // group_chunks
        stacked = jnp.concatenate([q[:, i * HD:(i + 1) * HD] for i in range(chunk_heads)], axis=0)
        scores = lax.dot_general(
            stacked, kv_heads[layer, 0, g, here], (((1,), (1,)), ((), ())),
            preferred_element_type=jnp.float32,
        ) * HD ** (-0.5)
        e = jnp.where(allowed[...] > 0.0, jnp.exp(scores), 0.0)
        p = (e * (1.0 / jnp.sum(e, axis=-1, keepdims=True))).astype(jnp.bfloat16)
        a = jnp.dot(p, kv_heads[layer, 1, g, here], preferred_element_type=jnp.float32)
        side_by_side = jnp.concatenate(
            [a[i * count:(i + 1) * count] for i in range(chunk_heads)], axis=1
        )
        return (mine[j].astype(jnp.float32) + side_by_side).astype(jnp.bfloat16)

    def attend_first(j):
        return attend(0, j, x_own, 0, rows, mask)

    def attend_local(j):
        return attend(1, j, next_own, 0, rows, mask)

    def attend_early(j):
        return attend(1, j, early_own, rows, early_rows, early_mask)

    def refill(c):
        @pl.when(c + SLOTS < total)
        def _():
            ring_copy(c + SLOTS).start()

    def run_span(layer, base, low, high, first, count, attends, finish, ready=None):
        here = slice(first, first + count)
        ring_copy(base + low).wait()
        q_held[low % 2, here] = query(layer, base + low, first, count)
        refill(jnp.int32(base + low))
        if ready is not None:
            ready()

        def one(j, carry):
            c = base + j
            ring_copy(c).wait()
            fresh = query(layer, c, first, count)
            done = [attended(j - 1) for attended in attends]
            q_held[lax.rem(j, 2), here] = fresh
            refill(c)
            finish(j - 1, *done)
            return carry

        if high - low > 1:
            lax.fori_loop(low + 1, high, one, 0)
        finish(high - 1, *[attended(high - 1) for attended in attends])

    lag, early_lag = 4, 7

    def pass_on(j):
        h_remote(j).wait_recv()
        forward_remote(j).start()
        picked = jnp.dot(
            early_chooser[...], next_own[j], preferred_element_type=jnp.float32
        ).astype(jnp.bfloat16)
        for slot in range(half):
            early_send[j, slot] = picked[slot * capacity:(slot + 1) * capacity]
        for k in range(half):
            early_remote(k, j).start()

    def take_local(j):
        forward_remote(j).wait_recv()
        absorb_next(next_own, next_other, 0, rows, j)

    def pass_early(j):
        for k in range(half):
            early_remote(k, j).wait_recv()
        early_forward(j).start()

    def take_early(j):
        early_forward(j).wait_recv()
        absorb_next(early_own, early_other, rows, early_rows, j)

    def send_next(j, done):
        h_send[j] = done
        h_remote(j).start()

        for delay, step in (
            (lag, pass_on), (lag + 1, take_local), (early_lag, pass_early), (early_lag + 1, take_early)
        ):
            @pl.when(j >= delay)
            def _(delay=delay, step=step):
                step(j - delay)

    def send_docs(j, done):
        picked = jnp.dot(late_chooser[...], done, preferred_element_type=jnp.float32)
        picked = picked.astype(jnp.bfloat16)
        for slot in range(len(late_masks)):
            packed[slot, :, cols(j)] = picked[slot * capacity:(slot + 1) * capacity]
        for k in reversed(range(1, len(late_masks))):
            doc_remote(k, j).start()
        own_store(j).start()

    def store_early(j, early):
        kept = jnp.where(valid[...] > 0.0, early.astype(jnp.float32), 0.0).astype(jnp.bfloat16)
        for slot in range(half):
            early_out[slot, :, cols(j)] = kept[slot * capacity:(slot + 1) * capacity]
        for slot in range(half):
            early_store(slot, j).start()

    def send_and_store(j, done, early):
        send_docs(j, done)
        store_early(j, early)

    lax.fori_loop(0, cols_wide // 128, fill_spread, 0)
    fill_mask(meta)
    fill_early_mask()
    clear_sums()
    with mark("PX_barrier"):
        pl.semaphore_wait(barrier, greeted)
    with mark("P1_xsend"):
        for j in range(n_chunks):
            x_copy(j).wait()
            x_remote(j).start()
    meta_remote().start()
    for c in range(SLOTS):
        ring_copy(c).start()
    with mark("P2_own"):
        absorb_half(x_own, side)
        multiply_half(0)
    with mark("P3_xwait"):
        for j in range(n_chunks):
            x_remote(j).wait()
    with mark("P4_other"):
        absorb_half(x_other, other)
        multiply_half(1)
    with mark("P5_kv"):
        keys_values(0)
        clear_sums()
    with mark("P6_first"):
        run_span(0, 0, 0, 1, 0, rows, (attend_first,), send_next, kv_remote(0).wait)
    with mark("P7_meta"):
        meta_remote().wait()
        for k in range(half):
            meta_on(k).start()
        fill_choosers(meta_next)
    with mark("P8_layer0"):
        run_span(0, 0, 1, n_chunks, 0, rows, (attend_first,), send_next)
    with mark("P9_rest"):
        fill_mask(meta_next)
        for k in range(half):
            meta_on(k).wait()
        fill_valid()
        behind = early_lag - lag
        for j in range(n_chunks - lag, n_chunks):
            pass_on(j)
            take_local(j - 1)
            pass_early(j - behind)
            take_early(j - 1 - behind)
    with mark("PA_last"):
        take_local(n_chunks - 1)
    with mark("PB_kv"):
        keys_values(1)
    with mark("PC_first"):
        run_span(1, n_chunks, 0, 1, 0, rows, (attend_local,), send_docs, kv_remote(1).wait)
    with mark("PD_local"):
        run_span(1, n_chunks, 1, LEAD, 0, rows, (attend_local,), send_docs)
    with mark("PE_early"):
        for j in range(n_chunks - behind, n_chunks):
            pass_early(j)
            take_early(j - 1)
        take_early(n_chunks - 1)
        keys_values(2)
    with mark("PF_both"):
        run_span(
            1, n_chunks, LEAD, n_chunks, 0, rows + early_rows, (attend_local, attend_early),
            send_and_store, kv_remote(2).wait,
        )
    with mark("PG_early"):
        run_span(1, STEPS * n_chunks, 0, LEAD, rows, early_rows, (attend_early,), store_early)
    with mark("PH_sends"):
        for j in range(n_chunks):
            h_remote(j).wait_send()
            forward_remote(j).wait_send()
            early_forward(j).wait_send()
            for k in range(half):
                early_remote(k, j).wait_send()
        for slot in range(half):
            early_stored(slot).wait()
        own_stored().wait()
    with mark("PI_docs"):
        for k in range(1, len(late_masks)):
            doc_all(k).wait()


def fused_device(sizes, hidden, doc_lengths, doc_target, norm_gain, q_weight, kv_weight):
    n_dp, n_pipe, docs = sizes
    rows, width = hidden.shape[1:]
    features = norm_gain.shape[1]
    n_chunks = width // CHUNK
    n_kv = kv_weight.shape[2]
    own_kv = KV_HEADS // 2
    capacity = rows // 4
    chunk_heads = CHUNK // HD
    bf16 = jnp.bfloat16
    dma = pltpu.SemaphoreType.DMA
    vmem = pltpu.VMEM
    early_masks, late_masks = split_masks(n_dp)
    half, n_late = len(early_masks), len(late_masks)
    early_rows = half * capacity
    most = rows + early_rows
    blocks = vmem((n_chunks, rows, CHUNK), bf16)
    early_blocks = vmem((n_chunks, early_rows, CHUNK), bf16)
    result = pl.pallas_call(
        functools.partial(fused_kernel, sizes),
        out_shape=jax.ShapeDtypeStruct((n_dp * capacity, width), bf16),
        in_specs=[
            pl.BlockSpec(memory_space=pl.ANY),
            pl.BlockSpec(memory_space=pltpu.VMEM),
            pl.BlockSpec(memory_space=pltpu.VMEM),
            pl.BlockSpec(memory_space=pltpu.VMEM),
            pl.BlockSpec(memory_space=pl.ANY),
            pl.BlockSpec(memory_space=pl.ANY),
        ],
        out_specs=pl.BlockSpec(memory_space=pl.ANY),
        scratch_shapes=[
            vmem((8, 128), jnp.int32),
            blocks, blocks, blocks, blocks, blocks, early_blocks, early_blocks,
            vmem((n_chunks, half, capacity, CHUNK), bf16),
            vmem((8, 128), jnp.int32),
            vmem((half, 8, 128), jnp.int32),
            vmem((rows, features), bf16),
            vmem((most, features), bf16),
            vmem((n_kv, n_kv), bf16),
            vmem((most, n_kv), jnp.float32),
            vmem((most, CHUNK), jnp.float32),
            vmem((most, CHUNK), jnp.float32),
            vmem((STEPS, own_kv, most, HD), bf16),
            vmem((STEPS, 2, own_kv, most, HD), bf16),
            vmem((features, n_kv), bf16),
            vmem((SLOTS, features, CHUNK), bf16),
            vmem((chunk_heads * rows, rows), jnp.float32),
            vmem((chunk_heads * early_rows, early_rows), jnp.float32),
            vmem((early_rows, CHUNK), jnp.float32),
            vmem((early_rows, rows), bf16),
            vmem((n_late * capacity, rows), bf16),
            vmem((2, most, CHUNK), bf16),
            vmem((n_late, capacity, width), bf16),
            vmem((half, capacity, width), bf16),
            dma((n_chunks,)), dma((n_chunks,)), dma((n_chunks,)), dma, dma,
            dma((features // KV_ROWS,)), dma((SLOTS,)), dma((STEPS + 1,)), dma((STEPS + 1,)),
            dma((n_chunks,)), dma((n_chunks,)), dma((n_chunks,)), dma((n_chunks,)),
            dma((n_late,)), dma((n_late,)), dma((half + 1,)),
            dma((half, n_chunks)), dma((half, n_chunks)), dma((n_chunks,)), dma((n_chunks,)),
            dma((half,)), dma((half,)),
        ],
        compiler_params=pltpu.CompilerParams(
            collective_id=0, has_side_effects=True, vmem_limit_bytes=67043328
        ),
    )(hidden[0], doc_lengths[0], doc_target[0], norm_gain, q_weight[0], kv_weight[0])
    return result[None]


def solution(mesh):
    placed = (
        P("pipe", "dp", "tensor"),
        P("pipe", "dp", None),
        P("pipe", "dp", None),
        P("pipe", None),
        P("pipe", None, "tensor"),
        P("pipe", None, "tensor"),
    )
    run = on_device
    if mesh.shape["tensor"] == 2 and mesh.shape["dp"] in (4, 8, 16):
        sizes = (mesh.shape["dp"], mesh.shape["pipe"], mesh.shape["dp"])
        run = functools.partial(fused_device, sizes)
    return jax.shard_map(
        run, mesh=mesh, in_specs=placed, out_specs=P("pipe", "dp", "tensor"), check_vma=False
    )
```

```python
import contextlib
import functools

import jax
import jax.numpy as jnp
from jax import lax
from jax.experimental import pallas as pl
from jax.experimental.pallas import tpu as pltpu
from jax.sharding import PartitionSpec as P

D = 8192
HD = 128
KV_HEADS = 8
STEPS = 2


def passed_along(block, axis, distance):
    devices = range(lax.axis_size(axis))
    route = [((i - distance) % len(devices), i) for i in devices]
    return lax.ppermute(block, axis, route)


def build_send(token_rows, lengths, targets, capacity, groups):
    ordinal = jnp.arange(groups, dtype=jnp.int32)
    offsets = jnp.cumsum(lengths) - lengths
    onehot = (targets[None, :] == ordinal[:, None]).astype(jnp.int32)
    doc_sizes = jnp.sum(onehot * lengths[None, :], axis=1)
    doc_starts = jnp.sum(onehot * offsets[None, :], axis=1)
    within = jnp.arange(capacity, dtype=jnp.int32)
    row_index = jnp.minimum(doc_starts[:, None] + within[None, :], token_rows.shape[0] - 1)
    picked = jnp.take(token_rows, row_index.reshape(-1), axis=0).reshape(
        groups, capacity, token_rows.shape[1]
    )
    inside = within[None, :] < doc_sizes[:, None]
    return (jnp.where(inside[:, :, None], picked, jnp.zeros_like(picked)), doc_sizes)


def doc_masks(lengths, length):
    within = jnp.arange(length, dtype=jnp.int32)
    doc_ends = jnp.cumsum(lengths)
    segment = jnp.sum((within[:, None] >= doc_ends[None, :]).astype(jnp.int32), axis=1)
    causal = within[:, None] >= within[None, :]
    return (segment[:, None] == segment[None, :]) & causal


def attend_heads(queries, kv_local, allowed, local_rank):
    row_count = queries.shape[0]
    local_heads = queries.shape[1] // HD
    per_group = D // HD // KV_HEADS
    kv_count = max(1, local_heads // per_group)
    kv_first = local_rank * local_heads // per_group
    kv_whole = lax.all_gather(kv_local, "tensor", axis=1, tiled=True)
    kv_heads = kv_whole.reshape(row_count, 2, HD, KV_HEADS)
    own_heads = lax.dynamic_slice_in_dim(kv_heads, kv_first, kv_count, 3)
    key_rows = own_heads[:, 0]
    values = own_heads[:, 1]
    grouped = queries.reshape(row_count, kv_count, local_heads // kv_count, HD)
    scores = jnp.einsum(
        "qcph,khc->cpqk", grouped, key_rows, preferred_element_type=jnp.float32
    ) * HD ** (-0.5)
    exp_scores = jnp.where(allowed[None, None], jnp.exp(scores), 0.0)
    probabilities = (exp_scores / jnp.sum(exp_scores, axis=-1, keepdims=True)).astype(jnp.bfloat16)
    attended = jnp.einsum(
        "cpqk,khc->qcph", probabilities, values, preferred_element_type=jnp.float32
    )
    return attended.reshape(row_count, queries.shape[1])


def layer_pass(current, gain_full, query_cols, kv_cols, allowed):
    local_rank = lax.axis_index("tensor")
    widened = current.astype(jnp.float32)
    whole = lax.all_gather(current, "tensor", axis=1, tiled=True)
    whole_wide = whole.astype(jnp.float32)
    scale_row = lax.rsqrt(jnp.sum(whole_wide * whole_wide, axis=-1) / D + 1e-05)
    normed_full = (whole_wide * scale_row[:, None] * gain_full).astype(jnp.bfloat16)
    query_sum = jnp.dot(normed_full, query_cols, preferred_element_type=jnp.float32)
    kv_sum = jnp.dot(normed_full, kv_cols, preferred_element_type=jnp.float32)
    queries = query_sum.astype(jnp.bfloat16)
    kv_local = kv_sum.astype(jnp.bfloat16)
    attended = attend_heads(queries, kv_local, allowed, local_rank)
    return (widened + attended).astype(jnp.bfloat16)


def on_device(hidden, doc_lengths, doc_target, norm_gain, q_weight, kv_weight):
    groups = lax.axis_size("dp")
    current = hidden[0]
    lengths = doc_lengths[0, 0]
    targets = doc_target[0, 0]
    capacity = current.shape[0] // 4
    gain_full = norm_gain[0]
    query_cols = q_weight[0]
    kv_cols = kv_weight[0]
    carried = jnp.stack([lengths, targets]).astype(jnp.bfloat16)
    for layer_step in range(STEPS):
        allowed = doc_masks(carried[0].astype(jnp.int32), current.shape[0])
        current = layer_pass(current, gain_full, query_cols, kv_cols, allowed)
        if layer_step + 1 < STEPS:
            current, carried = passed_along((current, carried), "pipe", 1)
    final_lengths = carried[0].astype(jnp.int32)
    final_targets = carried[1].astype(jnp.int32)
    packed, doc_sizes = build_send(current, final_lengths, final_targets, capacity, groups)
    received = lax.all_to_all(packed, "dp", split_axis=0, concat_axis=0, tiled=True)
    return received.reshape(1, groups * capacity, received.shape[2])


CHUNK = 256
SLOTS = 6
KV_ROWS = 1024
LEAD = 4
PIECES = 4


mark = contextlib.nullcontext


def split_masks(n_dp):
    early = [m for m in range(n_dp) if m >= n_dp // 2 and m % 2 == 0]
    return early, [m for m in range(n_dp) if m not in early]


def fused_kernel(
    sizes, hidden, lengths, targets, gain, wq, wkv, out, meta,
    x_own, x_other, h_send, next_own, next_other, early_own, early_other, early_send,
    meta_next, meta_early, normed_first, normed_next, spread, kv_acc, squares, scales,
    kv_send, kv_heads, kv_weights, ring, mask, early_mask, valid, early_chooser, late_chooser,
    q_held, packed, early_out,
    sem_x, sem_xs, sem_xr, sem_ms, sem_mr, sem_kvw, sem_ring, sem_kvs, sem_kvr,
    sem_hs, sem_hr, sem_fs, sem_fr, sem_as, sem_ar, sem_own,
    sem_es, sem_er, sem_gs, sem_gr, sem_mes, sem_mer,
):
    n_dp, n_pipe, docs = sizes
    rows, width = hidden.shape
    features = gain.shape[1]
    n_chunks = width // CHUNK
    n_kv = wkv.shape[1]
    half_blocks = width // KV_ROWS
    own_kv = kv_heads.shape[2]
    chunk_heads = CHUNK // HD
    group_chunks = n_chunks // own_kv
    capacity = packed.shape[1]
    early_masks, late_masks = split_masks(n_dp)
    half = len(early_masks)
    early_rows = half * capacity
    dp = lax.axis_index("dp")
    pipe = lax.axis_index("pipe")
    side = lax.axis_index("tensor")
    other = 1 - side
    following = lax.rem(pipe + 1, n_pipe)
    preceding = lax.rem(pipe + n_pipe - 1, n_pipe)
    total = STEPS * n_chunks + LEAD
    normed_of = (normed_first, normed_next)

    def partner(flips):
        index, bit = dp, 1
        while bit < n_dp:
            if flips & bit:
                index = index + bit - 2 * bit * lax.rem(dp // bit, 2)
            bit *= 2
        return index

    early_partners = [partner(m) for m in early_masks]
    late_partners = [partner(m) for m in late_masks]

    def cols(j):
        return pl.ds(pl.multiple_of(j * CHUNK, CHUNK), CHUNK)

    def kv_rows(which, b):
        return pl.ds(pl.multiple_of((which * half_blocks + b) * KV_ROWS, KV_ROWS), KV_ROWS)

    def kv_copy(order, b):
        here = kv_rows((side, other)[order], b)
        return pltpu.make_async_copy(
            wkv.at[here], kv_weights.at[here], sem_kvw.at[order * half_blocks + b]
        )

    def ring_copy(c):
        slot = lax.rem(c, SLOTS)
        return pltpu.make_async_copy(
            wq.at[:, cols(lax.rem(c, n_chunks))], ring.at[slot], sem_ring.at[slot]
        )

    def x_copy(j):
        return pltpu.make_async_copy(hidden.at[:, cols(j)], x_own.at[j], sem_x.at[j])

    def x_remote(j):
        return pltpu.make_async_remote_copy(
            x_own.at[j], x_other.at[j], sem_xs.at[j], sem_xr.at[j],
            device_id={"tensor": other}, device_id_type=pl.DeviceIdType.MESH,
        )

    def meta_remote():
        return pltpu.make_async_remote_copy(
            meta, meta_next, sem_ms, sem_mr,
            device_id={"pipe": following}, device_id_type=pl.DeviceIdType.MESH,
        )

    def meta_on(k):
        return pltpu.make_async_remote_copy(
            meta_next, meta_early.at[k], sem_mes.at[k], sem_mer.at[k],
            device_id={"dp": early_partners[k]}, device_id_type=pl.DeviceIdType.MESH,
        )

    def early_remote(k, j):
        return pltpu.make_async_remote_copy(
            early_send.at[j, k], early_own.at[j, k * capacity:(k + 1) * capacity],
            sem_es.at[k, j], sem_er.at[k, j],
            device_id={"dp": early_partners[k]}, device_id_type=pl.DeviceIdType.MESH,
        )

    def early_forward(j):
        return pltpu.make_async_remote_copy(
            early_own.at[j], early_other.at[j], sem_gs.at[j], sem_gr.at[j],
            device_id={"tensor": other}, device_id_type=pl.DeviceIdType.MESH,
        )

    parts = ((0, 0, rows), (1, 0, rows), (1, rows, early_rows))

    def kv_remote(part):
        layer, first, count = parts[part]
        here = pl.ds(first, count)
        return pltpu.make_async_remote_copy(
            kv_send.at[layer, :, here], kv_heads.at[layer, side, :, here],
            sem_kvs.at[part], sem_kvr.at[part],
            device_id={"tensor": other}, device_id_type=pl.DeviceIdType.MESH,
        )

    def h_remote(j):
        return pltpu.make_async_remote_copy(
            h_send.at[j], next_own.at[j], sem_hs.at[j], sem_hr.at[j],
            device_id={"pipe": following}, device_id_type=pl.DeviceIdType.MESH,
        )

    def forward_remote(j):
        return pltpu.make_async_remote_copy(
            next_own.at[j], next_other.at[j], sem_fs.at[j], sem_fr.at[j],
            device_id={"tensor": other}, device_id_type=pl.DeviceIdType.MESH,
        )

    def doc_rows(index):
        return pl.ds(pl.multiple_of(index * capacity, capacity), capacity)

    def doc_remote(k, j):
        return pltpu.make_async_remote_copy(
            packed.at[k, :, cols(j)], out.at[doc_rows(dp), cols(j)],
            sem_as.at[k], sem_ar.at[k],
            device_id={"dp": late_partners[k]}, device_id_type=pl.DeviceIdType.MESH,
        )

    def doc_all(k):
        return pltpu.make_async_remote_copy(
            packed.at[k], out.at[doc_rows(late_partners[k])],
            sem_as.at[k], sem_ar.at[k],
            device_id={"dp": late_partners[k]}, device_id_type=pl.DeviceIdType.MESH,
        )

    def own_store(j):
        return pltpu.make_async_copy(
            packed.at[0, :, cols(j)], out.at[doc_rows(dp), cols(j)], sem_own.at[half]
        )

    def own_stored():
        return pltpu.make_async_copy(packed.at[0], out.at[doc_rows(dp)], sem_own.at[half])

    def early_store(k, j):
        return pltpu.make_async_copy(
            early_out.at[k, :, cols(j)], out.at[doc_rows(early_partners[k]), cols(j)],
            sem_own.at[k],
        )

    def early_stored(k):
        return pltpu.make_async_copy(
            early_out.at[k], out.at[doc_rows(early_partners[k])], sem_own.at[k]
        )

    for j in range(n_chunks):
        x_copy(j).start()
    barrier = pltpu.get_barrier_semaphore()
    pl.semaphore_signal(
        barrier, inc=1, device_id={"tensor": other}, device_id_type=pl.DeviceIdType.MESH
    )
    pl.semaphore_signal(
        barrier, inc=1, device_id={"pipe": following}, device_id_type=pl.DeviceIdType.MESH
    )
    greeted = n_dp + 1
    if n_pipe > 2:
        pl.semaphore_signal(
            barrier, inc=1, device_id={"pipe": preceding}, device_id_type=pl.DeviceIdType.MESH
        )
        greeted += 1
    for away in range(1, n_dp):
        pl.semaphore_signal(
            barrier, inc=1, device_id={"dp": lax.rem(dp + away, n_dp)},
            device_id_type=pl.DeviceIdType.MESH,
        )
    for order in range(2):
        for b in range(half_blocks):
            kv_copy(order, b).start()

    meta[...] = jnp.zeros(meta.shape, jnp.int32)
    meta[0:1, 0:docs] = lengths[...]
    meta[1:2, 0:docs] = targets[...]
    cols_wide = spread.shape[0]
    out_col = lax.broadcasted_iota(jnp.int32, (128, n_kv), 1)
    wanted = lax.rem(out_col, HD) * KV_HEADS + out_col // HD

    def fill_spread(i, carry):
        base = pl.multiple_of(i * 128, 128)
        row = lax.broadcasted_iota(jnp.int32, (128, n_kv), 0) + base
        spread[pl.ds(base, 128), :] = (row == wanted).astype(jnp.float32).astype(jnp.bfloat16)
        return carry

    def fill_mask(source):
        row = lax.broadcasted_iota(jnp.int32, (rows, rows), 0)
        col = lax.broadcasted_iota(jnp.int32, (rows, rows), 1)
        row_doc = jnp.zeros((rows, rows), jnp.int32)
        col_doc = jnp.zeros((rows, rows), jnp.int32)
        end = jnp.zeros((1, 1), jnp.int32)
        for d in range(docs):
            end = end + source[0:1, d:d + 1]
            row_doc = row_doc + (row >= end).astype(jnp.int32)
            col_doc = col_doc + (col >= end).astype(jnp.int32)
        allowed = jnp.where((row_doc == col_doc) & (row >= col), 1.0, 0.0)
        for i in range(chunk_heads):
            mask[i * rows:(i + 1) * rows, :] = allowed

    def fill_early_mask():
        row = lax.broadcasted_iota(jnp.int32, (early_rows, early_rows), 0)
        col = lax.broadcasted_iota(jnp.int32, (early_rows, early_rows), 1)
        allowed = jnp.where((row // capacity == col // capacity) & (row >= col), 1.0, 0.0)
        for i in range(chunk_heads):
            early_mask[i * early_rows:(i + 1) * early_rows, :] = allowed

    def fill_valid():
        row = lax.broadcasted_iota(jnp.int32, (capacity, CHUNK), 0)
        for slot in range(half):
            size = jnp.zeros((1, 1), jnp.int32)
            for d in range(docs):
                here = meta_early[slot, 1:2, d:d + 1] == dp
                size = size + jnp.where(here, meta_early[slot, 0:1, d:d + 1], 0)
            valid[slot * capacity:(slot + 1) * capacity, :] = jnp.where(row < size, 1.0, 0.0)

    def fill_choosers(source):
        row = lax.broadcasted_iota(jnp.int32, (1, rows), 1)
        goals = [jnp.full((1, rows), -1, jnp.int32) for _ in range(2)]
        begin = jnp.zeros((1, 1), jnp.int32)
        for d in range(docs):
            end = begin + source[0:1, d:d + 1]
            target = source[1:2, d:d + 1]
            inside = (row >= begin) & (row < end)
            for i, partners in enumerate((early_partners, late_partners)):
                first = jnp.full((1, 1), -n_dp * capacity, jnp.int32)
                for k, index in enumerate(partners):
                    first = jnp.where(target == index, k * capacity, first)
                goals[i] = jnp.where(inside, first + row - begin, goals[i])
            begin = end
        for ref, goal in zip((early_chooser, late_chooser), goals):
            slot = lax.broadcasted_iota(jnp.int32, ref.shape, 0)
            ref[...] = (slot == goal).astype(jnp.float32).astype(jnp.bfloat16)

    def absorb_half(held, which):
        def one(j, acc):
            wide = held[j].astype(jnp.float32)
            where = cols(which * n_chunks + j)
            normed_first[:, where] = (wide * gain[:, where]).astype(jnp.bfloat16)
            return acc + wide * wide

        squares[0:rows] = lax.fori_loop(0, n_chunks, one, squares[0:rows])

    def multiply_half(order):
        which = (side, other)[order]

        def one(b, carry):
            kv_copy(order, b).wait()
            here = kv_rows(which, b)
            kv_acc[0:rows] += jnp.dot(
                normed_first[:, here], kv_weights[here, :], preferred_element_type=jnp.float32
            )
            return carry

        lax.fori_loop(0, half_blocks, one, 0)

    def absorb_next(mine, theirs, first, count, j):
        here = slice(first, first + count)
        left, right = cols(side * n_chunks + j), cols(other * n_chunks + j)
        a = mine[j].astype(jnp.float32)
        b = theirs[j].astype(jnp.float32)
        squares[here] += a * a + b * b
        a = (a * gain[:, left]).astype(jnp.bfloat16)
        b = (b * gain[:, right]).astype(jnp.bfloat16)
        normed_next[here, left] = a
        normed_next[here, right] = b
        kv_acc[here] += jnp.dot(
            jnp.concatenate([a, b], axis=1),
            jnp.concatenate([kv_weights[left, :], kv_weights[right, :]], axis=0),
            preferred_element_type=jnp.float32,
        )

    def clear_sums():
        kv_acc[...] = jnp.zeros(kv_acc.shape, jnp.float32)
        squares[...] = jnp.zeros(squares.shape, jnp.float32)

    def keys_values(part):
        layer, first, count = parts[part]
        here = slice(first, first + count)
        scale = lax.rsqrt(jnp.sum(squares[here], axis=-1, keepdims=True) / features + 1e-05)
        scales[here] = jnp.broadcast_to(scale, (count, CHUNK))
        kv_cols = (kv_acc[here] * scale).astype(jnp.bfloat16)
        for which, keep in ((other, False), (side, True)):
            start = pl.multiple_of(which * own_kv * HD, own_kv * HD)
            heads = jnp.dot(
                kv_cols, spread[:, pl.ds(start, own_kv * HD)], preferred_element_type=jnp.float32
            ).astype(jnp.bfloat16)
            for g in range(own_kv):
                if keep:
                    kv_heads[layer, side, g, here] = heads[:, g * HD:(g + 1) * HD]
                else:
                    kv_send[layer, g, here] = heads[:, g * HD:(g + 1) * HD]
            if not keep:
                kv_remote(part).start()

    def query_piece(layer, c, first, count, piece):
        deep = slice(piece * features // PIECES, (piece + 1) * features // PIECES)
        return jnp.dot(
            normed_of[layer][first:first + count, deep], ring[lax.rem(c, SLOTS), deep],
            preferred_element_type=jnp.float32,
        )

    def attend(layer, j, mine, first, count, allowed):
        here = slice(first, first + count)
        q = q_held[lax.rem(j, 2), here]
        g = j // group_chunks
        stacked = jnp.concatenate([q[:, i * HD:(i + 1) * HD] for i in range(chunk_heads)], axis=0)
        scores = lax.dot_general(
            stacked, kv_heads[layer, 0, g, here], (((1,), (1,)), ((), ())),
            preferred_element_type=jnp.float32,
        ) * HD ** (-0.5)
        yield
        e = jnp.where(allowed[...] > 0.0, jnp.exp(scores), 0.0)
        p = (e * (1.0 / jnp.sum(e, axis=-1, keepdims=True))).astype(jnp.bfloat16)
        yield
        a = jnp.dot(p, kv_heads[layer, 1, g, here], preferred_element_type=jnp.float32)
        side_by_side = jnp.concatenate(
            [a[i * count:(i + 1) * count] for i in range(chunk_heads)], axis=1
        )
        yield (mine[j].astype(jnp.float32) + side_by_side).astype(jnp.bfloat16)

    def attend_first(j):
        return attend(0, j, x_own, 0, rows, mask)

    def attend_local(j):
        return attend(1, j, next_own, 0, rows, mask)

    def attend_early(j):
        return attend(1, j, early_own, rows, early_rows, early_mask)

    def refill(c):
        @pl.when(c + SLOTS < total)
        def _():
            ring_copy(c + SLOTS).start()

    def first_query(layer, c, first, count):
        ring_copy(c).wait()
        product = query_piece(layer, c, first, count, 0)
        for piece in range(1, PIECES):
            product = product + query_piece(layer, c, first, count, piece)
        q_held[0, first:first + count] = (product * scales[first:first + count]).astype(jnp.bfloat16)
        refill(jnp.int32(c))

    def step(layer, c, slot, first, count, before, attends, settles, extras=()):
        ring_copy(c).wait()
        stages = [attended(before) for attended in attends]
        product = None
        for piece in range(PIECES):
            done = [next(stage, None) for stage in stages]
            if piece == 2:
                made = done
            if piece == 3:
                for settle, value in zip(settles, made):
                    settle(before, value)
            for extra in extras[piece:piece + 1]:
                extra()
            part = query_piece(layer, c, first, count, piece)
            product = part if product is None else product + part
        here = slice(first, first + count)
        q_held[slot, here] = (product * scales[here]).astype(jnp.bfloat16)

    def last_step(before, attends, settles):
        stages = [attended(before) for attended in attends]
        for piece in range(3):
            made = [next(stage) for stage in stages]
        for settle, value in zip(settles, made):
            settle(before, value)

    def keep_next(j, done):
        h_send[j] = done

    def pass_on_start(j):
        h_remote(j).wait_recv()
        forward_remote(j).start()

    def pass_on_pick(j):
        picked = jnp.dot(
            early_chooser[...], next_own[j], preferred_element_type=jnp.float32
        ).astype(jnp.bfloat16)
        for slot in range(half):
            early_send[j, slot] = picked[slot * capacity:(slot + 1) * capacity]

    def pass_on_send(j):
        for k in range(half):
            early_remote(k, j).start()

    def pass_on(j):
        pass_on_start(j)
        pass_on_pick(j)
        pass_on_send(j)

    def absorb_local(j):
        absorb_next(next_own, next_other, 0, rows, j)

    def absorb_early(j):
        absorb_next(early_own, early_other, rows, early_rows, j)

    def pass_early(j):
        for k in range(half):
            early_remote(k, j).wait_recv()
        early_forward(j).start()

    def pick_docs(j, done):
        picked = jnp.dot(late_chooser[...], done, preferred_element_type=jnp.float32)
        picked = picked.astype(jnp.bfloat16)
        for slot in range(len(late_masks)):
            packed[slot, :, cols(j)] = picked[slot * capacity:(slot + 1) * capacity]

    def send_docs(j):
        for k in reversed(range(1, len(late_masks))):
            doc_remote(k, j).start()
        own_store(j).start()

    def keep_early(j, early):
        kept = jnp.where(valid[...] > 0.0, early.astype(jnp.float32), 0.0).astype(jnp.bfloat16)
        for slot in range(half):
            early_out[slot, :, cols(j)] = kept[slot * capacity:(slot + 1) * capacity]

    def store_early(j):
        for slot in range(half):
            early_store(slot, j).start()

    lag, early_lag = 5, 10

    def first_span(low, high, stage):
        def one(j, carry):
            on, local, gone, early = j - lag, j - lag - 1, j - early_lag, j - early_lag - 1
            extras = [[], [], [], []]
            if stage >= 1:
                pass_on_start(on)
                forward_remote(local).wait_recv()
                extras[0].append(functools.partial(absorb_local, local))
                extras[1].append(functools.partial(pass_on_pick, on))
            if stage >= 2:
                pass_early(gone)
                early_forward(early).wait_recv()
                extras[2].append(functools.partial(absorb_early, early))
            step(
                0, j, lax.rem(j, 2), 0, rows, j - 1, (attend_first,), (keep_next,),
                [functools.partial(run_all, group) for group in extras],
            )
            h_remote(j - 1).start()
            if stage >= 1:
                pass_on_send(on)
            refill(j)
            return carry

        lax.fori_loop(low, high, one, 0)

    def run_all(group):
        for task in group:
            task()

    lax.fori_loop(0, cols_wide // 128, fill_spread, 0)
    fill_mask(meta)
    fill_early_mask()
    clear_sums()
    with mark("PX_barrier"):
        pl.semaphore_wait(barrier, greeted)
    with mark("P1_xsend"):
        for j in range(n_chunks):
            x_copy(j).wait()
            x_remote(j).start()
    meta_remote().start()
    for c in range(SLOTS):
        ring_copy(c).start()
    with mark("P2_own"):
        absorb_half(x_own, side)
        multiply_half(0)
    with mark("P3_xwait"):
        for j in range(n_chunks):
            x_remote(j).wait()
    with mark("P4_other"):
        absorb_half(x_other, other)
        multiply_half(1)
    with mark("P5_kv"):
        keys_values(0)
        clear_sums()
    with mark("P6_first"):
        first_query(0, 0, 0, rows)
        kv_remote(0).wait()
    with mark("P7_span0"):
        first_span(1, lag + 1, 0)
    with mark("P8_meta"):
        meta_remote().wait()
        for k in range(half):
            meta_on(k).start()
        fill_choosers(meta_next)
        pass_on(0)
    with mark("P9_span1"):
        first_span(lag + 1, early_lag + 1, 1)
    with mark("PA_early0"):
        pass_early(0)
    with mark("PB_span2"):
        first_span(early_lag + 1, n_chunks, 2)
    with mark("PC_rest"):
        last_step(n_chunks - 1, (attend_first,), (keep_next,))
        h_remote(n_chunks - 1).start()
        fill_mask(meta_next)
        for k in range(half):
            meta_on(k).wait()
        fill_valid()
        gone = n_chunks - early_lag
        for j in range(n_chunks - lag, n_chunks):
            pass_on_start(j)
            pass_on_pick(j)
            pass_on_send(j)
            forward_remote(j - 1).wait_recv()
            absorb_local(j - 1)
            for _ in range(2):
                if gone < j - 3:
                    pass_early(gone)
                    early_forward(gone - 1).wait_recv()
                    absorb_early(gone - 1)
                    gone += 1
    with mark("PD_last"):
        forward_remote(n_chunks - 1).wait_recv()
        absorb_local(n_chunks - 1)
    with mark("PE_kv"):
        keys_values(1)
    with mark("PF_first"):
        first_query(1, n_chunks, 0, rows)
        kv_remote(1).wait()
    with mark("PG_local"):
        ready = gone - 1
        for j in range(1, LEAD + 1):
            count = rows + early_rows if j == LEAD else rows
            waiting = [] if j == 1 else [i for i in range(ready, ready + j - 1) if j < LEAD]
            for i in waiting:
                early_forward(i).wait_recv()
            ready += len(waiting)
            step(
                1, n_chunks + j, j % 2, 0, count, j - 1, (attend_local,), (pick_docs,),
                [functools.partial(absorb_early, i) for i in waiting],
            )
            send_docs(j - 1)
            refill(jnp.int32(n_chunks + j))
            if j == 1:
                for i in range(gone, n_chunks):
                    pass_early(i)
            if j == LEAD - 1:
                for i in range(ready, n_chunks):
                    early_forward(i).wait_recv()
                    absorb_early(i)
                keys_values(2)
        kv_remote(2).wait()
    with mark("PH_both"):
        def both(j, carry):
            step(
                1, n_chunks + j, lax.rem(j, 2), 0, rows + early_rows, j - 1,
                (attend_local, attend_early), (pick_docs, keep_early),
            )
            send_docs(j - 1)
            store_early(j - 1)
            refill(n_chunks + j)
            return carry

        lax.fori_loop(LEAD + 1, n_chunks, both, 0)
    with mark("PI_turn"):
        step(
            1, total - LEAD, 0, rows, early_rows, n_chunks - 1,
            (attend_local, attend_early), (pick_docs, keep_early),
        )
        send_docs(n_chunks - 1)
        store_early(n_chunks - 1)
    with mark("PJ_early"):
        def behind(j, carry):
            step(
                1, total - LEAD + j, lax.rem(j, 2), rows, early_rows, j - 1,
                (attend_early,), (keep_early,),
            )
            store_early(j - 1)
            return carry

        lax.fori_loop(1, LEAD, behind, 0)
        last_step(LEAD - 1, (attend_early,), (keep_early,))
        store_early(LEAD - 1)
    with mark("PK_sends"):
        for j in range(n_chunks):
            h_remote(j).wait_send()
            forward_remote(j).wait_send()
            early_forward(j).wait_send()
            for k in range(half):
                early_remote(k, j).wait_send()
        for slot in range(half):
            early_stored(slot).wait()
        own_stored().wait()
    with mark("PL_docs"):
        for k in range(1, len(late_masks)):
            doc_all(k).wait()


def fused_device(sizes, hidden, doc_lengths, doc_target, norm_gain, q_weight, kv_weight):
    n_dp, n_pipe, docs = sizes
    rows, width = hidden.shape[1:]
    features = norm_gain.shape[1]
    n_chunks = width // CHUNK
    n_kv = kv_weight.shape[2]
    own_kv = KV_HEADS // 2
    capacity = rows // 4
    chunk_heads = CHUNK // HD
    bf16 = jnp.bfloat16
    dma = pltpu.SemaphoreType.DMA
    vmem = pltpu.VMEM
    early_masks, late_masks = split_masks(n_dp)
    half, n_late = len(early_masks), len(late_masks)
    early_rows = half * capacity
    most = rows + early_rows
    blocks = vmem((n_chunks, rows, CHUNK), bf16)
    early_blocks = vmem((n_chunks, early_rows, CHUNK), bf16)
    result = pl.pallas_call(
        functools.partial(fused_kernel, sizes),
        out_shape=jax.ShapeDtypeStruct((n_dp * capacity, width), bf16),
        in_specs=[
            pl.BlockSpec(memory_space=pl.ANY),
            pl.BlockSpec(memory_space=pltpu.VMEM),
            pl.BlockSpec(memory_space=pltpu.VMEM),
            pl.BlockSpec(memory_space=pltpu.VMEM),
            pl.BlockSpec(memory_space=pl.ANY),
            pl.BlockSpec(memory_space=pl.ANY),
        ],
        out_specs=pl.BlockSpec(memory_space=pl.ANY),
        scratch_shapes=[
            vmem((8, 128), jnp.int32),
            blocks, blocks, blocks, blocks, blocks, early_blocks, early_blocks,
            vmem((n_chunks, half, capacity, CHUNK), bf16),
            vmem((8, 128), jnp.int32),
            vmem((half, 8, 128), jnp.int32),
            vmem((rows, features), bf16),
            vmem((most, features), bf16),
            vmem((n_kv, n_kv), bf16),
            vmem((most, n_kv), jnp.float32),
            vmem((most, CHUNK), jnp.float32),
            vmem((most, CHUNK), jnp.float32),
            vmem((STEPS, own_kv, most, HD), bf16),
            vmem((STEPS, 2, own_kv, most, HD), bf16),
            vmem((features, n_kv), bf16),
            vmem((SLOTS, features, CHUNK), bf16),
            vmem((chunk_heads * rows, rows), jnp.float32),
            vmem((chunk_heads * early_rows, early_rows), jnp.float32),
            vmem((early_rows, CHUNK), jnp.float32),
            vmem((early_rows, rows), bf16),
            vmem((n_late * capacity, rows), bf16),
            vmem((2, most, CHUNK), bf16),
            vmem((n_late, capacity, width), bf16),
            vmem((half, capacity, width), bf16),
            dma((n_chunks,)), dma((n_chunks,)), dma((n_chunks,)), dma, dma,
            dma((features // KV_ROWS,)), dma((SLOTS,)), dma((STEPS + 1,)), dma((STEPS + 1,)),
            dma((n_chunks,)), dma((n_chunks,)), dma((n_chunks,)), dma((n_chunks,)),
            dma((n_late,)), dma((n_late,)), dma((half + 1,)),
            dma((half, n_chunks)), dma((half, n_chunks)), dma((n_chunks,)), dma((n_chunks,)),
            dma((half,)), dma((half,)),
        ],
        compiler_params=pltpu.CompilerParams(
            collective_id=0, has_side_effects=True, vmem_limit_bytes=67043328
        ),
    )(hidden[0], doc_lengths[0], doc_target[0], norm_gain, q_weight[0], kv_weight[0])
    return result[None]


def solution(mesh):
    placed = (
        P("pipe", "dp", "tensor"),
        P("pipe", "dp", None),
        P("pipe", "dp", None),
        P("pipe", None),
        P("pipe", None, "tensor"),
        P("pipe", None, "tensor"),
    )
    run = on_device
    if mesh.shape["tensor"] == 2 and mesh.shape["dp"] in (4, 8, 16):
        sizes = (mesh.shape["dp"], mesh.shape["pipe"], mesh.shape["dp"])
        run = functools.partial(fused_device, sizes)
    return jax.shard_map(
        run, mesh=mesh, in_specs=placed, out_specs=P("pipe", "dp", "tensor"), check_vma=False
    )
```

```python
import contextlib
import functools

import jax
import jax.numpy as jnp
from jax import lax
from jax.experimental import pallas as pl
from jax.experimental.pallas import tpu as pltpu
from jax.sharding import PartitionSpec as P

D = 8192
HD = 128
KV_HEADS = 8
STEPS = 2


def passed_along(block, axis, distance):
    devices = range(lax.axis_size(axis))
    route = [((i - distance) % len(devices), i) for i in devices]
    return lax.ppermute(block, axis, route)


def build_send(token_rows, lengths, targets, capacity, groups):
    ordinal = jnp.arange(groups, dtype=jnp.int32)
    offsets = jnp.cumsum(lengths) - lengths
    onehot = (targets[None, :] == ordinal[:, None]).astype(jnp.int32)
    doc_sizes = jnp.sum(onehot * lengths[None, :], axis=1)
    doc_starts = jnp.sum(onehot * offsets[None, :], axis=1)
    within = jnp.arange(capacity, dtype=jnp.int32)
    row_index = jnp.minimum(doc_starts[:, None] + within[None, :], token_rows.shape[0] - 1)
    picked = jnp.take(token_rows, row_index.reshape(-1), axis=0).reshape(
        groups, capacity, token_rows.shape[1]
    )
    inside = within[None, :] < doc_sizes[:, None]
    return (jnp.where(inside[:, :, None], picked, jnp.zeros_like(picked)), doc_sizes)


def doc_masks(lengths, length):
    within = jnp.arange(length, dtype=jnp.int32)
    doc_ends = jnp.cumsum(lengths)
    segment = jnp.sum((within[:, None] >= doc_ends[None, :]).astype(jnp.int32), axis=1)
    causal = within[:, None] >= within[None, :]
    return (segment[:, None] == segment[None, :]) & causal


def attend_heads(queries, kv_local, allowed, local_rank):
    row_count = queries.shape[0]
    local_heads = queries.shape[1] // HD
    per_group = D // HD // KV_HEADS
    kv_count = max(1, local_heads // per_group)
    kv_first = local_rank * local_heads // per_group
    kv_whole = lax.all_gather(kv_local, "tensor", axis=1, tiled=True)
    kv_heads = kv_whole.reshape(row_count, 2, HD, KV_HEADS)
    own_heads = lax.dynamic_slice_in_dim(kv_heads, kv_first, kv_count, 3)
    key_rows = own_heads[:, 0]
    values = own_heads[:, 1]
    grouped = queries.reshape(row_count, kv_count, local_heads // kv_count, HD)
    scores = jnp.einsum(
        "qcph,khc->cpqk", grouped, key_rows, preferred_element_type=jnp.float32
    ) * HD ** (-0.5)
    exp_scores = jnp.where(allowed[None, None], jnp.exp(scores), 0.0)
    probabilities = (exp_scores / jnp.sum(exp_scores, axis=-1, keepdims=True)).astype(jnp.bfloat16)
    attended = jnp.einsum(
        "cpqk,khc->qcph", probabilities, values, preferred_element_type=jnp.float32
    )
    return attended.reshape(row_count, queries.shape[1])


def layer_pass(current, gain_full, query_cols, kv_cols, allowed):
    local_rank = lax.axis_index("tensor")
    widened = current.astype(jnp.float32)
    whole = lax.all_gather(current, "tensor", axis=1, tiled=True)
    whole_wide = whole.astype(jnp.float32)
    scale_row = lax.rsqrt(jnp.sum(whole_wide * whole_wide, axis=-1) / D + 1e-05)
    normed_full = (whole_wide * scale_row[:, None] * gain_full).astype(jnp.bfloat16)
    query_sum = jnp.dot(normed_full, query_cols, preferred_element_type=jnp.float32)
    kv_sum = jnp.dot(normed_full, kv_cols, preferred_element_type=jnp.float32)
    queries = query_sum.astype(jnp.bfloat16)
    kv_local = kv_sum.astype(jnp.bfloat16)
    attended = attend_heads(queries, kv_local, allowed, local_rank)
    return (widened + attended).astype(jnp.bfloat16)


def on_device(hidden, doc_lengths, doc_target, norm_gain, q_weight, kv_weight):
    groups = lax.axis_size("dp")
    current = hidden[0]
    lengths = doc_lengths[0, 0]
    targets = doc_target[0, 0]
    capacity = current.shape[0] // 4
    gain_full = norm_gain[0]
    query_cols = q_weight[0]
    kv_cols = kv_weight[0]
    carried = jnp.stack([lengths, targets]).astype(jnp.bfloat16)
    for layer_step in range(STEPS):
        allowed = doc_masks(carried[0].astype(jnp.int32), current.shape[0])
        current = layer_pass(current, gain_full, query_cols, kv_cols, allowed)
        if layer_step + 1 < STEPS:
            current, carried = passed_along((current, carried), "pipe", 1)
    final_lengths = carried[0].astype(jnp.int32)
    final_targets = carried[1].astype(jnp.int32)
    packed, doc_sizes = build_send(current, final_lengths, final_targets, capacity, groups)
    received = lax.all_to_all(packed, "dp", split_axis=0, concat_axis=0, tiled=True)
    return received.reshape(1, groups * capacity, received.shape[2])


CHUNK = 256
SLOTS = 6
KV_ROWS = 1024
LEAD = 6
PIECES = 4


mark = contextlib.nullcontext


def split_masks(n_dp):
    early = [m for m in range(n_dp) if m >= n_dp // 2 and m % 2 == 0]
    return early, [m for m in range(n_dp) if m not in early]


def fused_kernel(
    sizes, hidden, lengths_in, targets_in, gain_in, wq, wkv, out, meta, lengths, targets, gain,
    x_own, x_other, h_send, next_own, next_other, early_own, early_other, early_send,
    meta_next, meta_early, normed_first, normed_next, spread, kv_acc, kv_cols, squares, scales,
    kv_send, kv_heads, kv_weights, ring, mask, early_mask, valid, early_chooser, late_chooser,
    q_held, begun, packed,
    sem_x, sem_xs, sem_xr, sem_ms, sem_mr, sem_kvw, sem_ring, sem_kvs, sem_kvr,
    sem_hs, sem_hr, sem_fs, sem_fr, sem_as, sem_ar,
    sem_es, sem_er, sem_gs, sem_gr, sem_mes, sem_mer, sem_in,
):
    n_dp, n_pipe, docs = sizes
    rows, width = hidden.shape
    features = gain_in.shape[1]
    n_chunks = width // CHUNK
    n_kv = wkv.shape[1]
    half_blocks = width // KV_ROWS
    own_kv = kv_heads.shape[2]
    chunk_heads = CHUNK // HD
    group_chunks = n_chunks // own_kv
    capacity = packed.shape[1]
    early_masks, late_masks = split_masks(n_dp)
    half = len(early_masks)
    early_rows = half * capacity
    dp = lax.axis_index("dp")
    pipe = lax.axis_index("pipe")
    side = lax.axis_index("tensor")
    other = 1 - side
    following = lax.rem(pipe + 1, n_pipe)
    preceding = lax.rem(pipe + n_pipe - 1, n_pipe)
    total = STEPS * n_chunks + LEAD
    normed_of = (normed_first, normed_next)

    def partner(flips):
        index, bit = dp, 1
        while bit < n_dp:
            if flips & bit:
                index = index + bit - 2 * bit * lax.rem(dp // bit, 2)
            bit *= 2
        return index

    early_partners = [partner(m) for m in early_masks]
    late_partners = [partner(m) for m in late_masks]

    def cols(j):
        return pl.ds(pl.multiple_of(j * CHUNK, CHUNK), CHUNK)

    def kv_rows(which, b):
        return pl.ds(pl.multiple_of((which * half_blocks + b) * KV_ROWS, KV_ROWS), KV_ROWS)

    def kv_copy(order, b):
        here = kv_rows((side, other)[order], b)
        return pltpu.make_async_copy(
            wkv.at[here], kv_weights.at[here], sem_kvw.at[order * half_blocks + b]
        )

    def ring_copy(c):
        slot = lax.rem(c, SLOTS)
        return pltpu.make_async_copy(
            wq.at[:, cols(lax.rem(c, n_chunks))], ring.at[slot], sem_ring.at[slot]
        )

    def x_copy(j):
        return pltpu.make_async_copy(hidden.at[:, cols(j)], x_own.at[j], sem_x.at[j])

    def x_remote(j):
        return pltpu.make_async_remote_copy(
            x_own.at[j], x_other.at[j], sem_xs.at[j], sem_xr.at[j],
            device_id={"tensor": other}, device_id_type=pl.DeviceIdType.MESH,
        )

    def meta_remote():
        return pltpu.make_async_remote_copy(
            meta, meta_next, sem_ms, sem_mr,
            device_id={"pipe": following}, device_id_type=pl.DeviceIdType.MESH,
        )

    def meta_on(k):
        return pltpu.make_async_remote_copy(
            meta_next, meta_early.at[k], sem_mes.at[k], sem_mer.at[k],
            device_id={"dp": early_partners[k]}, device_id_type=pl.DeviceIdType.MESH,
        )

    def early_remote(k, j):
        return pltpu.make_async_remote_copy(
            early_send.at[j, k], early_own.at[j, k * capacity:(k + 1) * capacity],
            sem_es.at[k, j], sem_er.at[k, j],
            device_id={"dp": early_partners[k]}, device_id_type=pl.DeviceIdType.MESH,
        )

    def early_forward(j):
        return pltpu.make_async_remote_copy(
            early_own.at[j], early_other.at[j], sem_gs.at[j], sem_gr.at[j],
            device_id={"tensor": other}, device_id_type=pl.DeviceIdType.MESH,
        )

    parts = ((0, 0, rows), (1, 0, rows), (1, rows, early_rows))

    def kv_remote(part):
        layer, first, count = parts[part]
        here = pl.ds(first, count)
        return pltpu.make_async_remote_copy(
            kv_send.at[layer, :, here], kv_heads.at[layer, side, :, here],
            sem_kvs.at[part], sem_kvr.at[part],
            device_id={"tensor": other}, device_id_type=pl.DeviceIdType.MESH,
        )

    def h_remote(j):
        return pltpu.make_async_remote_copy(
            h_send.at[j], next_own.at[j], sem_hs.at[j], sem_hr.at[j],
            device_id={"pipe": following}, device_id_type=pl.DeviceIdType.MESH,
        )

    def forward_remote(j):
        return pltpu.make_async_remote_copy(
            next_own.at[j], next_other.at[j], sem_fs.at[j], sem_fr.at[j],
            device_id={"tensor": other}, device_id_type=pl.DeviceIdType.MESH,
        )

    def doc_rows(index):
        return pl.ds(pl.multiple_of(index * capacity, capacity), capacity)

    def doc_remote(k, j):
        return pltpu.make_async_remote_copy(
            packed.at[k, :, cols(j)], out.at[doc_rows(dp), cols(j)],
            sem_as.at[k], sem_ar.at[k],
            device_id={"dp": late_partners[k]}, device_id_type=pl.DeviceIdType.MESH,
        )

    def doc_all(k):
        return pltpu.make_async_remote_copy(
            packed.at[k], out.at[doc_rows(late_partners[k])],
            sem_as.at[k], sem_ar.at[k],
            device_id={"dp": late_partners[k]}, device_id_type=pl.DeviceIdType.MESH,
        )

    small = [
        pltpu.make_async_copy(*pair, sem_in.at[i])
        for i, pair in enumerate(((lengths_in, lengths), (targets_in, targets), (gain_in, gain)))
    ]
    for j in range(n_chunks):
        x_copy(j).start()
    for copy in small:
        copy.start()
    barrier = pltpu.get_barrier_semaphore()
    pl.semaphore_signal(
        barrier, inc=1, device_id={"tensor": other}, device_id_type=pl.DeviceIdType.MESH
    )
    pl.semaphore_signal(
        barrier, inc=1, device_id={"pipe": following}, device_id_type=pl.DeviceIdType.MESH
    )
    greeted = n_dp + 1
    if n_pipe > 2:
        pl.semaphore_signal(
            barrier, inc=1, device_id={"pipe": preceding}, device_id_type=pl.DeviceIdType.MESH
        )
        greeted += 1
    for away in range(1, n_dp):
        pl.semaphore_signal(
            barrier, inc=1, device_id={"dp": lax.rem(dp + away, n_dp)},
            device_id_type=pl.DeviceIdType.MESH,
        )
    for order in range(2):
        for b in range(half_blocks):
            kv_copy(order, b).start()

    cols_wide = spread.shape[0]
    out_col = lax.broadcasted_iota(jnp.int32, (128, n_kv), 1)
    wanted = lax.rem(out_col, HD) * KV_HEADS + out_col // HD

    def fill_spread(i, carry):
        base = pl.multiple_of(i * 128, 128)
        row = lax.broadcasted_iota(jnp.int32, (128, n_kv), 0) + base
        spread[pl.ds(base, 128), :] = (row == wanted).astype(jnp.float32).astype(jnp.bfloat16)
        return carry

    def fill_mask(source):
        row = lax.broadcasted_iota(jnp.int32, (rows, rows), 0)
        col = lax.broadcasted_iota(jnp.int32, (rows, rows), 1)
        row_doc = jnp.zeros((rows, rows), jnp.int32)
        col_doc = jnp.zeros((rows, rows), jnp.int32)
        end = jnp.zeros((1, 1), jnp.int32)
        for d in range(docs):
            end = end + source[0:1, d:d + 1]
            row_doc = row_doc + (row >= end).astype(jnp.int32)
            col_doc = col_doc + (col >= end).astype(jnp.int32)
        allowed = jnp.where((row_doc == col_doc) & (row >= col), 1.0, 0.0)
        for i in range(chunk_heads):
            mask[i * rows:(i + 1) * rows, :] = allowed

    def fill_early_mask():
        row = lax.broadcasted_iota(jnp.int32, (early_rows, early_rows), 0)
        col = lax.broadcasted_iota(jnp.int32, (early_rows, early_rows), 1)
        allowed = jnp.where((row // capacity == col // capacity) & (row >= col), 1.0, 0.0)
        for i in range(chunk_heads):
            early_mask[i * early_rows:(i + 1) * early_rows, :] = allowed

    def fill_valid():
        row = lax.broadcasted_iota(jnp.int32, (capacity, CHUNK), 0)
        for slot in range(half):
            size = jnp.zeros((1, 1), jnp.int32)
            for d in range(docs):
                here = meta_early[slot, 1:2, d:d + 1] == dp
                size = size + jnp.where(here, meta_early[slot, 0:1, d:d + 1], 0)
            valid[slot * capacity:(slot + 1) * capacity, :] = jnp.where(row < size, 1.0, 0.0)

    def fill_choosers(source):
        row = lax.broadcasted_iota(jnp.int32, (1, rows), 1)
        goals = [jnp.full((1, rows), -1, jnp.int32) for _ in range(2)]
        begin = jnp.zeros((1, 1), jnp.int32)
        for d in range(docs):
            end = begin + source[0:1, d:d + 1]
            target = source[1:2, d:d + 1]
            inside = (row >= begin) & (row < end)
            for i, partners in enumerate((early_partners, late_partners)):
                first = jnp.full((1, 1), -n_dp * capacity, jnp.int32)
                for k, index in enumerate(partners):
                    first = jnp.where(target == index, k * capacity, first)
                goals[i] = jnp.where(inside, first + row - begin, goals[i])
            begin = end
        for ref, goal in zip((early_chooser, late_chooser), goals):
            slot = lax.broadcasted_iota(jnp.int32, ref.shape, 0)
            ref[...] = (slot == goal).astype(jnp.float32).astype(jnp.bfloat16)

    def absorb_half(held, which):
        def one(j, acc):
            wide = held[j].astype(jnp.float32)
            where = cols(which * n_chunks + j)
            normed_first[:, where] = (wide * gain[:, where]).astype(jnp.bfloat16)
            return acc + wide * wide

        squares[0:rows] = lax.fori_loop(0, n_chunks, one, squares[0:rows])

    def multiply_half(order):
        which = (side, other)[order]

        def one(b, carry):
            kv_copy(order, b).wait()
            here = kv_rows(which, b)
            kv_acc[0:rows] += jnp.dot(
                normed_first[:, here], kv_weights[here, :], preferred_element_type=jnp.float32
            )
            return carry

        lax.fori_loop(0, half_blocks, one, 0)

    def absorb_next(mine, theirs, first, count, chunks):
        here = slice(first, first + count)
        total = squares[here]
        left, right = [], []
        for j in chunks:
            for held, which in ((mine, side), (theirs, other)):
                where = cols(which * n_chunks + j)
                wide = held[j].astype(jnp.float32)
                total = total + wide * wide
                scaled = (wide * gain[:, where]).astype(jnp.bfloat16)
                normed_next[here, where] = scaled
                left.append(scaled)
                right.append(kv_weights[where, :])
        squares[here] = total
        kv_acc[here] += jnp.dot(
            jnp.concatenate(left, axis=1), jnp.concatenate(right, axis=0),
            preferred_element_type=jnp.float32,
        )

    def clear_sums():
        kv_acc[...] = jnp.zeros(kv_acc.shape, jnp.float32)
        squares[...] = jnp.zeros(squares.shape, jnp.float32)

    def keys_values(part):
        layer, first, count = parts[part]
        here = slice(first, first + count)
        scale = lax.rsqrt(jnp.sum(squares[here], axis=-1, keepdims=True) / features + 1e-05)
        scales[here] = jnp.broadcast_to(scale, (count, CHUNK))
        kv_cols[here] = (kv_acc[here] * scale).astype(jnp.bfloat16)
        heads = kv_spread(part, other)
        for g in range(own_kv):
            kv_send[layer, g, here] = heads[:, g * HD:(g + 1) * HD]
        kv_remote(part).start()

    def kv_spread(part, which):
        _, first, count = parts[part]
        start = pl.multiple_of(which * own_kv * HD, own_kv * HD)
        return jnp.dot(
            kv_cols[first:first + count], spread[:, pl.ds(start, own_kv * HD)],
            preferred_element_type=jnp.float32,
        ).astype(jnp.bfloat16)

    def keep_heads(part):
        layer, first, count = parts[part]
        heads = kv_spread(part, side)
        for g in range(own_kv):
            kv_heads[layer, side, g, first:first + count] = heads[:, g * HD:(g + 1) * HD]

    def query_piece(layer, c, first, count, piece):
        deep = slice(piece * features // PIECES, (piece + 1) * features // PIECES)
        return jnp.dot(
            normed_of[layer][first:first + count, deep], ring[lax.rem(c, SLOTS), deep],
            preferred_element_type=jnp.float32,
        )

    def attend(layer, j, mine, first, count, allowed):
        here = slice(first, first + count)
        q = q_held[lax.rem(j, 2), here]
        g = j // group_chunks
        stacked = jnp.concatenate([q[:, i * HD:(i + 1) * HD] for i in range(chunk_heads)], axis=0)
        scores = lax.dot_general(
            stacked, kv_heads[layer, 0, g, here], (((1,), (1,)), ((), ())),
            preferred_element_type=jnp.float32,
        ) * HD ** (-0.5)
        yield
        e = jnp.where(allowed[...] > 0.0, jnp.exp(scores), 0.0)
        p = (e * (1.0 / jnp.sum(e, axis=-1, keepdims=True))).astype(jnp.bfloat16)
        yield
        a = jnp.dot(p, kv_heads[layer, 1, g, here], preferred_element_type=jnp.float32)
        side_by_side = jnp.concatenate(
            [a[i * count:(i + 1) * count] for i in range(chunk_heads)], axis=1
        )
        yield (mine[j].astype(jnp.float32) + side_by_side).astype(jnp.bfloat16)

    def attend_first(j):
        return attend(0, j, x_own, 0, rows, mask)

    def attend_local(j):
        return attend(1, j, next_own, 0, rows, mask)

    def attend_early(j):
        return attend(1, j, early_own, rows, early_rows, early_mask)

    def refill(c):
        @pl.when(c + SLOTS < total)
        def _():
            ring_copy(c + SLOTS).start()

    def first_query(layer, c):
        ring_copy(c).wait()
        product = query_piece(layer, c, 0, rows, 0)
        for piece in range(1, PIECES):
            product = product + query_piece(layer, c, 0, rows, piece)
        q_held[0, 0:rows] = (product * scales[0:rows]).astype(jnp.bfloat16)
        refill(jnp.int32(c))

    lag, early_lag = 5, 10
    early_deep = (n_chunks - lag + 1) * CHUNK

    def query_part(c, low, high):
        product = None
        for start in (0, width):
            deep = slice(start + low, start + high)
            part = jnp.dot(
                normed_next[0:rows, deep], ring[lax.rem(c, SLOTS), deep],
                preferred_element_type=jnp.float32,
            )
            product = part if product is None else product + part
        return product

    def begin_query(c):
        ring_copy(c).wait()
        begun[...] = query_part(c, 0, early_deep)

    def end_query(c):
        product = begun[...] + query_part(c, early_deep, width)
        q_held[0, 0:rows] = (product * scales[0:rows]).astype(jnp.bfloat16)
        refill(jnp.int32(c))

    def step(layer, c, slot, first, count, before, attends, settles, extras=()):
        ring_copy(c).wait()
        stages = [attended(before) for attended in attends]
        product = None
        for piece in range(PIECES):
            done = [next(stage, None) for stage in stages]
            if piece == 2:
                made = done
            if piece == 3:
                for settle, value in zip(settles, made):
                    settle(before, value)
            for extra in extras[piece:piece + 1]:
                extra()
            part = query_piece(layer, c, first, count, piece)
            product = part if product is None else product + part
        here = slice(first, first + count)
        q_held[slot, here] = (product * scales[here]).astype(jnp.bfloat16)

    def last_step(before, attends, settles):
        stages = [attended(before) for attended in attends]
        for piece in range(3):
            made = [next(stage) for stage in stages]
        for settle, value in zip(settles, made):
            settle(before, value)

    def keep_next(j, done):
        h_send[j] = done

    def pass_on_start(j):
        h_remote(j).wait_recv()
        forward_remote(j).start()

    def pass_on_pick(j):
        picked = jnp.dot(
            early_chooser[...], next_own[j], preferred_element_type=jnp.float32
        ).astype(jnp.bfloat16)
        for slot in range(half):
            early_send[j, slot] = picked[slot * capacity:(slot + 1) * capacity]

    def pass_on_send(j):
        for k in range(half):
            early_remote(k, j).start()

    def pass_on(j):
        pass_on_start(j)
        pass_on_pick(j)
        pass_on_send(j)

    def absorb_local(*chunks):
        absorb_next(next_own, next_other, 0, rows, chunks)

    def absorb_early(*chunks):
        absorb_next(early_own, early_other, rows, early_rows, chunks)

    def pass_early(j):
        for k in range(half):
            early_remote(k, j).wait_recv()
        early_forward(j).start()

    def pick_docs(j, done):
        picked = jnp.dot(late_chooser[...], done, preferred_element_type=jnp.float32)
        picked = picked.astype(jnp.bfloat16)
        out[doc_rows(dp), cols(j)] = picked[0:capacity]
        for slot in range(1, len(late_masks)):
            packed[slot, :, cols(j)] = picked[slot * capacity:(slot + 1) * capacity]

    def send_docs(j):
        for k in reversed(range(1, len(late_masks))):
            doc_remote(k, j).start()

    def keep_early(j, early):
        kept = jnp.where(valid[...] > 0.0, early.astype(jnp.float32), 0.0).astype(jnp.bfloat16)
        for slot in range(half):
            out[doc_rows(early_partners[slot]), cols(j)] = kept[slot * capacity:(slot + 1) * capacity]

    def first_span(low, high, stage):
        def one(j, carry):
            on, local, gone, early = j - lag, j - lag - 1, j - early_lag, j - early_lag - 1
            extras = [[], [], [], []]
            if stage >= 1:
                pass_on_start(on)
                forward_remote(local).wait_recv()
                extras[0].append(functools.partial(absorb_local, local))
                extras[1].append(functools.partial(pass_on_pick, on))
            if stage >= 2:
                pass_early(gone)
                early_forward(early).wait_recv()
                extras[2].append(functools.partial(absorb_early, early))
            step(
                0, j, lax.rem(j, 2), 0, rows, j - 1, (attend_first,), (keep_next,),
                [functools.partial(run_all, group) for group in extras],
            )
            h_remote(j - 1).start()
            if stage >= 1:
                pass_on_send(on)
            refill(j)
            return carry

        lax.fori_loop(low, high, one, 0)

    def run_all(group):
        for task in group:
            task()

    lax.fori_loop(0, cols_wide // 128, fill_spread, 0)
    fill_early_mask()
    clear_sums()
    for copy in small:
        copy.wait()
    meta[...] = jnp.zeros(meta.shape, jnp.int32)
    meta[0:1, 0:docs] = lengths[...]
    meta[1:2, 0:docs] = targets[...]
    fill_mask(meta)
    with mark("PX_barrier"):
        pl.semaphore_wait(barrier, greeted)
    with mark("P1_xsend"):
        for j in range(n_chunks):
            x_copy(j).wait()
            x_remote(j).start()
    meta_remote().start()
    for c in range(SLOTS):
        ring_copy(c).start()
    with mark("P2_own"):
        absorb_half(x_own, side)
        multiply_half(0)
    with mark("P3_xwait"):
        for j in range(n_chunks):
            x_remote(j).wait()
    with mark("P4_other"):
        absorb_half(x_other, other)
        multiply_half(1)
    with mark("P5_kv"):
        keys_values(0)
    with mark("P6_first"):
        first_query(0, 0)
        keep_heads(0)
        kv_remote(0).wait()
    with mark("P7_span0"):
        first_span(1, lag + 1, 0)
    with mark("P8_meta"):
        meta_remote().wait()
        for k in range(half):
            meta_on(k).start()
        fill_choosers(meta_next)
        clear_sums()
        pass_on(0)
    with mark("P9_span1"):
        first_span(lag + 1, early_lag + 1, 1)
    with mark("PA_early0"):
        pass_early(0)
    with mark("PB_span2"):
        first_span(early_lag + 1, n_chunks, 2)
    with mark("PC_rest"):
        last_step(n_chunks - 1, (attend_first,), (keep_next,))
        h_remote(n_chunks - 1).start()
        fill_mask(meta_next)
        for k in range(half):
            meta_on(k).wait()
        fill_valid()
        gone = n_chunks - early_lag
        for j in range(n_chunks - lag, n_chunks):
            pass_on_start(j)
            pass_on_pick(j)
            pass_on_send(j)
            forward_remote(j - 1).wait_recv()
            absorb_local(j - 1)
            if j == n_chunks - lag + 1:
                begin_query(n_chunks)
            for _ in range(2):
                if gone < j - 4:
                    pass_early(gone)
                    early_forward(gone - 1).wait_recv()
                    absorb_early(gone - 1)
                    gone += 1
    with mark("PD_last"):
        forward_remote(n_chunks - 1).wait_recv()
        absorb_local(n_chunks - 1)
    with mark("PE_kv"):
        keys_values(1)
    with mark("PF_first"):
        end_query(n_chunks)
        keep_heads(1)
        kv_remote(1).wait()
    with mark("PG_local"):
        def local(j, carry):
            step(
                1, n_chunks + j, lax.rem(j, 2), 0, rows, j - 1, (attend_local,), (pick_docs,)
            )
            send_docs(j - 1)
            refill(n_chunks + j)
            return carry

        lax.fori_loop(1, LEAD - 1, local, 0)
        for i in range(gone, n_chunks):
            pass_early(i)
        lax.fori_loop(LEAD - 1, LEAD, local, 0)
        for i in range(gone - 1, n_chunks):
            early_forward(i).wait_recv()
        absorb_early(*range(gone - 1, n_chunks))
        keys_values(2)
        step(
            1, n_chunks + LEAD, LEAD % 2, 0, rows + early_rows, LEAD - 1, (attend_local,), (pick_docs,)
        )
        send_docs(LEAD - 1)
        refill(jnp.int32(n_chunks + LEAD))
        keep_heads(2)
        kv_remote(2).wait()
    with mark("PH_both"):
        def both(j, carry):
            step(
                1, n_chunks + j, lax.rem(j, 2), 0, rows + early_rows, j - 1,
                (attend_local, attend_early), (pick_docs, keep_early),
            )
            send_docs(j - 1)
            refill(n_chunks + j)
            return carry

        lax.fori_loop(LEAD + 1, n_chunks, both, 0)
    with mark("PI_turn"):
        step(
            1, total - LEAD, 0, rows, early_rows, n_chunks - 1,
            (attend_local, attend_early), (pick_docs, keep_early),
        )
        send_docs(n_chunks - 1)
    with mark("PJ_early"):
        def behind(j, carry):
            step(
                1, total - LEAD + j, lax.rem(j, 2), rows, early_rows, j - 1,
                (attend_early,), (keep_early,),
            )
            return carry

        lax.fori_loop(1, LEAD, behind, 0)
        last_step(LEAD - 1, (attend_early,), (keep_early,))
    with mark("PK_sends"):
        for j in range(n_chunks):
            h_remote(j).wait_send()
            forward_remote(j).wait_send()
            early_forward(j).wait_send()
            for k in range(half):
                early_remote(k, j).wait_send()
    with mark("PL_docs"):
        for k in range(1, len(late_masks)):
            doc_all(k).wait()


def put_out(held, out, sem):
    copy = pltpu.make_async_copy(held, out, sem)
    copy.start()
    copy.wait()


def fused_device(sizes, hidden, doc_lengths, doc_target, norm_gain, q_weight, kv_weight):
    n_dp, n_pipe, docs = sizes
    rows, width = hidden.shape[1:]
    features = norm_gain.shape[1]
    n_chunks = width // CHUNK
    n_kv = kv_weight.shape[2]
    own_kv = KV_HEADS // 2
    capacity = rows // 4
    chunk_heads = CHUNK // HD
    bf16 = jnp.bfloat16
    dma = pltpu.SemaphoreType.DMA
    vmem = pltpu.VMEM
    early_masks, late_masks = split_masks(n_dp)
    half, n_late = len(early_masks), len(late_masks)
    early_rows = half * capacity
    most = rows + early_rows
    blocks = vmem((n_chunks, rows, CHUNK), bf16)
    early_blocks = vmem((n_chunks, early_rows, CHUNK), bf16)
    result = pl.pallas_call(
        functools.partial(fused_kernel, sizes),
        out_shape=vmem((n_dp * capacity, width), bf16),
        in_specs=[
            pl.BlockSpec(memory_space=pl.ANY),
            pl.BlockSpec(memory_space=pl.ANY),
            pl.BlockSpec(memory_space=pl.ANY),
            pl.BlockSpec(memory_space=pl.ANY),
            pl.BlockSpec(memory_space=pl.ANY),
            pl.BlockSpec(memory_space=pl.ANY),
        ],
        out_specs=pl.BlockSpec(memory_space=vmem),
        scratch_shapes=[
            vmem((8, 128), jnp.int32),
            vmem((1, docs), jnp.int32), vmem((1, docs), jnp.int32), vmem((1, features), jnp.float32),
            blocks, blocks, blocks, blocks, blocks, early_blocks, early_blocks,
            vmem((n_chunks, half, capacity, CHUNK), bf16),
            vmem((8, 128), jnp.int32),
            vmem((half, 8, 128), jnp.int32),
            vmem((rows, features), bf16),
            vmem((most, features), bf16),
            vmem((n_kv, n_kv), bf16),
            vmem((most, n_kv), jnp.float32),
            vmem((most, n_kv), bf16),
            vmem((most, CHUNK), jnp.float32),
            vmem((most, CHUNK), jnp.float32),
            vmem((STEPS, own_kv, most, HD), bf16),
            vmem((STEPS, 2, own_kv, most, HD), bf16),
            vmem((features, n_kv), bf16),
            vmem((SLOTS, features, CHUNK), bf16),
            vmem((chunk_heads * rows, rows), jnp.float32),
            vmem((chunk_heads * early_rows, early_rows), jnp.float32),
            vmem((early_rows, CHUNK), jnp.float32),
            vmem((early_rows, rows), bf16),
            vmem((n_late * capacity, rows), bf16),
            vmem((2, most, CHUNK), bf16),
            vmem((rows, CHUNK), jnp.float32),
            vmem((n_late, capacity, width), bf16),
            dma((n_chunks,)), dma((n_chunks,)), dma((n_chunks,)), dma, dma,
            dma((features // KV_ROWS,)), dma((SLOTS,)), dma((STEPS + 1,)), dma((STEPS + 1,)),
            dma((n_chunks,)), dma((n_chunks,)), dma((n_chunks,)), dma((n_chunks,)),
            dma((n_late,)), dma((n_late,)),
            dma((half, n_chunks)), dma((half, n_chunks)), dma((n_chunks,)), dma((n_chunks,)),
            dma((half,)), dma((half,)), dma((3,)),
        ],
        compiler_params=pltpu.CompilerParams(
            collective_id=0, has_side_effects=True, vmem_limit_bytes=64800000
        ),
    )(hidden[0], doc_lengths[0], doc_target[0], norm_gain, q_weight[0], kv_weight[0])
    return pl.pallas_call(
        put_out,
        out_shape=jax.ShapeDtypeStruct((n_dp * capacity, width), bf16),
        in_specs=[pl.BlockSpec(memory_space=vmem)],
        out_specs=pl.BlockSpec(memory_space=pl.ANY),
        scratch_shapes=[dma],
        compiler_params=pltpu.CompilerParams(vmem_limit_bytes=4194304),
    )(result)[None]


def solution(mesh):
    placed = (
        P("pipe", "dp", "tensor"),
        P("pipe", "dp", None),
        P("pipe", "dp", None),
        P("pipe", None),
        P("pipe", None, "tensor"),
        P("pipe", None, "tensor"),
    )
    run = on_device
    if mesh.shape["tensor"] == 2 and mesh.shape["dp"] in (4, 8, 16):
        sizes = (mesh.shape["dp"], mesh.shape["pipe"], mesh.shape["dp"])
        run = functools.partial(fused_device, sizes)
    return jax.shard_map(
        run, mesh=mesh, in_specs=placed, out_specs=P("pipe", "dp", "tensor"), check_vma=False
    )
```

```python
import contextlib
import functools

import jax
import jax.numpy as jnp
from jax import lax
from jax.experimental import pallas as pl
from jax.experimental.pallas import tpu as pltpu
from jax.sharding import PartitionSpec as P

D = 8192
HD = 128
KV_HEADS = 8
STEPS = 2


def passed_along(block, axis, distance):
    devices = range(lax.axis_size(axis))
    route = [((i - distance) % len(devices), i) for i in devices]
    return lax.ppermute(block, axis, route)


def build_send(token_rows, lengths, targets, capacity, groups):
    ordinal = jnp.arange(groups, dtype=jnp.int32)
    offsets = jnp.cumsum(lengths) - lengths
    onehot = (targets[None, :] == ordinal[:, None]).astype(jnp.int32)
    doc_sizes = jnp.sum(onehot * lengths[None, :], axis=1)
    doc_starts = jnp.sum(onehot * offsets[None, :], axis=1)
    within = jnp.arange(capacity, dtype=jnp.int32)
    row_index = jnp.minimum(doc_starts[:, None] + within[None, :], token_rows.shape[0] - 1)
    picked = jnp.take(token_rows, row_index.reshape(-1), axis=0).reshape(
        groups, capacity, token_rows.shape[1]
    )
    inside = within[None, :] < doc_sizes[:, None]
    return (jnp.where(inside[:, :, None], picked, jnp.zeros_like(picked)), doc_sizes)


def doc_masks(lengths, length):
    within = jnp.arange(length, dtype=jnp.int32)
    doc_ends = jnp.cumsum(lengths)
    segment = jnp.sum((within[:, None] >= doc_ends[None, :]).astype(jnp.int32), axis=1)
    causal = within[:, None] >= within[None, :]
    return (segment[:, None] == segment[None, :]) & causal


def attend_heads(queries, kv_local, allowed, local_rank):
    row_count = queries.shape[0]
    local_heads = queries.shape[1] // HD
    per_group = D // HD // KV_HEADS
    kv_count = max(1, local_heads // per_group)
    kv_first = local_rank * local_heads // per_group
    kv_whole = lax.all_gather(kv_local, "tensor", axis=1, tiled=True)
    kv_heads = kv_whole.reshape(row_count, 2, HD, KV_HEADS)
    own_heads = lax.dynamic_slice_in_dim(kv_heads, kv_first, kv_count, 3)
    key_rows = own_heads[:, 0]
    values = own_heads[:, 1]
    grouped = queries.reshape(row_count, kv_count, local_heads // kv_count, HD)
    scores = jnp.einsum(
        "qcph,khc->cpqk", grouped, key_rows, preferred_element_type=jnp.float32
    ) * HD ** (-0.5)
    exp_scores = jnp.where(allowed[None, None], jnp.exp(scores), 0.0)
    probabilities = (exp_scores / jnp.sum(exp_scores, axis=-1, keepdims=True)).astype(jnp.bfloat16)
    attended = jnp.einsum(
        "cpqk,khc->qcph", probabilities, values, preferred_element_type=jnp.float32
    )
    return attended.reshape(row_count, queries.shape[1])


def layer_pass(current, gain_full, query_cols, kv_cols, allowed):
    local_rank = lax.axis_index("tensor")
    widened = current.astype(jnp.float32)
    whole = lax.all_gather(current, "tensor", axis=1, tiled=True)
    whole_wide = whole.astype(jnp.float32)
    scale_row = lax.rsqrt(jnp.sum(whole_wide * whole_wide, axis=-1) / D + 1e-05)
    normed_full = (whole_wide * scale_row[:, None] * gain_full).astype(jnp.bfloat16)
    query_sum = jnp.dot(normed_full, query_cols, preferred_element_type=jnp.float32)
    kv_sum = jnp.dot(normed_full, kv_cols, preferred_element_type=jnp.float32)
    queries = query_sum.astype(jnp.bfloat16)
    kv_local = kv_sum.astype(jnp.bfloat16)
    attended = attend_heads(queries, kv_local, allowed, local_rank)
    return (widened + attended).astype(jnp.bfloat16)


def on_device(hidden, doc_lengths, doc_target, norm_gain, q_weight, kv_weight):
    groups = lax.axis_size("dp")
    current = hidden[0]
    lengths = doc_lengths[0, 0]
    targets = doc_target[0, 0]
    capacity = current.shape[0] // 4
    gain_full = norm_gain[0]
    query_cols = q_weight[0]
    kv_cols = kv_weight[0]
    carried = jnp.stack([lengths, targets]).astype(jnp.bfloat16)
    for layer_step in range(STEPS):
        allowed = doc_masks(carried[0].astype(jnp.int32), current.shape[0])
        current = layer_pass(current, gain_full, query_cols, kv_cols, allowed)
        if layer_step + 1 < STEPS:
            current, carried = passed_along((current, carried), "pipe", 1)
    final_lengths = carried[0].astype(jnp.int32)
    final_targets = carried[1].astype(jnp.int32)
    packed, doc_sizes = build_send(current, final_lengths, final_targets, capacity, groups)
    received = lax.all_to_all(packed, "dp", split_axis=0, concat_axis=0, tiled=True)
    return received.reshape(1, groups * capacity, received.shape[2])


CHUNK = 256
SLOTS = 6
KV_ROWS = 1024
LEAD = 6
PIECES = 4


mark = contextlib.nullcontext


def split_masks(n_dp):
    early = [m for m in range(n_dp) if m >= n_dp // 2 and m % 2 == 0]
    return early, [m for m in range(n_dp) if m not in early]


def fused_kernel(
    sizes, hidden, lengths_in, targets_in, gain_in, wq, wkv, out, meta, lengths, targets, gain,
    x_own, x_other, h_send, next_own, next_other, early_own, early_other, early_send,
    meta_next, meta_early, normed_first, normed_next, spread, kv_acc, kv_cols, squares, scales,
    kv_send, kv_heads, kv_weights, ring, mask, early_mask, valid, early_chooser, late_chooser,
    q_held, begun, packed,
    sem_x, sem_xs, sem_xr, sem_ms, sem_mr, sem_kvw, sem_ring, sem_kvs, sem_kvr,
    sem_hs, sem_hr, sem_fs, sem_fr, sem_as, sem_ar,
    sem_es, sem_er, sem_gs, sem_gr, sem_mes, sem_mer, sem_in,
):
    n_dp, n_pipe, docs = sizes
    rows, width = hidden.shape
    features = gain_in.shape[1]
    n_chunks = width // CHUNK
    n_kv = wkv.shape[1]
    half_blocks = width // KV_ROWS
    own_kv = kv_heads.shape[2]
    chunk_heads = CHUNK // HD
    group_chunks = n_chunks // own_kv
    capacity = packed.shape[1]
    early_masks, late_masks = split_masks(n_dp)
    half = len(early_masks)
    early_rows = half * capacity
    dp = lax.axis_index("dp")
    pipe = lax.axis_index("pipe")
    side = lax.axis_index("tensor")
    other = 1 - side
    following = lax.rem(pipe + 1, n_pipe)
    preceding = lax.rem(pipe + n_pipe - 1, n_pipe)
    total = STEPS * n_chunks + LEAD
    normed_of = (normed_first, normed_next)

    def partner(flips):
        index, bit = dp, 1
        while bit < n_dp:
            if flips & bit:
                index = index + bit - 2 * bit * lax.rem(dp // bit, 2)
            bit *= 2
        return index

    early_partners = [partner(m) for m in early_masks]
    late_partners = [partner(m) for m in late_masks]

    def cols(j):
        return pl.ds(pl.multiple_of(j * CHUNK, CHUNK), CHUNK)

    def kv_rows(which, b):
        return pl.ds(pl.multiple_of((which * half_blocks + b) * KV_ROWS, KV_ROWS), KV_ROWS)

    def kv_copy(order, b):
        here = kv_rows((side, other)[order], b)
        return pltpu.make_async_copy(
            wkv.at[here], kv_weights.at[here], sem_kvw.at[order * half_blocks + b]
        )

    def ring_copy(c):
        slot = lax.rem(c, SLOTS)
        return pltpu.make_async_copy(
            wq.at[:, cols(lax.rem(c, n_chunks))], ring.at[slot], sem_ring.at[slot]
        )

    def x_copy(j):
        return pltpu.make_async_copy(hidden.at[:, cols(j)], x_own.at[j], sem_x.at[j])

    def x_remote():
        return pltpu.make_async_remote_copy(
            x_own, x_other, sem_xs, sem_xr,
            device_id={"tensor": other}, device_id_type=pl.DeviceIdType.MESH,
        )

    def meta_remote():
        return pltpu.make_async_remote_copy(
            meta, meta_next, sem_ms, sem_mr,
            device_id={"pipe": following}, device_id_type=pl.DeviceIdType.MESH,
        )

    def meta_on(k):
        return pltpu.make_async_remote_copy(
            meta_next, meta_early.at[k], sem_mes.at[k], sem_mer.at[k],
            device_id={"dp": early_partners[k]}, device_id_type=pl.DeviceIdType.MESH,
        )

    def early_remote(k, j):
        return pltpu.make_async_remote_copy(
            early_send.at[j, k], early_own.at[j, k * capacity:(k + 1) * capacity],
            sem_es.at[k], sem_er.at[k, j],
            device_id={"dp": early_partners[k]}, device_id_type=pl.DeviceIdType.MESH,
        )

    def early_forward(j):
        return pltpu.make_async_remote_copy(
            early_own.at[j], early_other.at[j], sem_gs, sem_gr.at[j],
            device_id={"tensor": other}, device_id_type=pl.DeviceIdType.MESH,
        )

    parts = ((0, 0, rows), (1, 0, rows), (1, rows, early_rows))

    def kv_remote(part):
        layer, first, count = parts[part]
        here = pl.ds(first, count)
        return pltpu.make_async_remote_copy(
            kv_send.at[layer, :, here], kv_heads.at[layer, side, :, here],
            sem_kvs.at[part], sem_kvr.at[part],
            device_id={"tensor": other}, device_id_type=pl.DeviceIdType.MESH,
        )

    def h_remote(j):
        return pltpu.make_async_remote_copy(
            h_send.at[j], next_own.at[j], sem_hs, sem_hr.at[j],
            device_id={"pipe": following}, device_id_type=pl.DeviceIdType.MESH,
        )

    def forward_remote(j):
        return pltpu.make_async_remote_copy(
            next_own.at[j], next_other.at[j], sem_fs, sem_fr.at[j],
            device_id={"tensor": other}, device_id_type=pl.DeviceIdType.MESH,
        )

    def doc_rows(index):
        return pl.ds(pl.multiple_of(index * capacity, capacity), capacity)

    def doc_remote(k, j):
        return pltpu.make_async_remote_copy(
            packed.at[k, :, cols(j)], out.at[doc_rows(dp), cols(j)],
            sem_as.at[k], sem_ar.at[k],
            device_id={"dp": late_partners[k]}, device_id_type=pl.DeviceIdType.MESH,
        )

    def doc_all(k):
        return pltpu.make_async_remote_copy(
            packed.at[k], out.at[doc_rows(late_partners[k])],
            sem_as.at[k], sem_ar.at[k],
            device_id={"dp": late_partners[k]}, device_id_type=pl.DeviceIdType.MESH,
        )

    small = [
        pltpu.make_async_copy(*pair, sem_in.at[i])
        for i, pair in enumerate(((lengths_in, lengths), (targets_in, targets), (gain_in, gain)))
    ]
    for j in range(n_chunks):
        x_copy(j).start()
    for copy in small:
        copy.start()
    barrier = pltpu.get_barrier_semaphore()
    pl.semaphore_signal(
        barrier, inc=1, device_id={"tensor": other}, device_id_type=pl.DeviceIdType.MESH
    )
    pl.semaphore_signal(
        barrier, inc=1, device_id={"pipe": following}, device_id_type=pl.DeviceIdType.MESH
    )
    greeted = n_dp + 1
    if n_pipe > 2:
        pl.semaphore_signal(
            barrier, inc=1, device_id={"pipe": preceding}, device_id_type=pl.DeviceIdType.MESH
        )
        greeted += 1
    for away in range(1, n_dp):
        pl.semaphore_signal(
            barrier, inc=1, device_id={"dp": lax.rem(dp + away, n_dp)},
            device_id_type=pl.DeviceIdType.MESH,
        )
    for order in range(2):
        for b in range(half_blocks):
            kv_copy(order, b).start()

    cols_wide = spread.shape[0]
    out_col = lax.broadcasted_iota(jnp.int32, (128, n_kv), 1)
    wanted = lax.rem(out_col, HD) * KV_HEADS + out_col // HD

    def fill_spread(i, carry):
        base = pl.multiple_of(i * 128, 128)
        row = lax.broadcasted_iota(jnp.int32, (128, n_kv), 0) + base
        spread[pl.ds(base, 128), :] = (row == wanted).astype(jnp.float32).astype(jnp.bfloat16)
        return carry

    def fill_mask(source):
        row = lax.broadcasted_iota(jnp.int32, (rows, rows), 0)
        col = lax.broadcasted_iota(jnp.int32, (rows, rows), 1)
        row_doc = jnp.zeros((rows, rows), jnp.int32)
        col_doc = jnp.zeros((rows, rows), jnp.int32)
        end = jnp.zeros((1, 1), jnp.int32)
        for d in range(docs):
            end = end + source[0:1, d:d + 1]
            row_doc = row_doc + (row >= end).astype(jnp.int32)
            col_doc = col_doc + (col >= end).astype(jnp.int32)
        allowed = jnp.where((row_doc == col_doc) & (row >= col), 1.0, 0.0)
        for i in range(chunk_heads):
            mask[i * rows:(i + 1) * rows, :] = allowed

    def fill_early_mask():
        row = lax.broadcasted_iota(jnp.int32, (early_rows, early_rows), 0)
        col = lax.broadcasted_iota(jnp.int32, (early_rows, early_rows), 1)
        allowed = jnp.where((row // capacity == col // capacity) & (row >= col), 1.0, 0.0)
        for i in range(chunk_heads):
            early_mask[i * early_rows:(i + 1) * early_rows, :] = allowed

    def fill_valid():
        row = lax.broadcasted_iota(jnp.int32, (capacity, CHUNK), 0)
        for slot in range(half):
            size = jnp.zeros((1, 1), jnp.int32)
            for d in range(docs):
                here = meta_early[slot, 1:2, d:d + 1] == dp
                size = size + jnp.where(here, meta_early[slot, 0:1, d:d + 1], 0)
            valid[slot * capacity:(slot + 1) * capacity, :] = jnp.where(row < size, 1.0, 0.0)

    def fill_choosers(source):
        row = lax.broadcasted_iota(jnp.int32, (1, rows), 1)
        goals = [jnp.full((1, rows), -1, jnp.int32) for _ in range(2)]
        begin = jnp.zeros((1, 1), jnp.int32)
        for d in range(docs):
            end = begin + source[0:1, d:d + 1]
            target = source[1:2, d:d + 1]
            inside = (row >= begin) & (row < end)
            for i, partners in enumerate((early_partners, late_partners)):
                first = jnp.full((1, 1), -n_dp * capacity, jnp.int32)
                for k, index in enumerate(partners):
                    first = jnp.where(target == index, k * capacity, first)
                goals[i] = jnp.where(inside, first + row - begin, goals[i])
            begin = end
        for ref, goal in zip((early_chooser, late_chooser), goals):
            slot = lax.broadcasted_iota(jnp.int32, ref.shape, 0)
            ref[...] = (slot == goal).astype(jnp.float32).astype(jnp.bfloat16)

    def absorb_half(held, which):
        def one(j, acc):
            wide = held[j].astype(jnp.float32)
            where = cols(which * n_chunks + j)
            normed_first[:, where] = (wide * gain[:, where]).astype(jnp.bfloat16)
            return acc + wide * wide

        squares[0:rows] = lax.fori_loop(0, n_chunks, one, squares[0:rows])

    def multiply_half(order):
        which = (side, other)[order]

        def one(b, carry):
            kv_copy(order, b).wait()
            here = kv_rows(which, b)
            kv_acc[0:rows] += jnp.dot(
                normed_first[:, here], kv_weights[here, :], preferred_element_type=jnp.float32
            )
            return carry

        lax.fori_loop(0, half_blocks, one, 0)

    def absorb_next(mine, theirs, first, count, chunks):
        here = slice(first, first + count)
        total = squares[here]
        left, right = [], []
        for j in chunks:
            for held, which in ((mine, side), (theirs, other)):
                where = cols(which * n_chunks + j)
                wide = held[j].astype(jnp.float32)
                total = total + wide * wide
                scaled = (wide * gain[:, where]).astype(jnp.bfloat16)
                normed_next[here, where] = scaled
                left.append(scaled)
                right.append(kv_weights[where, :])
        squares[here] = total
        kv_acc[here] += jnp.dot(
            jnp.concatenate(left, axis=1), jnp.concatenate(right, axis=0),
            preferred_element_type=jnp.float32,
        )

    def clear_sums():
        kv_acc[...] = jnp.zeros(kv_acc.shape, jnp.float32)
        squares[...] = jnp.zeros(squares.shape, jnp.float32)

    def keys_values(part):
        layer, first, count = parts[part]
        here = slice(first, first + count)
        scale = lax.rsqrt(jnp.sum(squares[here], axis=-1, keepdims=True) / features + 1e-05)
        scales[here] = jnp.broadcast_to(scale, (count, CHUNK))
        kv_cols[here] = (kv_acc[here] * scale).astype(jnp.bfloat16)
        heads = kv_spread(part, other)
        for g in range(own_kv):
            kv_send[layer, g, here] = heads[:, g * HD:(g + 1) * HD]
        kv_remote(part).start()

    def kv_spread(part, which):
        _, first, count = parts[part]
        start = pl.multiple_of(which * own_kv * HD, own_kv * HD)
        return jnp.dot(
            kv_cols[first:first + count], spread[:, pl.ds(start, own_kv * HD)],
            preferred_element_type=jnp.float32,
        ).astype(jnp.bfloat16)

    def keep_heads(part):
        layer, first, count = parts[part]
        heads = kv_spread(part, side)
        for g in range(own_kv):
            kv_heads[layer, side, g, first:first + count] = heads[:, g * HD:(g + 1) * HD]

    def query_piece(layer, c, first, count, piece):
        deep = slice(piece * features // PIECES, (piece + 1) * features // PIECES)
        return jnp.dot(
            normed_of[layer][first:first + count, deep], ring[lax.rem(c, SLOTS), deep],
            preferred_element_type=jnp.float32,
        )

    def attend(layer, j, mine, first, count, allowed):
        here = slice(first, first + count)
        q = q_held[lax.rem(j, 2), here]
        g = j // group_chunks
        stacked = jnp.concatenate([q[:, i * HD:(i + 1) * HD] for i in range(chunk_heads)], axis=0)
        scores = lax.dot_general(
            stacked, kv_heads[layer, 0, g, here], (((1,), (1,)), ((), ())),
            preferred_element_type=jnp.float32,
        ) * HD ** (-0.5)
        yield
        e = jnp.where(allowed[...] > 0.0, jnp.exp(scores), 0.0)
        p = (e * (1.0 / jnp.sum(e, axis=-1, keepdims=True))).astype(jnp.bfloat16)
        yield
        a = jnp.dot(p, kv_heads[layer, 1, g, here], preferred_element_type=jnp.float32)
        side_by_side = jnp.concatenate(
            [a[i * count:(i + 1) * count] for i in range(chunk_heads)], axis=1
        )
        yield (mine[j].astype(jnp.float32) + side_by_side).astype(jnp.bfloat16)

    def attend_first(j):
        return attend(0, j, x_own, 0, rows, mask)

    def attend_local(j):
        return attend(1, j, next_own, 0, rows, mask)

    def attend_early(j):
        return attend(1, j, early_own, rows, early_rows, early_mask)

    def refill(c):
        @pl.when(c + SLOTS < total)
        def _():
            ring_copy(c + SLOTS).start()

    def first_query(layer, c):
        ring_copy(c).wait()
        product = query_piece(layer, c, 0, rows, 0)
        for piece in range(1, PIECES):
            product = product + query_piece(layer, c, 0, rows, piece)
        q_held[0, 0:rows] = (product * scales[0:rows]).astype(jnp.bfloat16)
        refill(jnp.int32(c))

    lag, early_lag = 5, 10
    early_deep = (n_chunks - lag + 1) * CHUNK

    def query_part(c, low, high):
        product = None
        for start in (0, width):
            deep = slice(start + low, start + high)
            part = jnp.dot(
                normed_next[0:rows, deep], ring[lax.rem(c, SLOTS), deep],
                preferred_element_type=jnp.float32,
            )
            product = part if product is None else product + part
        return product

    def begin_query(c):
        ring_copy(c).wait()
        begun[...] = query_part(c, 0, early_deep)

    def end_query(c):
        product = begun[...] + query_part(c, early_deep, width)
        q_held[0, 0:rows] = (product * scales[0:rows]).astype(jnp.bfloat16)
        refill(jnp.int32(c))

    def step(layer, c, slot, first, count, before, attends, settles, extras=()):
        ring_copy(c).wait()
        stages = [attended(before) for attended in attends]
        product = None
        for piece in range(PIECES):
            done = [next(stage, None) for stage in stages]
            if piece == 2:
                made = done
            if piece == 3:
                for settle, value in zip(settles, made):
                    settle(before, value)
            for extra in extras[piece:piece + 1]:
                extra()
            part = query_piece(layer, c, first, count, piece)
            product = part if product is None else product + part
        here = slice(first, first + count)
        q_held[slot, here] = (product * scales[here]).astype(jnp.bfloat16)

    def last_step(before, attends, settles):
        stages = [attended(before) for attended in attends]
        for piece in range(3):
            made = [next(stage) for stage in stages]
        for settle, value in zip(settles, made):
            settle(before, value)

    def keep_next(j, done):
        h_send[j] = done

    def pass_on_start(j):
        h_remote(j).wait_recv()
        forward_remote(j).start()

    def pass_on_pick(j):
        picked = jnp.dot(
            early_chooser[...], next_own[j], preferred_element_type=jnp.float32
        ).astype(jnp.bfloat16)
        for slot in range(half):
            early_send[j, slot] = picked[slot * capacity:(slot + 1) * capacity]

    def pass_on_send(j):
        for k in range(half):
            early_remote(k, j).start()

    def pass_on(j):
        pass_on_start(j)
        pass_on_pick(j)
        pass_on_send(j)

    def absorb_local(*chunks):
        absorb_next(next_own, next_other, 0, rows, chunks)

    def absorb_early(*chunks):
        absorb_next(early_own, early_other, rows, early_rows, chunks)

    def pass_early(j):
        for k in range(half):
            early_remote(k, j).wait_recv()
        early_forward(j).start()

    def pick_docs(j, done):
        picked = jnp.dot(late_chooser[...], done, preferred_element_type=jnp.float32)
        picked = picked.astype(jnp.bfloat16)
        out[doc_rows(dp), cols(j)] = picked[0:capacity]
        for slot in range(1, len(late_masks)):
            packed[slot, :, cols(j)] = picked[slot * capacity:(slot + 1) * capacity]

    def send_docs(j):
        for k in reversed(range(1, len(late_masks))):
            doc_remote(k, j).start()

    def keep_early(j, early):
        kept = jnp.where(valid[...] > 0.0, early.astype(jnp.float32), 0.0).astype(jnp.bfloat16)
        for slot in range(half):
            out[doc_rows(early_partners[slot]), cols(j)] = kept[slot * capacity:(slot + 1) * capacity]

    def first_span(low, high, stage):
        def one(j, carry):
            on, local, gone, early = j - lag, j - lag - 1, j - early_lag, j - early_lag - 1
            extras = [[], [], [], []]
            if stage >= 1:
                pass_on_start(on)
                forward_remote(local).wait_recv()
                extras[0].append(functools.partial(absorb_local, local))
                extras[1].append(functools.partial(pass_on_pick, on))
            if stage >= 2:
                pass_early(gone)
                early_forward(early).wait_recv()
                extras[2].append(functools.partial(absorb_early, early))
            step(
                0, j, lax.rem(j, 2), 0, rows, j - 1, (attend_first,), (keep_next,),
                [functools.partial(run_all, group) for group in extras],
            )
            h_remote(j - 1).start()
            if stage >= 1:
                pass_on_send(on)
            refill(j)
            return carry

        lax.fori_loop(low, high, one, 0)

    def run_all(group):
        for task in group:
            task()

    lax.fori_loop(0, cols_wide // 128, fill_spread, 0)
    fill_early_mask()
    clear_sums()
    for copy in small:
        copy.wait()
    meta[...] = jnp.zeros(meta.shape, jnp.int32)
    meta[0:1, 0:docs] = lengths[...]
    meta[1:2, 0:docs] = targets[...]
    fill_mask(meta)
    with mark("PX_barrier"):
        pl.semaphore_wait(barrier, greeted)
    with mark("P1_xsend"):
        for j in range(n_chunks):
            x_copy(j).wait()
        x_remote().start()
    meta_remote().start()
    for c in range(SLOTS):
        ring_copy(c).start()
    with mark("P2_own"):
        absorb_half(x_own, side)
        multiply_half(0)
    with mark("P3_xwait"):
        x_remote().wait()
    with mark("P4_other"):
        absorb_half(x_other, other)
        multiply_half(1)
    with mark("P5_kv"):
        keys_values(0)
    with mark("P6_first"):
        first_query(0, 0)
        keep_heads(0)
        kv_remote(0).wait()
    with mark("P7_span0"):
        first_span(1, lag + 1, 0)
    with mark("P8_meta"):
        meta_remote().wait()
        for k in range(half):
            meta_on(k).start()
        fill_choosers(meta_next)
        clear_sums()
        pass_on(0)
    with mark("P9_span1"):
        first_span(lag + 1, early_lag + 1, 1)
    with mark("PA_early0"):
        pass_early(0)
    with mark("PB_span2"):
        first_span(early_lag + 1, n_chunks, 2)
    with mark("PC_rest"):
        last_step(n_chunks - 1, (attend_first,), (keep_next,))
        h_remote(n_chunks - 1).start()
        fill_mask(meta_next)
        for k in range(half):
            meta_on(k).wait()
        fill_valid()
        gone = n_chunks - early_lag
        for j in range(n_chunks - lag, n_chunks):
            pass_on_start(j)
            pass_on_pick(j)
            pass_on_send(j)
            forward_remote(j - 1).wait_recv()
            absorb_local(j - 1)
            if j == n_chunks - lag + 1:
                begin_query(n_chunks)
            for _ in range(2):
                if gone < j - 4:
                    pass_early(gone)
                    early_forward(gone - 1).wait_recv()
                    absorb_early(gone - 1)
                    gone += 1
    with mark("PD_last"):
        forward_remote(n_chunks - 1).wait_recv()
        absorb_local(n_chunks - 1)
    with mark("PE_kv"):
        keys_values(1)
    with mark("PF_first"):
        end_query(n_chunks)
        keep_heads(1)
        kv_remote(1).wait()
    with mark("PG_local"):
        def local(j, carry):
            step(
                1, n_chunks + j, lax.rem(j, 2), 0, rows, j - 1, (attend_local,), (pick_docs,)
            )
            send_docs(j - 1)
            refill(n_chunks + j)
            return carry

        lax.fori_loop(1, LEAD - 1, local, 0)
        for i in range(gone, n_chunks):
            pass_early(i)
        lax.fori_loop(LEAD - 1, LEAD, local, 0)
        for i in range(gone - 1, n_chunks):
            early_forward(i).wait_recv()
        absorb_early(*range(gone - 1, n_chunks))
        keys_values(2)
        step(
            1, n_chunks + LEAD, LEAD % 2, 0, rows + early_rows, LEAD - 1, (attend_local,), (pick_docs,)
        )
        send_docs(LEAD - 1)
        refill(jnp.int32(n_chunks + LEAD))
        keep_heads(2)
        kv_remote(2).wait()
    with mark("PH_both"):
        def both(j, carry):
            step(
                1, n_chunks + j, lax.rem(j, 2), 0, rows + early_rows, j - 1,
                (attend_local, attend_early), (pick_docs, keep_early),
            )
            send_docs(j - 1)
            refill(n_chunks + j)
            return carry

        lax.fori_loop(LEAD + 1, n_chunks, both, 0)
    with mark("PI_turn"):
        step(
            1, total - LEAD, 0, rows, early_rows, n_chunks - 1,
            (attend_local, attend_early), (pick_docs, keep_early),
        )
        send_docs(n_chunks - 1)
    with mark("PJ_early"):
        def behind(j, carry):
            step(
                1, total - LEAD + j, lax.rem(j, 2), rows, early_rows, j - 1,
                (attend_early,), (keep_early,),
            )
            return carry

        lax.fori_loop(1, LEAD, behind, 0)
        last_step(LEAD - 1, (attend_early,), (keep_early,))
    with mark("PK_sends"):
        for held, there, sent, got in (
            (h_send, next_own, sem_hs, sem_hr.at[0]),
            (next_own, next_other, sem_fs, sem_fr.at[0]),
            (early_own, early_other, sem_gs, sem_gr.at[0]),
        ):
            whom = {"pipe": following} if held is h_send else {"tensor": other}
            pltpu.make_async_remote_copy(
                held, there, sent, got, device_id=whom, device_id_type=pl.DeviceIdType.MESH
            ).wait_send()
        for k in range(half):
            pltpu.make_async_remote_copy(
                early_send.at[:, k], early_own.at[:, k * capacity:(k + 1) * capacity],
                sem_es.at[k], sem_er.at[k, 0],
                device_id={"dp": early_partners[k]}, device_id_type=pl.DeviceIdType.MESH,
            ).wait_send()
    with mark("PL_docs"):
        for k in range(1, len(late_masks)):
            doc_all(k).wait()


def put_out(held, out, sem):
    copy = pltpu.make_async_copy(held, out, sem)
    copy.start()
    copy.wait()


def fused_device(sizes, hidden, doc_lengths, doc_target, norm_gain, q_weight, kv_weight):
    n_dp, n_pipe, docs = sizes
    rows, width = hidden.shape[1:]
    features = norm_gain.shape[1]
    n_chunks = width // CHUNK
    n_kv = kv_weight.shape[2]
    own_kv = KV_HEADS // 2
    capacity = rows // 4
    chunk_heads = CHUNK // HD
    bf16 = jnp.bfloat16
    dma = pltpu.SemaphoreType.DMA
    vmem = pltpu.VMEM
    early_masks, late_masks = split_masks(n_dp)
    half, n_late = len(early_masks), len(late_masks)
    early_rows = half * capacity
    most = rows + early_rows
    blocks = vmem((n_chunks, rows, CHUNK), bf16)
    early_blocks = vmem((n_chunks, early_rows, CHUNK), bf16)
    result = pl.pallas_call(
        functools.partial(fused_kernel, sizes),
        out_shape=vmem((n_dp * capacity, width), bf16),
        in_specs=[
            pl.BlockSpec(memory_space=pl.ANY),
            pl.BlockSpec(memory_space=pl.ANY),
            pl.BlockSpec(memory_space=pl.ANY),
            pl.BlockSpec(memory_space=pl.ANY),
            pl.BlockSpec(memory_space=pl.ANY),
            pl.BlockSpec(memory_space=pl.ANY),
        ],
        out_specs=pl.BlockSpec(memory_space=vmem),
        scratch_shapes=[
            vmem((8, 128), jnp.int32),
            vmem((1, docs), jnp.int32), vmem((1, docs), jnp.int32), vmem((1, features), jnp.float32),
            blocks, blocks, blocks, blocks, blocks, early_blocks, early_blocks,
            vmem((n_chunks, half, capacity, CHUNK), bf16),
            vmem((8, 128), jnp.int32),
            vmem((half, 8, 128), jnp.int32),
            vmem((rows, features), bf16),
            vmem((most, features), bf16),
            vmem((n_kv, n_kv), bf16),
            vmem((most, n_kv), jnp.float32),
            vmem((most, n_kv), bf16),
            vmem((most, CHUNK), jnp.float32),
            vmem((most, CHUNK), jnp.float32),
            vmem((STEPS, own_kv, most, HD), bf16),
            vmem((STEPS, 2, own_kv, most, HD), bf16),
            vmem((features, n_kv), bf16),
            vmem((SLOTS, features, CHUNK), bf16),
            vmem((chunk_heads * rows, rows), jnp.float32),
            vmem((chunk_heads * early_rows, early_rows), jnp.float32),
            vmem((early_rows, CHUNK), jnp.float32),
            vmem((early_rows, rows), bf16),
            vmem((n_late * capacity, rows), bf16),
            vmem((2, most, CHUNK), bf16),
            vmem((rows, CHUNK), jnp.float32),
            vmem((n_late, capacity, width), bf16),
            dma((n_chunks,)), dma, dma, dma, dma,
            dma((features // KV_ROWS,)), dma((SLOTS,)), dma((STEPS + 1,)), dma((STEPS + 1,)),
            dma, dma((n_chunks,)), dma, dma((n_chunks,)),
            dma((n_late,)), dma((n_late,)),
            dma((half,)), dma((half, n_chunks)), dma, dma((n_chunks,)),
            dma((half,)), dma((half,)), dma((3,)),
        ],
        compiler_params=pltpu.CompilerParams(
            collective_id=0, has_side_effects=True, vmem_limit_bytes=64800000
        ),
    )(hidden[0], doc_lengths[0], doc_target[0], norm_gain, q_weight[0], kv_weight[0])
    return pl.pallas_call(
        put_out,
        out_shape=jax.ShapeDtypeStruct((n_dp * capacity, width), bf16),
        in_specs=[pl.BlockSpec(memory_space=vmem)],
        out_specs=pl.BlockSpec(memory_space=pl.ANY),
        scratch_shapes=[dma],
        compiler_params=pltpu.CompilerParams(vmem_limit_bytes=4194304),
    )(result)[None]


def solution(mesh):
    placed = (
        P("pipe", "dp", "tensor"),
        P("pipe", "dp", None),
        P("pipe", "dp", None),
        P("pipe", None),
        P("pipe", None, "tensor"),
        P("pipe", None, "tensor"),
    )
    run = on_device
    if mesh.shape["tensor"] == 2 and mesh.shape["dp"] in (4, 8, 16):
        sizes = (mesh.shape["dp"], mesh.shape["pipe"], mesh.shape["dp"])
        run = functools.partial(fused_device, sizes)
    return jax.shard_map(
        run, mesh=mesh, in_specs=placed, out_specs=P("pipe", "dp", "tensor"), check_vma=False
    )
```

```python
import contextlib
import functools

import jax
import jax.numpy as jnp
from jax import lax
from jax.experimental import pallas as pl
from jax.experimental.pallas import tpu as pltpu
from jax.sharding import PartitionSpec as P

D = 8192
HD = 128
KV_HEADS = 8
STEPS = 2


def passed_along(block, axis, distance):
    devices = range(lax.axis_size(axis))
    route = [((i - distance) % len(devices), i) for i in devices]
    return lax.ppermute(block, axis, route)


def build_send(token_rows, lengths, targets, capacity, groups):
    ordinal = jnp.arange(groups, dtype=jnp.int32)
    offsets = jnp.cumsum(lengths) - lengths
    onehot = (targets[None, :] == ordinal[:, None]).astype(jnp.int32)
    doc_sizes = jnp.sum(onehot * lengths[None, :], axis=1)
    doc_starts = jnp.sum(onehot * offsets[None, :], axis=1)
    within = jnp.arange(capacity, dtype=jnp.int32)
    row_index = jnp.minimum(doc_starts[:, None] + within[None, :], token_rows.shape[0] - 1)
    picked = jnp.take(token_rows, row_index.reshape(-1), axis=0).reshape(
        groups, capacity, token_rows.shape[1]
    )
    inside = within[None, :] < doc_sizes[:, None]
    return (jnp.where(inside[:, :, None], picked, jnp.zeros_like(picked)), doc_sizes)


def doc_masks(lengths, length):
    within = jnp.arange(length, dtype=jnp.int32)
    doc_ends = jnp.cumsum(lengths)
    segment = jnp.sum((within[:, None] >= doc_ends[None, :]).astype(jnp.int32), axis=1)
    causal = within[:, None] >= within[None, :]
    return (segment[:, None] == segment[None, :]) & causal


def attend_heads(queries, kv_local, allowed, local_rank):
    row_count = queries.shape[0]
    local_heads = queries.shape[1] // HD
    per_group = D // HD // KV_HEADS
    kv_count = max(1, local_heads // per_group)
    kv_first = local_rank * local_heads // per_group
    kv_whole = lax.all_gather(kv_local, "tensor", axis=1, tiled=True)
    kv_heads = kv_whole.reshape(row_count, 2, HD, KV_HEADS)
    own_heads = lax.dynamic_slice_in_dim(kv_heads, kv_first, kv_count, 3)
    key_rows = own_heads[:, 0]
    values = own_heads[:, 1]
    grouped = queries.reshape(row_count, kv_count, local_heads // kv_count, HD)
    scores = jnp.einsum(
        "qcph,khc->cpqk", grouped, key_rows, preferred_element_type=jnp.float32
    ) * HD ** (-0.5)
    exp_scores = jnp.where(allowed[None, None], jnp.exp(scores), 0.0)
    probabilities = (exp_scores / jnp.sum(exp_scores, axis=-1, keepdims=True)).astype(jnp.bfloat16)
    attended = jnp.einsum(
        "cpqk,khc->qcph", probabilities, values, preferred_element_type=jnp.float32
    )
    return attended.reshape(row_count, queries.shape[1])


def layer_pass(current, gain_full, query_cols, kv_cols, allowed):
    local_rank = lax.axis_index("tensor")
    widened = current.astype(jnp.float32)
    whole = lax.all_gather(current, "tensor", axis=1, tiled=True)
    whole_wide = whole.astype(jnp.float32)
    scale_row = lax.rsqrt(jnp.sum(whole_wide * whole_wide, axis=-1) / D + 1e-05)
    normed_full = (whole_wide * scale_row[:, None] * gain_full).astype(jnp.bfloat16)
    query_sum = jnp.dot(normed_full, query_cols, preferred_element_type=jnp.float32)
    kv_sum = jnp.dot(normed_full, kv_cols, preferred_element_type=jnp.float32)
    queries = query_sum.astype(jnp.bfloat16)
    kv_local = kv_sum.astype(jnp.bfloat16)
    attended = attend_heads(queries, kv_local, allowed, local_rank)
    return (widened + attended).astype(jnp.bfloat16)


def on_device(hidden, doc_lengths, doc_target, norm_gain, q_weight, kv_weight):
    groups = lax.axis_size("dp")
    current = hidden[0]
    lengths = doc_lengths[0, 0]
    targets = doc_target[0, 0]
    capacity = current.shape[0] // 4
    gain_full = norm_gain[0]
    query_cols = q_weight[0]
    kv_cols = kv_weight[0]
    carried = jnp.stack([lengths, targets]).astype(jnp.bfloat16)
    for layer_step in range(STEPS):
        allowed = doc_masks(carried[0].astype(jnp.int32), current.shape[0])
        current = layer_pass(current, gain_full, query_cols, kv_cols, allowed)
        if layer_step + 1 < STEPS:
            current, carried = passed_along((current, carried), "pipe", 1)
    final_lengths = carried[0].astype(jnp.int32)
    final_targets = carried[1].astype(jnp.int32)
    packed, doc_sizes = build_send(current, final_lengths, final_targets, capacity, groups)
    received = lax.all_to_all(packed, "dp", split_axis=0, concat_axis=0, tiled=True)
    return received.reshape(1, groups * capacity, received.shape[2])


CHUNK = 256
SLOTS = 6
KV_ROWS = 1024
LEAD = 6
PIECES = 4


mark = contextlib.nullcontext


def split_masks(n_dp):
    early = [m for m in range(n_dp) if m >= n_dp // 2 and m % 2 == 0]
    return early, [m for m in range(n_dp) if m not in early]


def fused_kernel(
    sizes, hidden, lengths_in, targets_in, gain_in, wq, wkv, out, meta, lengths, targets, gain,
    x_own, x_other, h_send, next_own, next_other, early_own, early_other, early_send,
    meta_next, meta_early, normed_first, normed_next, spread, kv_acc, kv_cols, squares, scales,
    kv_send, kv_heads, kv_weights, ring, mask, early_mask, valid, early_chooser, late_chooser,
    q_held, begun, packed,
    sem_x, sem_xs, sem_xr, sem_ms, sem_mr, sem_kvw, sem_ring, sem_kvs, sem_kvr,
    sem_hs, sem_hr, sem_fs, sem_fr, sem_as, sem_ar,
    sem_es, sem_er, sem_gs, sem_gr, sem_mes, sem_mer, sem_in,
):
    n_dp, n_pipe, docs = sizes
    rows, width = hidden.shape
    features = gain_in.shape[1]
    n_chunks = width // CHUNK
    n_kv = wkv.shape[1]
    half_blocks = width // KV_ROWS
    own_kv = kv_heads.shape[2]
    chunk_heads = CHUNK // HD
    group_chunks = n_chunks // own_kv
    capacity = packed.shape[1]
    early_masks, late_masks = split_masks(n_dp)
    half = len(early_masks)
    early_rows = half * capacity
    dp = lax.axis_index("dp")
    pipe = lax.axis_index("pipe")
    side = lax.axis_index("tensor")
    other = 1 - side
    following = lax.rem(pipe + 1, n_pipe)
    preceding = lax.rem(pipe + n_pipe - 1, n_pipe)
    total = STEPS * n_chunks + LEAD
    normed_of = (normed_first, normed_next)

    def partner(flips):
        index, bit = dp, 1
        while bit < n_dp:
            if flips & bit:
                index = index + bit - 2 * bit * lax.rem(dp // bit, 2)
            bit *= 2
        return index

    early_partners = [partner(m) for m in early_masks]
    late_partners = [partner(m) for m in late_masks]

    def cols(j):
        return pl.ds(pl.multiple_of(j * CHUNK, CHUNK), CHUNK)

    def kv_rows(which, b):
        return pl.ds(pl.multiple_of((which * half_blocks + b) * KV_ROWS, KV_ROWS), KV_ROWS)

    def kv_copy(order, b):
        here = kv_rows((side, other)[order], b)
        return pltpu.make_async_copy(
            wkv.at[here], kv_weights.at[here], sem_kvw.at[order * half_blocks + b]
        )

    def ring_copy(c):
        slot = lax.rem(c, SLOTS)
        return pltpu.make_async_copy(
            wq.at[:, cols(lax.rem(c, n_chunks))], ring.at[slot], sem_ring.at[slot]
        )

    def x_copy(j):
        return pltpu.make_async_copy(hidden.at[:, cols(j)], x_own.at[j], sem_x.at[j])

    def x_remote():
        return pltpu.make_async_remote_copy(
            x_own, x_other, sem_xs, sem_xr,
            device_id={"tensor": other}, device_id_type=pl.DeviceIdType.MESH,
        )

    def meta_remote():
        return pltpu.make_async_remote_copy(
            meta, meta_next, sem_ms, sem_mr,
            device_id={"pipe": following}, device_id_type=pl.DeviceIdType.MESH,
        )

    def meta_on(k):
        return pltpu.make_async_remote_copy(
            meta_next, meta_early.at[k], sem_mes.at[k], sem_mer.at[k],
            device_id={"dp": early_partners[k]}, device_id_type=pl.DeviceIdType.MESH,
        )

    def early_remote(k, j):
        return pltpu.make_async_remote_copy(
            early_send.at[j, k], early_own.at[j, k * capacity:(k + 1) * capacity],
            sem_es.at[k], sem_er.at[k, j],
            device_id={"dp": early_partners[k]}, device_id_type=pl.DeviceIdType.MESH,
        )

    def early_forward(j):
        return pltpu.make_async_remote_copy(
            early_own.at[j], early_other.at[j], sem_gs, sem_gr.at[j],
            device_id={"tensor": other}, device_id_type=pl.DeviceIdType.MESH,
        )

    parts = ((0, 0, rows), (1, 0, rows), (1, rows, early_rows))

    def kv_remote(part):
        layer, first, count = parts[part]
        here = pl.ds(first, count)
        return pltpu.make_async_remote_copy(
            kv_send.at[layer, :, here], kv_heads.at[layer, side, :, here],
            sem_kvs.at[part], sem_kvr.at[part],
            device_id={"tensor": other}, device_id_type=pl.DeviceIdType.MESH,
        )

    def h_remote(j):
        return pltpu.make_async_remote_copy(
            h_send.at[j], next_own.at[j], sem_hs, sem_hr.at[j],
            device_id={"pipe": following}, device_id_type=pl.DeviceIdType.MESH,
        )

    def forward_remote(j):
        return pltpu.make_async_remote_copy(
            next_own.at[j], next_other.at[j], sem_fs, sem_fr.at[j],
            device_id={"tensor": other}, device_id_type=pl.DeviceIdType.MESH,
        )

    def doc_rows(index):
        return pl.ds(pl.multiple_of(index * capacity, capacity), capacity)

    def doc_remote(k, j):
        return pltpu.make_async_remote_copy(
            packed.at[k, :, cols(j)], out.at[doc_rows(dp), cols(j)],
            sem_as.at[k], sem_ar.at[k],
            device_id={"dp": late_partners[k]}, device_id_type=pl.DeviceIdType.MESH,
        )

    def doc_all(k):
        return pltpu.make_async_remote_copy(
            packed.at[k], out.at[doc_rows(late_partners[k])],
            sem_as.at[k], sem_ar.at[k],
            device_id={"dp": late_partners[k]}, device_id_type=pl.DeviceIdType.MESH,
        )

    small = [
        pltpu.make_async_copy(*pair, sem_in.at[i])
        for i, pair in enumerate(((lengths_in, lengths), (targets_in, targets), (gain_in, gain)))
    ]
    for j in range(n_chunks):
        x_copy(j).start()
    for copy in small:
        copy.start()
    barrier = pltpu.get_barrier_semaphore()
    pl.semaphore_signal(
        barrier, inc=1, device_id={"tensor": other}, device_id_type=pl.DeviceIdType.MESH
    )
    pl.semaphore_signal(
        barrier, inc=1, device_id={"pipe": following}, device_id_type=pl.DeviceIdType.MESH
    )
    greeted = n_dp + 1
    if n_pipe > 2:
        pl.semaphore_signal(
            barrier, inc=1, device_id={"pipe": preceding}, device_id_type=pl.DeviceIdType.MESH
        )
        greeted += 1
    for away in range(1, n_dp):
        pl.semaphore_signal(
            barrier, inc=1, device_id={"dp": lax.rem(dp + away, n_dp)},
            device_id_type=pl.DeviceIdType.MESH,
        )
    for order in range(2):
        for b in range(half_blocks):
            kv_copy(order, b).start()

    cols_wide = spread.shape[0]
    out_col = lax.broadcasted_iota(jnp.int32, (128, n_kv), 1)
    wanted = lax.rem(out_col, HD) * KV_HEADS + out_col // HD

    def fill_spread(i, carry):
        base = pl.multiple_of(i * 128, 128)
        row = lax.broadcasted_iota(jnp.int32, (128, n_kv), 0) + base
        spread[pl.ds(base, 128), :] = (row == wanted).astype(jnp.float32).astype(jnp.bfloat16)
        return carry

    def fill_mask(source):
        row = lax.broadcasted_iota(jnp.int32, (rows, rows), 0)
        col = lax.broadcasted_iota(jnp.int32, (rows, rows), 1)
        row_doc = jnp.zeros((rows, rows), jnp.int32)
        col_doc = jnp.zeros((rows, rows), jnp.int32)
        end = jnp.zeros((1, 1), jnp.int32)
        for d in range(docs):
            end = end + source[0:1, d:d + 1]
            row_doc = row_doc + (row >= end).astype(jnp.int32)
            col_doc = col_doc + (col >= end).astype(jnp.int32)
        allowed = jnp.where((row_doc == col_doc) & (row >= col), 1.0, 0.0)
        for i in range(chunk_heads):
            mask[i * rows:(i + 1) * rows, :] = allowed

    def fill_early_mask():
        row = lax.broadcasted_iota(jnp.int32, (early_rows, early_rows), 0)
        col = lax.broadcasted_iota(jnp.int32, (early_rows, early_rows), 1)
        allowed = jnp.where((row // capacity == col // capacity) & (row >= col), 1.0, 0.0)
        for i in range(chunk_heads):
            early_mask[i * early_rows:(i + 1) * early_rows, :] = allowed

    def fill_valid():
        row = lax.broadcasted_iota(jnp.int32, (capacity, CHUNK), 0)
        for slot in range(half):
            size = jnp.zeros((1, 1), jnp.int32)
            for d in range(docs):
                here = meta_early[slot, 1:2, d:d + 1] == dp
                size = size + jnp.where(here, meta_early[slot, 0:1, d:d + 1], 0)
            valid[slot * capacity:(slot + 1) * capacity, :] = jnp.where(row < size, 1.0, 0.0)

    def fill_choosers(source):
        row = lax.broadcasted_iota(jnp.int32, (1, rows), 1)
        goals = [jnp.full((1, rows), -1, jnp.int32) for _ in range(2)]
        begin = jnp.zeros((1, 1), jnp.int32)
        for d in range(docs):
            end = begin + source[0:1, d:d + 1]
            target = source[1:2, d:d + 1]
            inside = (row >= begin) & (row < end)
            for i, partners in enumerate((early_partners, late_partners)):
                first = jnp.full((1, 1), -n_dp * capacity, jnp.int32)
                for k, index in enumerate(partners):
                    first = jnp.where(target == index, k * capacity, first)
                goals[i] = jnp.where(inside, first + row - begin, goals[i])
            begin = end
        for ref, goal in zip((early_chooser, late_chooser), goals):
            slot = lax.broadcasted_iota(jnp.int32, ref.shape, 0)
            ref[...] = (slot == goal).astype(jnp.float32).astype(jnp.bfloat16)

    def absorb_half(held, which):
        def one(j, acc):
            wide = held[j].astype(jnp.float32)
            where = cols(which * n_chunks + j)
            normed_first[:, where] = (wide * gain[:, where]).astype(jnp.bfloat16)
            return acc + wide * wide

        squares[0:rows] = lax.fori_loop(0, n_chunks, one, squares[0:rows])

    def multiply_half(order):
        which = (side, other)[order]

        def one(b, carry):
            kv_copy(order, b).wait()
            here = kv_rows(which, b)
            kv_acc[0:rows] += jnp.dot(
                normed_first[:, here], kv_weights[here, :], preferred_element_type=jnp.float32
            )
            return carry

        lax.fori_loop(0, half_blocks, one, 0)

    def absorb_next(mine, theirs, first, count, chunks):
        here = slice(first, first + count)
        total = squares[here]
        left, right = [], []
        for j in chunks:
            for held, which in ((mine, side), (theirs, other)):
                where = cols(which * n_chunks + j)
                wide = held[j].astype(jnp.float32)
                total = total + wide * wide
                scaled = (wide * gain[:, where]).astype(jnp.bfloat16)
                normed_next[here, where] = scaled
                left.append(scaled)
                right.append(kv_weights[where, :])
        squares[here] = total
        kv_acc[here] += jnp.dot(
            jnp.concatenate(left, axis=1), jnp.concatenate(right, axis=0),
            preferred_element_type=jnp.float32,
        )

    def clear_sums():
        kv_acc[...] = jnp.zeros(kv_acc.shape, jnp.float32)
        squares[...] = jnp.zeros(squares.shape, jnp.float32)

    def keys_values(part):
        layer, first, count = parts[part]
        here = slice(first, first + count)
        scale = lax.rsqrt(jnp.sum(squares[here], axis=-1, keepdims=True) / features + 1e-05)
        scales[here] = jnp.broadcast_to(scale, (count, CHUNK))
        kv_cols[here] = (kv_acc[here] * scale).astype(jnp.bfloat16)
        heads = kv_spread(part, other)
        for g in range(own_kv):
            kv_send[layer, g, here] = heads[:, g * HD:(g + 1) * HD]
        kv_remote(part).start()

    def kv_spread(part, which):
        _, first, count = parts[part]
        start = pl.multiple_of(which * own_kv * HD, own_kv * HD)
        return jnp.dot(
            kv_cols[first:first + count], spread[:, pl.ds(start, own_kv * HD)],
            preferred_element_type=jnp.float32,
        ).astype(jnp.bfloat16)

    def keep_heads(part):
        layer, first, count = parts[part]
        heads = kv_spread(part, side)
        for g in range(own_kv):
            kv_heads[layer, side, g, first:first + count] = heads[:, g * HD:(g + 1) * HD]

    def query_piece(layer, c, first, count, piece):
        deep = slice(piece * features // PIECES, (piece + 1) * features // PIECES)
        return jnp.dot(
            normed_of[layer][first:first + count, deep], ring[lax.rem(c, SLOTS), deep],
            preferred_element_type=jnp.float32,
        )

    def attend(layer, j, mine, first, count, allowed):
        here = slice(first, first + count)
        q = q_held[lax.rem(j, 2), here]
        g = j // group_chunks
        stacked = jnp.concatenate([q[:, i * HD:(i + 1) * HD] for i in range(chunk_heads)], axis=0)
        scores = lax.dot_general(
            stacked, kv_heads[layer, 0, g, here], (((1,), (1,)), ((), ())),
            preferred_element_type=jnp.float32,
        ) * HD ** (-0.5)
        yield
        e = jnp.where(allowed[...] > 0.0, jnp.exp(scores), 0.0)
        p = (e * (1.0 / jnp.sum(e, axis=-1, keepdims=True))).astype(jnp.bfloat16)
        yield
        a = jnp.dot(p, kv_heads[layer, 1, g, here], preferred_element_type=jnp.float32)
        side_by_side = jnp.concatenate(
            [a[i * count:(i + 1) * count] for i in range(chunk_heads)], axis=1
        )
        yield (mine[j].astype(jnp.float32) + side_by_side).astype(jnp.bfloat16)

    def attend_first(j):
        return attend(0, j, x_own, 0, rows, mask)

    def attend_local(j):
        return attend(1, j, next_own, 0, rows, mask)

    def attend_early(j):
        return attend(1, j, early_own, rows, early_rows, early_mask)

    def refill(c):
        @pl.when(c + SLOTS < total)
        def _():
            ring_copy(c + SLOTS).start()

    def first_query(layer, c):
        ring_copy(c).wait()
        product = query_piece(layer, c, 0, rows, 0)
        for piece in range(1, PIECES):
            product = product + query_piece(layer, c, 0, rows, piece)
        q_held[0, 0:rows] = (product * scales[0:rows]).astype(jnp.bfloat16)
        refill(jnp.int32(c))

    lag, early_lag = 5, 10
    early_deep = (n_chunks - lag + 1) * CHUNK

    def query_part(c, low, high):
        product = None
        for start in (0, width):
            deep = slice(start + low, start + high)
            part = jnp.dot(
                normed_next[0:rows, deep], ring[lax.rem(c, SLOTS), deep],
                preferred_element_type=jnp.float32,
            )
            product = part if product is None else product + part
        return product

    def begin_query(j):
        ring_copy(n_chunks + j).wait()
        begun[j] = query_part(n_chunks + j, 0, early_deep)

    def end_query(j):
        product = begun[j] + query_part(n_chunks + j, early_deep, width)
        q_held[j, 0:rows] = (product * scales[0:rows]).astype(jnp.bfloat16)
        refill(jnp.int32(n_chunks + j))

    def step(layer, c, slot, first, count, before, attends, settles, extras=()):
        ring_copy(c).wait()
        stages = [attended(before) for attended in attends]
        product = None
        for piece in range(PIECES):
            done = [next(stage, None) for stage in stages]
            if piece == 2:
                made = done
            if piece == 3:
                for settle, value in zip(settles, made):
                    settle(before, value)
            for extra in extras[piece:piece + 1]:
                extra()
            part = query_piece(layer, c, first, count, piece)
            product = part if product is None else product + part
        here = slice(first, first + count)
        q_held[slot, here] = (product * scales[here]).astype(jnp.bfloat16)

    def last_step(before, attends, settles):
        stages = [attended(before) for attended in attends]
        for piece in range(3):
            made = [next(stage) for stage in stages]
        for settle, value in zip(settles, made):
            settle(before, value)

    def keep_next(j, done):
        h_send[j] = done

    def pass_on_start(j):
        h_remote(j).wait_recv()
        forward_remote(j).start()

    def pass_on_pick(j):
        picked = jnp.dot(
            early_chooser[...], next_own[j], preferred_element_type=jnp.float32
        ).astype(jnp.bfloat16)
        for slot in range(half):
            early_send[j, slot] = picked[slot * capacity:(slot + 1) * capacity]

    def pass_on_send(j):
        for k in range(half):
            early_remote(k, j).start()

    def pass_on(j):
        pass_on_start(j)
        pass_on_pick(j)
        pass_on_send(j)

    def absorb_local(*chunks):
        absorb_next(next_own, next_other, 0, rows, chunks)

    def absorb_early(*chunks):
        absorb_next(early_own, early_other, rows, early_rows, chunks)

    def pass_early(j):
        for k in range(half):
            early_remote(k, j).wait_recv()
        early_forward(j).start()

    def pick_docs(j, done):
        picked = jnp.dot(late_chooser[...], done, preferred_element_type=jnp.float32)
        picked = picked.astype(jnp.bfloat16)
        out[doc_rows(dp), cols(j)] = picked[0:capacity]
        for slot in range(1, len(late_masks)):
            packed[slot, :, cols(j)] = picked[slot * capacity:(slot + 1) * capacity]

    def send_docs(j):
        for k in reversed(range(1, len(late_masks))):
            doc_remote(k, j).start()

    def keep_early(j, early):
        kept = jnp.where(valid[...] > 0.0, early.astype(jnp.float32), 0.0).astype(jnp.bfloat16)
        for slot in range(half):
            out[doc_rows(early_partners[slot]), cols(j)] = kept[slot * capacity:(slot + 1) * capacity]

    def first_span(low, high, stage):
        def one(j, carry):
            on, local, gone, early = j - lag, j - lag - 1, j - early_lag, j - early_lag - 1
            extras = [[], [], [], []]
            if stage >= 1:
                pass_on_start(on)
                forward_remote(local).wait_recv()
                extras[0].append(functools.partial(absorb_local, local))
                extras[1].append(functools.partial(pass_on_pick, on))
            if stage >= 2:
                pass_early(gone)
                early_forward(early).wait_recv()
                extras[2].append(functools.partial(absorb_early, early))
            step(
                0, j, lax.rem(j, 2), 0, rows, j - 1, (attend_first,), (keep_next,),
                [functools.partial(run_all, group) for group in extras],
            )
            h_remote(j - 1).start()
            if stage >= 1:
                pass_on_send(on)
            refill(j)
            return carry

        lax.fori_loop(low, high, one, 0)

    def run_all(group):
        for task in group:
            task()

    lax.fori_loop(0, cols_wide // 128, fill_spread, 0)
    fill_early_mask()
    clear_sums()
    for copy in small:
        copy.wait()
    meta[...] = jnp.zeros(meta.shape, jnp.int32)
    meta[0:1, 0:docs] = lengths[...]
    meta[1:2, 0:docs] = targets[...]
    fill_mask(meta)
    with mark("PX_barrier"):
        pl.semaphore_wait(barrier, greeted)
    with mark("P1_xsend"):
        for j in range(n_chunks):
            x_copy(j).wait()
        x_remote().start()
    meta_remote().start()
    for c in range(SLOTS):
        ring_copy(c).start()
    with mark("P2_own"):
        absorb_half(x_own, side)
        multiply_half(0)
    with mark("P3_xwait"):
        x_remote().wait()
    with mark("P4_other"):
        absorb_half(x_other, other)
        multiply_half(1)
    with mark("P5_kv"):
        keys_values(0)
    with mark("P6_first"):
        first_query(0, 0)
        keep_heads(0)
        kv_remote(0).wait()
    with mark("P7_span0"):
        first_span(1, lag + 1, 0)
    with mark("P8_meta"):
        meta_remote().wait()
        for k in range(half):
            meta_on(k).start()
        fill_choosers(meta_next)
        clear_sums()
        pass_on(0)
    with mark("P9_span1"):
        first_span(lag + 1, early_lag + 1, 1)
    with mark("PA_early0"):
        pass_early(0)
    with mark("PB_span2"):
        first_span(early_lag + 1, n_chunks, 2)
    with mark("PC_rest"):
        last_step(n_chunks - 1, (attend_first,), (keep_next,))
        h_remote(n_chunks - 1).start()
        fill_mask(meta_next)
        for k in range(half):
            meta_on(k).wait()
        fill_valid()
        gone = n_chunks - early_lag
        for j in range(n_chunks - lag, n_chunks):
            pass_on_start(j)
            pass_on_pick(j)
            pass_on_send(j)
            forward_remote(j - 1).wait_recv()
            absorb_local(j - 1)
            if j == n_chunks - lag + 1:
                begin_query(0)
            for _ in range(2):
                if gone < j - 4:
                    pass_early(gone)
                    early_forward(gone - 1).wait_recv()
                    absorb_early(gone - 1)
                    gone += 1
            if j == n_chunks - 2:
                begin_query(1)
    with mark("PD_last"):
        forward_remote(n_chunks - 1).wait_recv()
        absorb_local(n_chunks - 1)
    with mark("PE_kv"):
        keys_values(1)
    with mark("PF_first"):
        end_query(0)
        keep_heads(1)
        end_query(1)
        kv_remote(1).wait()
        last_step(0, (attend_local,), (pick_docs,))
        send_docs(0)
    with mark("PG_local"):
        def local(j, carry):
            step(
                1, n_chunks + j, lax.rem(j, 2), 0, rows, j - 1, (attend_local,), (pick_docs,)
            )
            send_docs(j - 1)
            refill(n_chunks + j)
            return carry

        lax.fori_loop(2, LEAD - 1, local, 0)
        for i in range(gone, n_chunks):
            pass_early(i)
        lax.fori_loop(LEAD - 1, LEAD, local, 0)
        for i in range(gone - 1, n_chunks):
            early_forward(i).wait_recv()
        absorb_early(*range(gone - 1, n_chunks))
        keys_values(2)
        step(
            1, n_chunks + LEAD, LEAD % 2, 0, rows + early_rows, LEAD - 1, (attend_local,), (pick_docs,)
        )
        send_docs(LEAD - 1)
        refill(jnp.int32(n_chunks + LEAD))
        keep_heads(2)
        kv_remote(2).wait()
    with mark("PH_both"):
        def both(j, carry):
            step(
                1, n_chunks + j, lax.rem(j, 2), 0, rows + early_rows, j - 1,
                (attend_local, attend_early), (pick_docs, keep_early),
            )
            send_docs(j - 1)
            refill(n_chunks + j)
            return carry

        lax.fori_loop(LEAD + 1, n_chunks, both, 0)
    with mark("PI_turn"):
        step(
            1, total - LEAD, 0, rows, early_rows, n_chunks - 1,
            (attend_local, attend_early), (pick_docs, keep_early),
        )
        send_docs(n_chunks - 1)
    with mark("PJ_early"):
        def behind(j, carry):
            step(
                1, total - LEAD + j, lax.rem(j, 2), rows, early_rows, j - 1,
                (attend_early,), (keep_early,),
            )
            return carry

        lax.fori_loop(1, LEAD, behind, 0)
        last_step(LEAD - 1, (attend_early,), (keep_early,))
    with mark("PK_sends"):
        for held, there, sent, got in (
            (h_send, next_own, sem_hs, sem_hr.at[0]),
            (next_own, next_other, sem_fs, sem_fr.at[0]),
            (early_own, early_other, sem_gs, sem_gr.at[0]),
        ):
            whom = {"pipe": following} if held is h_send else {"tensor": other}
            pltpu.make_async_remote_copy(
                held, there, sent, got, device_id=whom, device_id_type=pl.DeviceIdType.MESH
            ).wait_send()
        for k in range(half):
            pltpu.make_async_remote_copy(
                early_send.at[:, k], early_own.at[:, k * capacity:(k + 1) * capacity],
                sem_es.at[k], sem_er.at[k, 0],
                device_id={"dp": early_partners[k]}, device_id_type=pl.DeviceIdType.MESH,
            ).wait_send()
    with mark("PL_docs"):
        for k in range(1, len(late_masks)):
            doc_all(k).wait()


def put_out(held, out, sem):
    copy = pltpu.make_async_copy(held, out, sem)
    copy.start()
    copy.wait()


def fused_device(sizes, hidden, doc_lengths, doc_target, norm_gain, q_weight, kv_weight):
    n_dp, n_pipe, docs = sizes
    rows, width = hidden.shape[1:]
    features = norm_gain.shape[1]
    n_chunks = width // CHUNK
    n_kv = kv_weight.shape[2]
    own_kv = KV_HEADS // 2
    capacity = rows // 4
    chunk_heads = CHUNK // HD
    bf16 = jnp.bfloat16
    dma = pltpu.SemaphoreType.DMA
    vmem = pltpu.VMEM
    early_masks, late_masks = split_masks(n_dp)
    half, n_late = len(early_masks), len(late_masks)
    early_rows = half * capacity
    most = rows + early_rows
    blocks = vmem((n_chunks, rows, CHUNK), bf16)
    early_blocks = vmem((n_chunks, early_rows, CHUNK), bf16)
    result = pl.pallas_call(
        functools.partial(fused_kernel, sizes),
        out_shape=vmem((n_dp * capacity, width), bf16),
        in_specs=[
            pl.BlockSpec(memory_space=pl.ANY),
            pl.BlockSpec(memory_space=pl.ANY),
            pl.BlockSpec(memory_space=pl.ANY),
            pl.BlockSpec(memory_space=pl.ANY),
            pl.BlockSpec(memory_space=pl.ANY),
            pl.BlockSpec(memory_space=pl.ANY),
        ],
        out_specs=pl.BlockSpec(memory_space=vmem),
        scratch_shapes=[
            vmem((8, 128), jnp.int32),
            vmem((1, docs), jnp.int32), vmem((1, docs), jnp.int32), vmem((1, features), jnp.float32),
            blocks, blocks, blocks, blocks, blocks, early_blocks, early_blocks,
            vmem((n_chunks, half, capacity, CHUNK), bf16),
            vmem((8, 128), jnp.int32),
            vmem((half, 8, 128), jnp.int32),
            vmem((rows, features), bf16),
            vmem((most, features), bf16),
            vmem((n_kv, n_kv), bf16),
            vmem((most, n_kv), jnp.float32),
            vmem((most, n_kv), bf16),
            vmem((most, CHUNK), jnp.float32),
            vmem((most, CHUNK), jnp.float32),
            vmem((STEPS, own_kv, most, HD), bf16),
            vmem((STEPS, 2, own_kv, most, HD), bf16),
            vmem((features, n_kv), bf16),
            vmem((SLOTS, features, CHUNK), bf16),
            vmem((chunk_heads * rows, rows), jnp.float32),
            vmem((chunk_heads * early_rows, early_rows), jnp.float32),
            vmem((early_rows, CHUNK), jnp.float32),
            vmem((early_rows, rows), bf16),
            vmem((n_late * capacity, rows), bf16),
            vmem((2, most, CHUNK), bf16),
            vmem((2, rows, CHUNK), jnp.float32),
            vmem((n_late, capacity, width), bf16),
            dma((n_chunks,)), dma, dma, dma, dma,
            dma((features // KV_ROWS,)), dma((SLOTS,)), dma((STEPS + 1,)), dma((STEPS + 1,)),
            dma, dma((n_chunks,)), dma, dma((n_chunks,)),
            dma((n_late,)), dma((n_late,)),
            dma((half,)), dma((half, n_chunks)), dma, dma((n_chunks,)),
            dma((half,)), dma((half,)), dma((3,)),
        ],
        compiler_params=pltpu.CompilerParams(
            collective_id=0, has_side_effects=True, vmem_limit_bytes=64800000
        ),
    )(hidden[0], doc_lengths[0], doc_target[0], norm_gain, q_weight[0], kv_weight[0])
    return pl.pallas_call(
        put_out,
        out_shape=jax.ShapeDtypeStruct((n_dp * capacity, width), bf16),
        in_specs=[pl.BlockSpec(memory_space=vmem)],
        out_specs=pl.BlockSpec(memory_space=pl.ANY),
        scratch_shapes=[dma],
        compiler_params=pltpu.CompilerParams(vmem_limit_bytes=4194304),
    )(result)[None]


def solution(mesh):
    placed = (
        P("pipe", "dp", "tensor"),
        P("pipe", "dp", None),
        P("pipe", "dp", None),
        P("pipe", None),
        P("pipe", None, "tensor"),
        P("pipe", None, "tensor"),
    )
    run = on_device
    if mesh.shape["tensor"] == 2 and mesh.shape["dp"] in (4, 8, 16):
        sizes = (mesh.shape["dp"], mesh.shape["pipe"], mesh.shape["dp"])
        run = functools.partial(fused_device, sizes)
    return jax.shard_map(
        run, mesh=mesh, in_specs=placed, out_specs=P("pipe", "dp", "tensor"), check_vma=False
    )
```

```python
import contextlib
import functools

import jax
import jax.numpy as jnp
from jax import lax
from jax.experimental import pallas as pl
from jax.experimental.pallas import tpu as pltpu
from jax.sharding import PartitionSpec as P

D = 8192
HD = 128
KV_HEADS = 8
STEPS = 2


def passed_along(block, axis, distance):
    devices = range(lax.axis_size(axis))
    route = [((i - distance) % len(devices), i) for i in devices]
    return lax.ppermute(block, axis, route)


def build_send(token_rows, lengths, targets, capacity, groups):
    ordinal = jnp.arange(groups, dtype=jnp.int32)
    offsets = jnp.cumsum(lengths) - lengths
    onehot = (targets[None, :] == ordinal[:, None]).astype(jnp.int32)
    doc_sizes = jnp.sum(onehot * lengths[None, :], axis=1)
    doc_starts = jnp.sum(onehot * offsets[None, :], axis=1)
    within = jnp.arange(capacity, dtype=jnp.int32)
    row_index = jnp.minimum(doc_starts[:, None] + within[None, :], token_rows.shape[0] - 1)
    picked = jnp.take(token_rows, row_index.reshape(-1), axis=0).reshape(
        groups, capacity, token_rows.shape[1]
    )
    inside = within[None, :] < doc_sizes[:, None]
    return (jnp.where(inside[:, :, None], picked, jnp.zeros_like(picked)), doc_sizes)


def doc_masks(lengths, length):
    within = jnp.arange(length, dtype=jnp.int32)
    doc_ends = jnp.cumsum(lengths)
    segment = jnp.sum((within[:, None] >= doc_ends[None, :]).astype(jnp.int32), axis=1)
    causal = within[:, None] >= within[None, :]
    return (segment[:, None] == segment[None, :]) & causal


def attend_heads(queries, kv_local, allowed, local_rank):
    row_count = queries.shape[0]
    local_heads = queries.shape[1] // HD
    per_group = D // HD // KV_HEADS
    kv_count = max(1, local_heads // per_group)
    kv_first = local_rank * local_heads // per_group
    kv_whole = lax.all_gather(kv_local, "tensor", axis=1, tiled=True)
    kv_heads = kv_whole.reshape(row_count, 2, HD, KV_HEADS)
    own_heads = lax.dynamic_slice_in_dim(kv_heads, kv_first, kv_count, 3)
    key_rows = own_heads[:, 0]
    values = own_heads[:, 1]
    grouped = queries.reshape(row_count, kv_count, local_heads // kv_count, HD)
    scores = jnp.einsum(
        "qcph,khc->cpqk", grouped, key_rows, preferred_element_type=jnp.float32
    ) * HD ** (-0.5)
    exp_scores = jnp.where(allowed[None, None], jnp.exp(scores), 0.0)
    probabilities = (exp_scores / jnp.sum(exp_scores, axis=-1, keepdims=True)).astype(jnp.bfloat16)
    attended = jnp.einsum(
        "cpqk,khc->qcph", probabilities, values, preferred_element_type=jnp.float32
    )
    return attended.reshape(row_count, queries.shape[1])


def layer_pass(current, gain_full, query_cols, kv_cols, allowed):
    local_rank = lax.axis_index("tensor")
    widened = current.astype(jnp.float32)
    whole = lax.all_gather(current, "tensor", axis=1, tiled=True)
    whole_wide = whole.astype(jnp.float32)
    scale_row = lax.rsqrt(jnp.sum(whole_wide * whole_wide, axis=-1) / D + 1e-05)
    normed_full = (whole_wide * scale_row[:, None] * gain_full).astype(jnp.bfloat16)
    query_sum = jnp.dot(normed_full, query_cols, preferred_element_type=jnp.float32)
    kv_sum = jnp.dot(normed_full, kv_cols, preferred_element_type=jnp.float32)
    queries = query_sum.astype(jnp.bfloat16)
    kv_local = kv_sum.astype(jnp.bfloat16)
    attended = attend_heads(queries, kv_local, allowed, local_rank)
    return (widened + attended).astype(jnp.bfloat16)


def on_device(hidden, doc_lengths, doc_target, norm_gain, q_weight, kv_weight):
    groups = lax.axis_size("dp")
    current = hidden[0]
    lengths = doc_lengths[0, 0]
    targets = doc_target[0, 0]
    capacity = current.shape[0] // 4
    gain_full = norm_gain[0]
    query_cols = q_weight[0]
    kv_cols = kv_weight[0]
    carried = jnp.stack([lengths, targets]).astype(jnp.bfloat16)
    for layer_step in range(STEPS):
        allowed = doc_masks(carried[0].astype(jnp.int32), current.shape[0])
        current = layer_pass(current, gain_full, query_cols, kv_cols, allowed)
        if layer_step + 1 < STEPS:
            current, carried = passed_along((current, carried), "pipe", 1)
    final_lengths = carried[0].astype(jnp.int32)
    final_targets = carried[1].astype(jnp.int32)
    packed, doc_sizes = build_send(current, final_lengths, final_targets, capacity, groups)
    received = lax.all_to_all(packed, "dp", split_axis=0, concat_axis=0, tiled=True)
    return received.reshape(1, groups * capacity, received.shape[2])


CHUNK = 256
SLOTS = 6
KV_ROWS = 1024
LEAD = 6
PIECES = 4


mark = contextlib.nullcontext


def split_masks(n_dp):
    early = [m for m in range(n_dp) if m >= n_dp // 2 and m % 2 == 0]
    return early, [m for m in range(n_dp) if m not in early]


def fused_kernel(
    sizes, hidden, lengths_in, targets_in, gain_in, wq, wkv, out, meta, lengths, targets, gain,
    x_own, x_other, h_send, next_own, next_other, early_own, early_other, early_send,
    meta_next, meta_early, normed_first, normed_next, spread, kv_acc, kv_cols, squares, scales,
    kv_send, kv_heads, kv_weights, ring, mask, early_mask, valid, early_chooser, late_chooser,
    q_held, begun, packed,
    sem_x, sem_xs, sem_xr, sem_ms, sem_mr, sem_kvw, sem_ring, sem_kvs, sem_kvr,
    sem_hs, sem_hr, sem_fs, sem_fr, sem_as, sem_ar,
    sem_es, sem_er, sem_gs, sem_gr, sem_mes, sem_mer, sem_in,
):
    n_dp, n_pipe, docs = sizes
    rows, width = hidden.shape
    features = gain_in.shape[1]
    n_chunks = width // CHUNK
    n_kv = wkv.shape[1]
    half_blocks = width // KV_ROWS
    own_kv = kv_heads.shape[2]
    chunk_heads = CHUNK // HD
    group_chunks = n_chunks // own_kv
    capacity = packed.shape[1]
    early_masks, late_masks = split_masks(n_dp)
    half = len(early_masks)
    early_rows = half * capacity
    dp = lax.axis_index("dp")
    pipe = lax.axis_index("pipe")
    side = lax.axis_index("tensor")
    other = 1 - side
    following = lax.rem(pipe + 1, n_pipe)
    preceding = lax.rem(pipe + n_pipe - 1, n_pipe)
    total = STEPS * n_chunks + LEAD
    normed_of = (normed_first, normed_next)

    def partner(flips):
        index, bit = dp, 1
        while bit < n_dp:
            if flips & bit:
                index = index + bit - 2 * bit * lax.rem(dp // bit, 2)
            bit *= 2
        return index

    early_partners = [partner(m) for m in early_masks]
    late_partners = [partner(m) for m in late_masks]

    def cols(j):
        return pl.ds(pl.multiple_of(j * CHUNK, CHUNK), CHUNK)

    def kv_rows(which, b):
        return pl.ds(pl.multiple_of((which * half_blocks + b) * KV_ROWS, KV_ROWS), KV_ROWS)

    def kv_copy(order, b):
        here = kv_rows((side, other)[order], b)
        return pltpu.make_async_copy(
            wkv.at[here], kv_weights.at[here], sem_kvw.at[order * half_blocks + b]
        )

    def ring_copy(c):
        slot = lax.rem(c, SLOTS)
        return pltpu.make_async_copy(
            wq.at[:, cols(lax.rem(c, n_chunks))], ring.at[slot], sem_ring.at[slot]
        )

    def x_copy(j):
        return pltpu.make_async_copy(hidden.at[:, cols(j)], x_own.at[j], sem_x)

    def x_remote():
        return pltpu.make_async_remote_copy(
            x_own, x_other, sem_xs, sem_xr,
            device_id={"tensor": other}, device_id_type=pl.DeviceIdType.MESH,
        )

    def meta_remote():
        return pltpu.make_async_remote_copy(
            meta, meta_next, sem_ms, sem_mr,
            device_id={"pipe": following}, device_id_type=pl.DeviceIdType.MESH,
        )

    def meta_on(k):
        return pltpu.make_async_remote_copy(
            meta_next, meta_early.at[k], sem_mes.at[k], sem_mer.at[k],
            device_id={"dp": early_partners[k]}, device_id_type=pl.DeviceIdType.MESH,
        )

    def early_remote(k, j):
        return pltpu.make_async_remote_copy(
            early_send.at[j, k], early_own.at[j, k * capacity:(k + 1) * capacity],
            sem_es.at[k], sem_er.at[j],
            device_id={"dp": early_partners[k]}, device_id_type=pl.DeviceIdType.MESH,
        )

    def early_forward(j):
        return pltpu.make_async_remote_copy(
            early_own.at[j], early_other.at[j], sem_gs, sem_gr.at[j],
            device_id={"tensor": other}, device_id_type=pl.DeviceIdType.MESH,
        )

    parts = ((0, 0, rows), (1, 0, rows), (1, rows, early_rows))

    def kv_remote(part):
        layer, first, count = parts[part]
        here = pl.ds(first, count)
        return pltpu.make_async_remote_copy(
            kv_send.at[layer, :, here], kv_heads.at[layer, side, :, here],
            sem_kvs.at[part], sem_kvr.at[part],
            device_id={"tensor": other}, device_id_type=pl.DeviceIdType.MESH,
        )

    def h_remote(j):
        return pltpu.make_async_remote_copy(
            h_send.at[j], next_own.at[j], sem_hs, sem_hr.at[j],
            device_id={"pipe": following}, device_id_type=pl.DeviceIdType.MESH,
        )

    def forward_remote(j):
        return pltpu.make_async_remote_copy(
            next_own.at[j], next_other.at[j], sem_fs, sem_fr.at[j],
            device_id={"tensor": other}, device_id_type=pl.DeviceIdType.MESH,
        )

    def doc_rows(index):
        return pl.ds(pl.multiple_of(index * capacity, capacity), capacity)

    def doc_remote(k, j):
        return pltpu.make_async_remote_copy(
            packed.at[k, :, cols(j)], out.at[doc_rows(dp), cols(j)],
            sem_as.at[k], sem_ar.at[k],
            device_id={"dp": late_partners[k]}, device_id_type=pl.DeviceIdType.MESH,
        )

    def doc_all(k):
        return pltpu.make_async_remote_copy(
            packed.at[k], out.at[doc_rows(late_partners[k])],
            sem_as.at[k], sem_ar.at[k],
            device_id={"dp": late_partners[k]}, device_id_type=pl.DeviceIdType.MESH,
        )

    small = [
        pltpu.make_async_copy(*pair, sem_in.at[i])
        for i, pair in enumerate(((lengths_in, lengths), (targets_in, targets), (gain_in, gain)))
    ]
    for j in range(n_chunks):
        x_copy(j).start()
    for copy in small:
        copy.start()
    barrier = pltpu.get_barrier_semaphore()
    pl.semaphore_signal(
        barrier, inc=1, device_id={"tensor": other}, device_id_type=pl.DeviceIdType.MESH
    )
    pl.semaphore_signal(
        barrier, inc=1, device_id={"pipe": following}, device_id_type=pl.DeviceIdType.MESH
    )
    greeted = n_dp + 1
    if n_pipe > 2:
        pl.semaphore_signal(
            barrier, inc=1, device_id={"pipe": preceding}, device_id_type=pl.DeviceIdType.MESH
        )
        greeted += 1
    for away in range(1, n_dp):
        pl.semaphore_signal(
            barrier, inc=1, device_id={"dp": lax.rem(dp + away, n_dp)},
            device_id_type=pl.DeviceIdType.MESH,
        )
    for order in range(2):
        for b in range(half_blocks):
            kv_copy(order, b).start()

    cols_wide = spread.shape[0]
    out_col = lax.broadcasted_iota(jnp.int32, (128, n_kv), 1)
    wanted = lax.rem(out_col, HD) * KV_HEADS + out_col // HD

    def fill_spread(i, carry):
        base = pl.multiple_of(i * 128, 128)
        row = lax.broadcasted_iota(jnp.int32, (128, n_kv), 0) + base
        spread[pl.ds(base, 128), :] = (row == wanted).astype(jnp.float32).astype(jnp.bfloat16)
        return carry

    def fill_mask(source):
        row = lax.broadcasted_iota(jnp.int32, (rows, rows), 0)
        col = lax.broadcasted_iota(jnp.int32, (rows, rows), 1)
        row_doc = jnp.zeros((rows, rows), jnp.int32)
        col_doc = jnp.zeros((rows, rows), jnp.int32)
        end = jnp.zeros((1, 1), jnp.int32)
        for d in range(docs):
            end = end + source[0:1, d:d + 1]
            row_doc = row_doc + (row >= end).astype(jnp.int32)
            col_doc = col_doc + (col >= end).astype(jnp.int32)
        allowed = jnp.where((row_doc == col_doc) & (row >= col), 1.0, 0.0)
        for i in range(chunk_heads):
            mask[i * rows:(i + 1) * rows, :] = allowed

    def fill_early_mask():
        row = lax.broadcasted_iota(jnp.int32, (early_rows, early_rows), 0)
        col = lax.broadcasted_iota(jnp.int32, (early_rows, early_rows), 1)
        allowed = jnp.where((row // capacity == col // capacity) & (row >= col), 1.0, 0.0)
        for i in range(chunk_heads):
            early_mask[i * early_rows:(i + 1) * early_rows, :] = allowed

    def fill_valid():
        row = lax.broadcasted_iota(jnp.int32, (capacity, CHUNK), 0)
        for slot in range(half):
            size = jnp.zeros((1, 1), jnp.int32)
            for d in range(docs):
                here = meta_early[slot, 1:2, d:d + 1] == dp
                size = size + jnp.where(here, meta_early[slot, 0:1, d:d + 1], 0)
            valid[slot * capacity:(slot + 1) * capacity, :] = jnp.where(row < size, 1.0, 0.0)

    def fill_choosers(source):
        row = lax.broadcasted_iota(jnp.int32, (1, rows), 1)
        goals = [jnp.full((1, rows), -1, jnp.int32) for _ in range(2)]
        begin = jnp.zeros((1, 1), jnp.int32)
        for d in range(docs):
            end = begin + source[0:1, d:d + 1]
            target = source[1:2, d:d + 1]
            inside = (row >= begin) & (row < end)
            for i, partners in enumerate((early_partners, late_partners)):
                first = jnp.full((1, 1), -n_dp * capacity, jnp.int32)
                for k, index in enumerate(partners):
                    first = jnp.where(target == index, k * capacity, first)
                goals[i] = jnp.where(inside, first + row - begin, goals[i])
            begin = end
        for ref, goal in zip((early_chooser, late_chooser), goals):
            slot = lax.broadcasted_iota(jnp.int32, ref.shape, 0)
            ref[...] = (slot == goal).astype(jnp.float32).astype(jnp.bfloat16)

    def absorb_half(held, which):
        def one(j, acc):
            wide = held[j].astype(jnp.float32)
            where = cols(which * n_chunks + j)
            normed_first[:, where] = (wide * gain[:, where]).astype(jnp.bfloat16)
            return acc + wide * wide

        squares[0:rows] = lax.fori_loop(0, n_chunks, one, squares[0:rows])

    def multiply_half(order):
        which = (side, other)[order]

        def one(b, carry):
            kv_copy(order, b).wait()
            here = kv_rows(which, b)
            kv_acc[0:rows] += jnp.dot(
                normed_first[:, here], kv_weights[here, :], preferred_element_type=jnp.float32
            )
            return carry

        lax.fori_loop(0, half_blocks, one, 0)

    def absorb_next(mine, theirs, first, count, chunks):
        here = slice(first, first + count)
        total = squares[here]
        left, right = [], []
        for j in chunks:
            for held, which in ((mine, side), (theirs, other)):
                where = cols(which * n_chunks + j)
                wide = held[j].astype(jnp.float32)
                total = total + wide * wide
                scaled = (wide * gain[:, where]).astype(jnp.bfloat16)
                normed_next[here, where] = scaled
                left.append(scaled)
                right.append(kv_weights[where, :])
        squares[here] = total
        kv_acc[here] += jnp.dot(
            jnp.concatenate(left, axis=1), jnp.concatenate(right, axis=0),
            preferred_element_type=jnp.float32,
        )

    def clear_sums():
        kv_acc[...] = jnp.zeros(kv_acc.shape, jnp.float32)
        squares[...] = jnp.zeros(squares.shape, jnp.float32)

    def keys_values(part):
        layer, first, count = parts[part]
        here = slice(first, first + count)
        scale = lax.rsqrt(jnp.sum(squares[here], axis=-1, keepdims=True) / features + 1e-05)
        scales[here] = jnp.broadcast_to(scale, (count, CHUNK))
        kv_cols[here] = (kv_acc[here] * scale).astype(jnp.bfloat16)
        heads = kv_spread(part, other)
        for g in range(own_kv):
            kv_send[layer, g, here] = heads[:, g * HD:(g + 1) * HD]
        kv_remote(part).start()

    def kv_spread(part, which):
        _, first, count = parts[part]
        start = pl.multiple_of(which * own_kv * HD, own_kv * HD)
        return jnp.dot(
            kv_cols[first:first + count], spread[:, pl.ds(start, own_kv * HD)],
            preferred_element_type=jnp.float32,
        ).astype(jnp.bfloat16)

    def keep_heads(part):
        layer, first, count = parts[part]
        heads = kv_spread(part, side)
        for g in range(own_kv):
            kv_heads[layer, side, g, first:first + count] = heads[:, g * HD:(g + 1) * HD]

    def query_piece(layer, c, first, count, piece):
        deep = slice(piece * features // PIECES, (piece + 1) * features // PIECES)
        return jnp.dot(
            normed_of[layer][first:first + count, deep], ring[lax.rem(c, SLOTS), deep],
            preferred_element_type=jnp.float32,
        )

    def attend(layer, j, mine, first, count, allowed):
        here = slice(first, first + count)
        q = q_held[lax.rem(j, 2), here]
        g = j // group_chunks
        stacked = jnp.concatenate([q[:, i * HD:(i + 1) * HD] for i in range(chunk_heads)], axis=0)
        scores = lax.dot_general(
            stacked, kv_heads[layer, 0, g, here], (((1,), (1,)), ((), ())),
            preferred_element_type=jnp.float32,
        ) * HD ** (-0.5)
        yield
        e = jnp.where(allowed[...] > 0.0, jnp.exp(scores), 0.0)
        p = (e * (1.0 / jnp.sum(e, axis=-1, keepdims=True))).astype(jnp.bfloat16)
        yield
        a = jnp.dot(p, kv_heads[layer, 1, g, here], preferred_element_type=jnp.float32)
        side_by_side = jnp.concatenate(
            [a[i * count:(i + 1) * count] for i in range(chunk_heads)], axis=1
        )
        yield (mine[j].astype(jnp.float32) + side_by_side).astype(jnp.bfloat16)

    def attend_first(j):
        return attend(0, j, x_own, 0, rows, mask)

    def attend_local(j):
        return attend(1, j, next_own, 0, rows, mask)

    def attend_early(j):
        return attend(1, j, early_own, rows, early_rows, early_mask)

    def refill(c):
        @pl.when(c + SLOTS < total)
        def _():
            ring_copy(c + SLOTS).start()

    def first_query(layer, c):
        ring_copy(c).wait()
        product = query_piece(layer, c, 0, rows, 0)
        for piece in range(1, PIECES):
            product = product + query_piece(layer, c, 0, rows, piece)
        q_held[0, 0:rows] = (product * scales[0:rows]).astype(jnp.bfloat16)
        refill(jnp.int32(c))

    lag, early_lag = 5, 10
    early_deep = (n_chunks - lag + 1) * CHUNK

    def query_part(c, low, high):
        product = None
        for start in (0, width):
            deep = slice(start + low, start + high)
            part = jnp.dot(
                normed_next[0:rows, deep], ring[lax.rem(c, SLOTS), deep],
                preferred_element_type=jnp.float32,
            )
            product = part if product is None else product + part
        return product

    def begin_query(j):
        ring_copy(n_chunks + j).wait()
        begun[j] = query_part(n_chunks + j, 0, early_deep)

    def end_query(j):
        product = begun[j] + query_part(n_chunks + j, early_deep, width)
        q_held[j, 0:rows] = (product * scales[0:rows]).astype(jnp.bfloat16)
        refill(jnp.int32(n_chunks + j))

    def step(layer, c, slot, first, count, before, attends, settles, extras=()):
        ring_copy(c).wait()
        stages = [attended(before) for attended in attends]
        product = None
        for piece in range(PIECES):
            done = [next(stage, None) for stage in stages]
            if piece == 2:
                made = done
            if piece == 3:
                for settle, value in zip(settles, made):
                    settle(before, value)
            for extra in extras[piece:piece + 1]:
                extra()
            part = query_piece(layer, c, first, count, piece)
            product = part if product is None else product + part
        here = slice(first, first + count)
        q_held[slot, here] = (product * scales[here]).astype(jnp.bfloat16)

    def last_step(before, attends, settles):
        stages = [attended(before) for attended in attends]
        for piece in range(3):
            made = [next(stage) for stage in stages]
        for settle, value in zip(settles, made):
            settle(before, value)

    def keep_next(j, done):
        h_send[j] = done

    def pass_on_start(j):
        h_remote(j).wait_recv()
        forward_remote(j).start()

    def pass_on_pick(j):
        picked = jnp.dot(
            early_chooser[...], next_own[j], preferred_element_type=jnp.float32
        ).astype(jnp.bfloat16)
        for slot in range(half):
            early_send[j, slot] = picked[slot * capacity:(slot + 1) * capacity]

    def pass_on_send(j):
        for k in range(half):
            early_remote(k, j).start()

    def pass_on(j):
        pass_on_start(j)
        pass_on_pick(j)
        pass_on_send(j)

    def absorb_local(*chunks):
        absorb_next(next_own, next_other, 0, rows, chunks)

    def absorb_early(*chunks):
        absorb_next(early_own, early_other, rows, early_rows, chunks)

    def pass_early(j):
        pltpu.make_async_remote_copy(
            normed_next.at[rows:rows + early_rows, 0:CHUNK], early_own.at[j], sem_es.at[0], sem_er.at[j],
            device_id={"dp": early_partners[0]}, device_id_type=pl.DeviceIdType.MESH,
        ).wait_recv()
        early_forward(j).start()

    def pick_docs(j, done):
        picked = jnp.dot(late_chooser[...], done, preferred_element_type=jnp.float32)
        picked = picked.astype(jnp.bfloat16)
        out[doc_rows(dp), cols(j)] = picked[0:capacity]
        for slot in range(1, len(late_masks)):
            packed[slot, :, cols(j)] = picked[slot * capacity:(slot + 1) * capacity]

    def send_docs(j):
        for k in reversed(range(1, len(late_masks))):
            doc_remote(k, j).start()

    def keep_early(j, early):
        kept = jnp.where(valid[...] > 0.0, early.astype(jnp.float32), 0.0).astype(jnp.bfloat16)
        for slot in range(half):
            out[doc_rows(early_partners[slot]), cols(j)] = kept[slot * capacity:(slot + 1) * capacity]

    def first_span(low, high, stage):
        def one(j, carry):
            on, local, gone, early = j - lag, j - lag - 1, j - early_lag, j - early_lag - 1
            extras = [[], [], [], []]
            if stage >= 1:
                pass_on_start(on)
                forward_remote(local).wait_recv()
                extras[0].append(functools.partial(absorb_local, local))
                extras[1].append(functools.partial(pass_on_pick, on))
            if stage >= 2:
                pass_early(gone)
                early_forward(early).wait_recv()
                extras[2].append(functools.partial(absorb_early, early))
            step(
                0, j, lax.rem(j, 2), 0, rows, j - 1, (attend_first,), (keep_next,),
                [functools.partial(run_all, group) for group in extras],
            )
            h_remote(j - 1).start()
            if stage >= 1:
                pass_on_send(on)
            refill(j)
            return carry

        lax.fori_loop(low, high, one, 0)

    def run_all(group):
        for task in group:
            task()

    lax.fori_loop(0, cols_wide // 128, fill_spread, 0)
    fill_early_mask()
    clear_sums()
    for copy in small:
        copy.wait()
    meta[...] = jnp.zeros(meta.shape, jnp.int32)
    meta[0:1, 0:docs] = lengths[...]
    meta[1:2, 0:docs] = targets[...]
    fill_mask(meta)
    with mark("PX_barrier"):
        pl.semaphore_wait(barrier, greeted)
    with mark("P1_xsend"):
        pltpu.make_async_copy(h_send, x_own, sem_x).wait()
        x_remote().start()
    meta_remote().start()
    for c in range(SLOTS):
        ring_copy(c).start()
    with mark("P2_own"):
        absorb_half(x_own, side)
        multiply_half(0)
    with mark("P3_xwait"):
        x_remote().wait()
    with mark("P4_other"):
        absorb_half(x_other, other)
        multiply_half(1)
    with mark("P5_kv"):
        keys_values(0)
    with mark("P6_first"):
        first_query(0, 0)
        keep_heads(0)
        kv_remote(0).wait()
    with mark("P7_span0"):
        first_span(1, lag + 1, 0)
    with mark("P8_meta"):
        meta_remote().wait()
        for k in range(half):
            meta_on(k).start()
        fill_choosers(meta_next)
        clear_sums()
        pass_on(0)
    with mark("P9_span1"):
        first_span(lag + 1, early_lag + 1, 1)
    with mark("PA_early0"):
        pass_early(0)
    with mark("PB_span2"):
        first_span(early_lag + 1, n_chunks, 2)
    with mark("PC_rest"):
        last_step(n_chunks - 1, (attend_first,), (keep_next,))
        h_remote(n_chunks - 1).start()
        fill_mask(meta_next)
        for k in range(half):
            meta_on(k).wait()
        fill_valid()
        gone = n_chunks - early_lag
        for j in range(n_chunks - lag, n_chunks):
            pass_on_start(j)
            pass_on_pick(j)
            pass_on_send(j)
            forward_remote(j - 1).wait_recv()
            absorb_local(j - 1)
            if j == n_chunks - lag + 1:
                begin_query(0)
            for _ in range(2):
                if gone < j - 4:
                    pass_early(gone)
                    early_forward(gone - 1).wait_recv()
                    absorb_early(gone - 1)
                    gone += 1
            if j == n_chunks - 2:
                begin_query(1)
    with mark("PD_last"):
        forward_remote(n_chunks - 1).wait_recv()
        absorb_local(n_chunks - 1)
    with mark("PE_kv"):
        keys_values(1)
    with mark("PF_first"):
        end_query(0)
        keep_heads(1)
        end_query(1)
        kv_remote(1).wait()
        last_step(0, (attend_local,), (pick_docs,))
        send_docs(0)
    with mark("PG_local"):
        def local(j, carry):
            step(
                1, n_chunks + j, lax.rem(j, 2), 0, rows, j - 1, (attend_local,), (pick_docs,)
            )
            send_docs(j - 1)
            refill(n_chunks + j)
            return carry

        lax.fori_loop(2, LEAD - 1, local, 0)
        for i in range(gone, n_chunks):
            pass_early(i)
        lax.fori_loop(LEAD - 1, LEAD, local, 0)
        for i in range(gone - 1, n_chunks):
            early_forward(i).wait_recv()
        absorb_early(*range(gone - 1, n_chunks))
        keys_values(2)
        step(
            1, n_chunks + LEAD, LEAD % 2, 0, rows + early_rows, LEAD - 1, (attend_local,), (pick_docs,)
        )
        send_docs(LEAD - 1)
        refill(jnp.int32(n_chunks + LEAD))
        keep_heads(2)
        kv_remote(2).wait()
    with mark("PH_both"):
        def both(j, carry):
            step(
                1, n_chunks + j, lax.rem(j, 2), 0, rows + early_rows, j - 1,
                (attend_local, attend_early), (pick_docs, keep_early),
            )
            send_docs(j - 1)
            refill(n_chunks + j)
            return carry

        lax.fori_loop(LEAD + 1, n_chunks, both, 0)
    with mark("PI_turn"):
        step(
            1, total - LEAD, 0, rows, early_rows, n_chunks - 1,
            (attend_local, attend_early), (pick_docs, keep_early),
        )
        send_docs(n_chunks - 1)
    with mark("PJ_early"):
        def behind(j, carry):
            step(
                1, total - LEAD + j, lax.rem(j, 2), rows, early_rows, j - 1,
                (attend_early,), (keep_early,),
            )
            return carry

        lax.fori_loop(1, LEAD, behind, 0)
        last_step(LEAD - 1, (attend_early,), (keep_early,))
    with mark("PK_sends"):
        for held, there, sent, got in (
            (h_send, next_own, sem_hs, sem_hr.at[0]),
            (next_own, next_other, sem_fs, sem_fr.at[0]),
            (early_own, early_other, sem_gs, sem_gr.at[0]),
        ):
            whom = {"pipe": following} if held is h_send else {"tensor": other}
            pltpu.make_async_remote_copy(
                held, there, sent, got, device_id=whom, device_id_type=pl.DeviceIdType.MESH
            ).wait_send()
        for k in range(half):
            pltpu.make_async_remote_copy(
                early_send.at[:, k], early_own.at[:, k * capacity:(k + 1) * capacity],
                sem_es.at[k], sem_er.at[0],
                device_id={"dp": early_partners[k]}, device_id_type=pl.DeviceIdType.MESH,
            ).wait_send()
    with mark("PL_docs"):
        for k in range(1, len(late_masks)):
            doc_all(k).wait()


def put_out(held, out, sem):
    copy = pltpu.make_async_copy(held, out, sem)
    copy.start()
    copy.wait()


def fused_device(sizes, hidden, doc_lengths, doc_target, norm_gain, q_weight, kv_weight):
    n_dp, n_pipe, docs = sizes
    rows, width = hidden.shape[1:]
    features = norm_gain.shape[1]
    n_chunks = width // CHUNK
    n_kv = kv_weight.shape[2]
    own_kv = KV_HEADS // 2
    capacity = rows // 4
    chunk_heads = CHUNK // HD
    bf16 = jnp.bfloat16
    dma = pltpu.SemaphoreType.DMA
    vmem = pltpu.VMEM
    early_masks, late_masks = split_masks(n_dp)
    half, n_late = len(early_masks), len(late_masks)
    early_rows = half * capacity
    most = rows + early_rows
    blocks = vmem((n_chunks, rows, CHUNK), bf16)
    early_blocks = vmem((n_chunks, early_rows, CHUNK), bf16)
    result = pl.pallas_call(
        functools.partial(fused_kernel, sizes),
        out_shape=vmem((n_dp * capacity, width), bf16),
        in_specs=[
            pl.BlockSpec(memory_space=pl.ANY),
            pl.BlockSpec(memory_space=pl.ANY),
            pl.BlockSpec(memory_space=pl.ANY),
            pl.BlockSpec(memory_space=pl.ANY),
            pl.BlockSpec(memory_space=pl.ANY),
            pl.BlockSpec(memory_space=pl.ANY),
        ],
        out_specs=pl.BlockSpec(memory_space=vmem),
        scratch_shapes=[
            vmem((8, 128), jnp.int32),
            vmem((1, docs), jnp.int32), vmem((1, docs), jnp.int32), vmem((1, features), jnp.float32),
            blocks, blocks, blocks, blocks, blocks, early_blocks, early_blocks,
            vmem((n_chunks, half, capacity, CHUNK), bf16),
            vmem((8, 128), jnp.int32),
            vmem((half, 8, 128), jnp.int32),
            vmem((rows, features), bf16),
            vmem((most, features), bf16),
            vmem((n_kv, n_kv), bf16),
            vmem((most, n_kv), jnp.float32),
            vmem((most, n_kv), bf16),
            vmem((most, CHUNK), jnp.float32),
            vmem((most, CHUNK), jnp.float32),
            vmem((STEPS, own_kv, most, HD), bf16),
            vmem((STEPS, 2, own_kv, most, HD), bf16),
            vmem((features, n_kv), bf16),
            vmem((SLOTS, features, CHUNK), bf16),
            vmem((chunk_heads * rows, rows), jnp.float32),
            vmem((chunk_heads * early_rows, early_rows), jnp.float32),
            vmem((early_rows, CHUNK), jnp.float32),
            vmem((early_rows, rows), bf16),
            vmem((n_late * capacity, rows), bf16),
            vmem((2, most, CHUNK), bf16),
            vmem((2, rows, CHUNK), jnp.float32),
            vmem((n_late, capacity, width), bf16),
            dma, dma, dma, dma, dma,
            dma((features // KV_ROWS,)), dma((SLOTS,)), dma((STEPS + 1,)), dma((STEPS + 1,)),
            dma, dma((n_chunks,)), dma, dma((n_chunks,)),
            dma((n_late,)), dma((n_late,)),
            dma((half,)), dma((n_chunks,)), dma, dma((n_chunks,)),
            dma((half,)), dma((half,)), dma((3,)),
        ],
        compiler_params=pltpu.CompilerParams(
            collective_id=0, has_side_effects=True, vmem_limit_bytes=64800000
        ),
    )(hidden[0], doc_lengths[0], doc_target[0], norm_gain, q_weight[0], kv_weight[0])
    return pl.pallas_call(
        put_out,
        out_shape=jax.ShapeDtypeStruct((n_dp * capacity, width), bf16),
        in_specs=[pl.BlockSpec(memory_space=vmem)],
        out_specs=pl.BlockSpec(memory_space=pl.ANY),
        scratch_shapes=[dma],
        compiler_params=pltpu.CompilerParams(vmem_limit_bytes=4194304),
    )(result)[None]


def solution(mesh):
    placed = (
        P("pipe", "dp", "tensor"),
        P("pipe", "dp", None),
        P("pipe", "dp", None),
        P("pipe", None),
        P("pipe", None, "tensor"),
        P("pipe", None, "tensor"),
    )
    run = on_device
    if mesh.shape["tensor"] == 2 and mesh.shape["dp"] in (4, 8, 16):
        sizes = (mesh.shape["dp"], mesh.shape["pipe"], mesh.shape["dp"])
        run = functools.partial(fused_device, sizes)
    return jax.shard_map(
        run, mesh=mesh, in_specs=placed, out_specs=P("pipe", "dp", "tensor"), check_vma=False
    )
```
